32 devices in a mesh: row: 8 (over z, x), col: 4 (over y, core).
Axes of the slice: x: 2, y: 2, z: 4, core: 2. Of those that a mesh axis runs over, the one named last changes fastest.
Arguments:
- positions: float32 [3, 32, 16, 256], P(None, 'row', 'col'), may hold values from 0 to 1
- masses: float32 [32, 16, 256], P('row', 'col'), may hold values from 0.002 to 0.02
- counts: int32 [32, 16, 4], P('row', 'col'), may hold values from 1 to 64, as said below
- multipoles: float32 [32, 16, 224], P('row', 'col'), may hold values from -6 to 6
- parent_local: float32 [16, 8, 112], P('row', 'col'), may hold values from -6 to 6
- m2l_ops: float32 [343, 3136], replicated, may hold values from -0.0625 to 0.0625
- l2l_ops: float32 [8, 56, 56], replicated, may hold values from -0.75 to 0.75
- check_to_equiv: float32 [56, 56], replicated, may hold values from -0.1875 to 0.1875
Outputs:
- potential: float32 [32, 16, 256], P('row', 'col')
- local_densities: float32 [32, 16, 224], P('row', 'col')
The draws below stay inside these ranges and needn't reach their ends.
Inputs may be any that keep to these rules, and one draw needn't show every extreme that they name: Occupancy is clustered: leaves' counts vary strongly between regions of the box.
All inputs are finite; a program needn't handle non-finite values.
Results may differ from the reference program's by a relative error of at most 0.0003.
Values sent between devices are 32-bit elements; how exact they have to be, the bound alone decides.
No kernel may reach another device: no remote copies, remote signals or barrier semaphores. Data moves between devices by JAX's collectives and lax.ppermute only.
A program may use at most 128 MiB of HBM per device.

```python
import math
import jax
import jax.numpy as jnp
import numpy as np
from jax import lax

BX = 4
BY = 4
LZ = 4
CAP = 64
P_SIZE = 4
Q = 56
NX = 32
NY = 16


def draw_counts(key, part):
    level_key = jax.random.fold_in(key, 101)
    base_key = jax.random.fold_in(key, 202)
    levels = jax.random.randint(level_key, (NX // BX, NY // BY), 0, 4, dtype=jnp.int32)
    levels = jnp.repeat(jnp.repeat(levels, BX, axis=0), BY, axis=1)[..., None]
    divisor = jnp.power(jnp.int32(2), levels).astype(jnp.int32)
    base = jax.random.randint(base_key, (NX, NY, LZ), 1, CAP + 1, dtype=jnp.int32)
    counts = jnp.maximum(base // divisor, 1).astype(jnp.int32)
    return counts.at[0, 0, 0].set(jnp.int32(CAP))


def draw_positions(key, part):
    shape = (3, NX, NY, LZ * CAP)
    pick_key = jax.random.fold_in(key, 301)
    side_key = jax.random.fold_in(key, 302)
    jitter_key = jax.random.fold_in(key, 303)
    middle_key = jax.random.fold_in(key, 304)
    share = 0.6
    pick = jax.random.uniform(pick_key, shape, jnp.float32) < share
    side = jax.random.uniform(side_key, shape, jnp.float32) < 0.5
    jitter = jax.random.uniform(jitter_key, shape, jnp.float32, 0.0, 0.02)
    ends = jnp.where(side, 1.0 - jitter, jitter)
    middle = jax.random.uniform(middle_key, shape, jnp.float32, 0.0, 1.0)
    return jnp.where(pick, ends, middle).astype(jnp.float32)


def level_of(rng, dims, pieces, least, largest):
    level, own = 1.0, jax.random.fold_in(rng, 6)
    for axis_at, blocks in pieces:
        heights = jnp.exp(jax.random.uniform(jax.random.fold_in(own, axis_at), (blocks,), jnp.float32, least / len(pieces), largest / len(pieces)))
        level = level * jnp.repeat(heights, dims[axis_at] // blocks).reshape([-1 if axis == axis_at else 1 for axis in range(len(dims))])
    return level


def normal_values(stream_key, extent, deviation, limit, cuts=(), kind=jnp.bfloat16):
    values = deviation * jax.random.normal(stream_key, extent, jnp.float32)
    if cuts:
        values = values * level_of(stream_key, extent, cuts, -0.22, 0.18)
    return jnp.clip(values, -limit, limit).astype(kind)


def setup_inputs(seed: int = 0) -> dict:
    keys = jax.random.split(jax.random.key(seed), 9)
    positions = draw_positions(jax.random.fold_in(keys[8], 71), 0)
    masses = jnp.clip(jnp.exp(math.log(0.02) - 2.30258502 * jax.random.uniform(keys[1], (NX, NY, LZ * CAP), jnp.float32) ** level_of(keys[1], (NX, NY, LZ * CAP), ((0, 8), (1, 4)), -0.2, 0.2)), 0.002, 0.02)
    counts = draw_counts(jax.random.fold_in(keys[8], 71), 0)
    multipoles = normal_values(keys[3], (NX, NY, LZ * Q), 1.0, 6.0, ((0, 8), (1, 4)), jnp.float32)
    parent_local = normal_values(keys[4], (NX // 2, NY // 2, (LZ // 2) * Q), 1.0, 6.0, ((0, 8), (1, 4)), jnp.float32)
    m2l_ops = normal_values(keys[5], (343, Q * Q), (189 * Q) ** -0.5, 0.0625, (), jnp.float32)
    l2l_ops = normal_values(keys[6], (8, Q, Q), Q ** -0.5, 0.75, (), jnp.float32)
    check_to_equiv = normal_values(keys[7], (Q, Q), (16 * Q) ** -0.5, 0.1875, (), jnp.float32)
    return {"positions": positions, "masses": masses, "counts": counts, "multipoles": multipoles, "parent_local": parent_local, "m2l_ops": m2l_ops, "l2l_ops": l2l_ops, "check_to_equiv": check_to_equiv}


SOFTEN = 0.05

def surface_points():
    steps_grid = np.stack(np.meshgrid(np.arange(P_SIZE), np.arange(P_SIZE), np.arange(P_SIZE), indexing='ij'), -1).reshape(-1, 3)
    on_face = np.any((steps_grid == 0) | (steps_grid == P_SIZE - 1), axis=1)
    chosen = steps_grid[on_face] / (P_SIZE - 1)
    return jnp.asarray(0.5 + 1.4 * (chosen - 0.5), jnp.float32)

def admits(shift, parity):
    return (shift >= -2 - parity) & (shift <= 3 - parity)

def admitted(shift_x, shift_y, shift_z, parity_x, parity_y, parity_z):
    distant = jnp.maximum(jnp.maximum(jnp.abs(shift_x), jnp.abs(shift_y)), jnp.abs(shift_z)) >= 2
    return admits(shift_x, parity_x) & admits(shift_y, parity_y) & admits(shift_z, parity_z) & distant

def downward(m2l_check, parent_local, l2l_ops, check_to_equiv):
    parent_x, parent_y, parent_width = parent_local.shape
    parent_z = parent_width // Q
    parents = parent_local.reshape(parent_x, parent_y, parent_z, Q)
    spread = jnp.einsum('xyzq,oqr->xyzor', parents, l2l_ops, precision=lax.Precision.HIGHEST)
    spread = spread.reshape(parent_x, parent_y, parent_z, 2, 2, 2, Q).transpose(0, 3, 1, 4, 2, 5, 6)
    spread = spread.reshape(2 * parent_x, 2 * parent_y, 2 * parent_z, Q)
    check_field = m2l_check + spread
    return jnp.einsum('xyzq,qr->xyzr', check_field, check_to_equiv, precision=lax.Precision.HIGHEST)

def near_field(targets, padded):
    size_x, size_y, size_z, slot_count = targets.shape[1:]
    summed = jnp.zeros((size_x, size_y, size_z, slot_count), jnp.float32)
    for shift_x in (-1, 0, 1):
        for shift_y in (-1, 0, 1):
            for shift_z in (-1, 0, 1):
                sources = padded[:, 1 + shift_x:1 + shift_x + size_x, 1 + shift_y:1 + shift_y + size_y, 1 + shift_z:1 + shift_z + size_z, :]
                distance = jnp.zeros((size_x, size_y, size_z, slot_count, slot_count), jnp.float32) + SOFTEN * SOFTEN
                for comp, shift in enumerate((shift_x, shift_y, shift_z)):
                    gap = targets[comp][..., :, None] - (sources[comp][..., None, :] + float(shift))
                    distance = distance + gap * gap
                summed = summed + lax.optimization_barrier(jnp.sum(sources[3][..., None, :] * lax.rsqrt(distance), axis=-1))
    return summed

def far_field(targets, local_field, points):
    distance = jnp.zeros(targets.shape[1:] + (points.shape[0],), jnp.float32)
    for comp in range(3):
        gap = targets[comp][..., None] - points[:, comp]
        distance = distance + gap * gap
    return jnp.einsum('xyzcq,xyzq->xyzc', lax.rsqrt(distance), local_field, precision=lax.Precision.HIGHEST)

def m2l_whole(multipoles, m2l_ops):
    grid_cells = multipoles.reshape(NX, NY, LZ, Q)
    matrices = m2l_ops.reshape(343, Q, Q)
    padded = jnp.pad(grid_cells, ((3, 3), (3, 3), (3, 3), (0, 0)))
    parity_x = (jnp.arange(NX, dtype=jnp.int32) % 2)[:, None, None]
    parity_y = (jnp.arange(NY, dtype=jnp.int32) % 2)[None, :, None]
    parity_z = (jnp.arange(LZ, dtype=jnp.int32) % 2)[None, None, :]

    def step_offset(summed, offset_id):
        shift_x = offset_id // 49 - 3
        shift_y = offset_id // 7 % 7 - 3
        shift_z = offset_id % 7 - 3
        starts = ((shift_x + 3).astype(jnp.int32), (shift_y + 3).astype(jnp.int32), (shift_z + 3).astype(jnp.int32), jnp.int32(0))
        sources = lax.dynamic_slice(padded, starts, (NX, NY, LZ, Q))
        weights = admitted(shift_x, shift_y, shift_z, parity_x, parity_y, parity_z).astype(jnp.float32)
        contribution = jnp.einsum('xyzq,qr->xyzr', sources, matrices[offset_id], precision=lax.Precision.HIGHEST)
        return (summed + weights[..., None] * contribution, None)
    start_sum = jnp.zeros((NX, NY, LZ, Q), jnp.float32)
    summed, _ = lax.scan(step_offset, start_sum, jnp.arange(343, dtype=jnp.int32))
    return summed

def reference(positions, masses, counts, multipoles, parent_local, m2l_ops, l2l_ops, check_to_equiv):
    slot_index = jnp.arange(CAP, dtype=jnp.int32)
    alive_mask = (slot_index < counts[..., None]).astype(jnp.float32)
    targets = positions.reshape(3, NX, NY, LZ, CAP)
    weighed = masses.reshape(NX, NY, LZ, CAP) * alive_mask
    packed = jnp.concatenate([targets, weighed[None]], 0)
    padded = jnp.pad(packed, ((0, 0), (1, 1), (1, 1), (1, 1), (0, 0)))
    m2l_check = m2l_whole(multipoles, m2l_ops)
    local_field = downward(m2l_check, parent_local, l2l_ops, check_to_equiv)
    points = surface_points()

    def one_row(row_id):
        row_block = lax.dynamic_slice_in_dim(padded, row_id, 3, 1)
        row_targets = lax.dynamic_slice_in_dim(targets, row_id, 1, 1)
        row_local = lax.dynamic_slice_in_dim(local_field, row_id, 1, 0)
        return near_field(row_targets, row_block) + far_field(row_targets, row_local, points)
    field_rows = lax.map(one_row, jnp.arange(NX, dtype=jnp.int32))
    potential = field_rows.reshape(NX, NY, LZ, CAP) * alive_mask
    return (potential.reshape(NX, NY, LZ * CAP), local_field.reshape(NX, NY, LZ * Q))
```

```python
import functools

import jax
import jax.numpy as jnp
import numpy as np
from jax import lax
from jax.experimental import pallas as pl
from jax.experimental.pallas import tpu as pltpu
from jax.sharding import PartitionSpec as P

CAP = 64
P_SIZE = 4
Q = 56
SOFTEN = 0.05
LANES = 128
BIG = 2.0**100
DEAD = 2.0**120
F32, BF16 = jnp.float32, jnp.bfloat16
REACH = 3
SPAN = 2 * REACH + 1
KROWS = 136


def surface_points():
    steps = np.stack(
        np.meshgrid(np.arange(P_SIZE), np.arange(P_SIZE), np.arange(P_SIZE), indexing="ij"), -1
    ).reshape(-1, 3)
    on_face = np.any((steps == 0) | (steps == P_SIZE - 1), axis=1)
    return (0.5 + 1.4 * (steps[on_face] / (P_SIZE - 1) - 0.5)).astype(np.float32)


def admits(shift, parity):
    return -2 - parity <= shift <= 3 - parity


def split2(x):
    hi = x.astype(BF16)
    return hi, (x - hi.astype(F32)).astype(BF16)


def split3(x):
    hi = x.astype(BF16).astype(F32)
    rest = x - hi
    mid = rest.astype(BF16).astype(F32)
    return hi, mid, rest - mid


def dot(a, b):
    return jnp.dot(a, b, preferred_element_type=F32)


def dot_exact(a, b):
    return jnp.dot(a, b, preferred_element_type=F32, precision=lax.Precision.HIGHEST)


def column_weights(masses, counts, x, y, sz):
    lane = lax.broadcasted_iota(jnp.int32, (1, sz * CAP), 1)
    limit = jnp.zeros((1, sz * CAP), jnp.int32)
    for z in range(sz):
        limit = jnp.where(lane // CAP == z, counts[x, y, z], limit)
    return jnp.where(lane % CAP < limit, masses, 0.0)


def pack_row_kernel(dims, pos, mass, counts, poles, first, last):
    sx, sy, sz = dims
    width = sz * Q
    for out, x0, xp in ((first, 0, 0), (last, sx - REACH, sx - 1)):
        out[...] = jnp.zeros_like(out)
        for x in range(REACH):
            out[x * sy : (x + 1) * sy, 0:width] = poles[x0 + x]
        base = REACH * sy
        for c in range(3):
            out[base + c * sy : base + (c + 1) * sy, :] = pos[c, xp] - 0.5
        for y in range(sy):
            row = base + 3 * sy + y
            out[row : row + 1, :] = column_weights(mass[xp, y : y + 1, :], counts, xp, y, sz)


def pack_col_kernel(dims, pos, mass, counts, poles, low, high, first, last):
    sx, sy, sz = dims
    width = sz * Q
    base_in = REACH * sy
    base = REACH * (sx + 2 * REACH)
    px = sx + 2
    for out, y0, yp in ((first, 0, 0), (last, sy - REACH, sy - 1)):
        out[...] = jnp.zeros_like(out)
        for x in range(sx + 2 * REACH):
            if x < REACH:
                rows = low[x * sy + y0 : x * sy + y0 + REACH, :]
                out[x * REACH : (x + 1) * REACH, :] = rows
            elif x < REACH + sx:
                rows = poles[x - REACH, y0 : y0 + REACH, :]
                out[x * REACH : (x + 1) * REACH, 0:width] = rows
            else:
                at = (x - REACH - sx) * sy + y0
                out[x * REACH : (x + 1) * REACH, :] = high[at : at + REACH, :]
        for c in range(4):
            for x in range(px):
                if x == 0:
                    row = low[base_in + c * sy + yp : base_in + c * sy + yp + 1, :]
                elif x == px - 1:
                    row = high[base_in + c * sy + yp : base_in + c * sy + yp + 1, :]
                elif c < 3:
                    row = pos[c, x - 1, yp : yp + 1, :] - 0.5
                else:
                    row = column_weights(mass[x - 1, yp : yp + 1, :], counts, x - 1, yp, sz)
                out[base + c * px + x : base + c * px + x + 1, :] = row


def gather_constant(dims):
    sx, sy, _ = dims
    cells = [(x + REACH, y + REACH) for x in range(sx) for y in range(sy)]
    cells += [(x, y + REACH) for x in range(REACH) for y in range(sy)]
    cells += [(x + REACH + sx, y + REACH) for x in range(REACH) for y in range(sy)]
    cells += [(x, y) for x in range(sx + 2 * REACH) for y in range(REACH)]
    cells += [(x, y + REACH + sy) for x in range(sx + 2 * REACH) for y in range(REACH)]
    at = {cell: i for i, cell in enumerate(cells)}
    pick = np.zeros((2 * LANES, sx * sy * LANES), np.float32)
    for x in range(sx):
        for y in range(sy):
            for a in range(SPAN):
                for b in range(SPAN):
                    if admits(a - REACH, x % 2) and admits(b - REACH, y % 2):
                        for half in range(2):
                            col = (x * sy + y) * LANES + half * 64 + a * SPAN + b
                            pick[half * LANES + at[(x + a, y + b)], col] = 1.0
    return pick


def spread_constant(dims):
    sx, sy, sz = dims
    parents = (sx // 2) * (sy // 2) * (sz // 2)
    pick = np.zeros((sx * sy * sz, 8 * parents), np.float32)
    for z in range(sz):
        for x in range(sx):
            for y in range(sy):
                octant = 4 * (x % 2) + 2 * (y % 2) + z % 2
                parent = ((z // 2) * (sx // 2) + x // 2) * (sy // 2) + y // 2
                pick[(z * sx + x) * sy + y, octant * parents + parent] = 1.0
    return pick


def main_kernel(
    dims,
    pos, mass, counts, poles, low1, high1, low2, high2, parents, ops, tail, l2l, c2e, pick, spread,
    points,
    potential, local_out,
    su, feats, lhs, rfeats, near, sm, picked, lm, raw, table, dens, sems,
):
    sx, sy, sz = dims
    hx, hy = sx + 2, sy + 2
    cols = sx * sy
    tiles = raw.shape[0]
    width = ops.shape[1]

    whole = width // LANES

    def fetch(j):
        return pltpu.make_async_copy(ops.at[:, pl.ds(j * LANES, LANES)], raw.at[j], sems.at[j])

    for j in range(whole):
        fetch(j).start()
    if whole < tiles:
        raw[whole] = tail[...]

    su[...] = jnp.zeros_like(su)
    base1 = REACH * sy
    base2 = REACH * (sx + 2 * REACH)
    for c in range(4):
        for x in range(sx):
            at = (x + 1) * hy + 1
            if c < 3:
                su[c, at : at + sy, :] = pos[c, x] - 0.5
            else:
                for y in range(sy):
                    su[c, at + y : at + y + 1, :] = column_weights(
                        mass[x, y : y + 1, :], counts, x, y, sz
                    )
        su[c, 1 : 1 + sy, :] = low1[base1 + c * sy : base1 + (c + 1) * sy, :]
        at = (hx - 1) * hy + 1
        su[c, at : at + sy, :] = high1[base1 + c * sy : base1 + (c + 1) * sy, :]
        for x in range(hx):
            row = base2 + c * hx + x
            su[c, x * hy : x * hy + 1, :] = low2[row : row + 1, :]
            su[c, x * hy + hy - 1 : x * hy + hy, :] = high2[row : row + 1, :]

    groups = su.shape[1] // 8
    for half in range(2):
        lanes = slice(half * LANES, (half + 1) * LANES)
        shape = (8, LANES)

        def of_group(i, carry, half=half, lanes=lanes):
            at = pl.multiple_of(i * 8, 8)
            rows = lax.broadcasted_iota(jnp.int32, shape, 0) + at
            lane = lax.broadcasted_iota(jnp.int32, shape, 1) + half * LANES
            arrays = [su[c, pl.ds(at, 8), lanes] for c in range(4)]
            for k, value in source_features_at(sz, hy, arrays, rows, lane):
                feats[half, pl.ds(at * KROWS + k, 8, stride=KROWS), :] = value
            return carry

        lax.fori_loop(0, groups, of_group, 0)

    def turn(i, carry):
        at = pl.multiple_of(i * KROWS, 8)
        for half in range(2):
            block = feats[half, pl.ds(at, LANES), :]
            to = pl.multiple_of(i * (2 * LANES) + half * LANES, LANES)
            lhs[pl.ds(to, LANES), :] = block.T.astype(BF16)
        return carry

    lax.fori_loop(0, hx * hy, turn, 0)

    for half in range(2):
        lanes = slice(half * LANES, (half + 1) * LANES)
        for i in range(cols // 8):
            at = i * 8
            rows = lax.broadcasted_iota(jnp.int32, (8, LANES), 0) + at
            lane = lax.broadcasted_iota(jnp.int32, (8, LANES), 1) + half * LANES
            arrays = [
                jnp.concatenate(
                    [pos[c, (at + r) // sy] for r in range(0, 8, sy)], axis=0
                )[:, lanes]
                - 0.5
                for c in range(3)
            ]
            for k, value in target_features_at(dims, arrays, rows, lane):
                rfeats[half, pl.ds(at * KROWS + k, 8, stride=KROWS), :] = value

    def near_row(x, carry):
        for y in range(sy):
            at = pl.multiple_of((x * sy + y) * KROWS, 8)
            rhs = jnp.concatenate(
                [rfeats[0, pl.ds(at, LANES), :], rfeats[1, pl.ds(at, LANES), :]], axis=1
            ).astype(BF16)
            total = [jnp.zeros((8, LANES), F32) for _ in range(2)]
            for dx in range(3):
                for dy in range(3):
                    src = ((x + dx) * hy + y + dy) * (sz * CAP)
                    for z in range(sz):
                        rows = pl.multiple_of(src + z * CAP, CAP)
                        d2 = dot(lhs[pl.ds(rows, CAP), :], rhs)
                        for half in range(2):
                            if any(abs(z - t) <= 1 for t in (2 * half, 2 * half + 1)):
                                part = lax.rsqrt(d2[:, half * LANES : (half + 1) * LANES])
                                total[half] = total[half] + jnp.sum(
                                    part.reshape(CAP // 8, 8, LANES), axis=0
                                )
            near[pl.ds(x * sy + y, 1), :] = jnp.concatenate(
                [jnp.sum(part, axis=0, keepdims=True) for part in total], axis=1
            )
        return carry

    lax.fori_loop(0, sx, near_row, 0)

    sm[...] = jnp.zeros_like(sm)
    for x in range(sx):
        sm[x * sy : (x + 1) * sy, 0 : sz * Q] = poles[x]
    at = cols
    for ref, count in (
        (low1, REACH * sy),
        (high1, REACH * sy),
        (low2, REACH * (sx + 2 * REACH)),
        (high2, REACH * (sx + 2 * REACH)),
    ):
        sm[at : at + count, :] = ref[0:count, :]
        at += count
    for pair in range(sz // 2):
        his, los = [], []
        for zi in range(2):
            z = 2 * pair + zi
            rolled = pltpu.roll(sm[...], (2 * LANES - z * Q) % (2 * LANES), 1)[:, 0:LANES]
            hi, lo = split2(rolled.T[0:64, :])
            his.append(hi)
            los.append(lo)
        keep = lax.broadcasted_iota(jnp.int32, (64, 2 * LANES), 0) < Q
        his = jnp.where(keep, jnp.concatenate(his, axis=1).astype(F32), 0.0)
        los = jnp.where(keep, jnp.concatenate(los, axis=1).astype(F32), 0.0)
        picked[...] = jnp.concatenate([his, los], axis=0).astype(BF16)
        for xy in range(0, cols, 2):
            block = dot(picked[...], pick[:, xy * LANES : (xy + 2) * LANES])
            for i in range(2):
                lm[pair, pl.ds(xy + i, 2 * 64, stride=cols), :] = block[
                    :, i * LANES : (i + 1) * LANES
                ]

    ab = lax.broadcasted_iota(jnp.int32, (64, LANES), 0)
    closeby = (jnp.abs(ab // SPAN - REACH) <= 1) & (jnp.abs(ab % SPAN - REACH) <= 1)
    for j in range(tiles):
        if j < whole:
            fetch(j).wait()
        for c in range(SPAN):
            block = raw[j, pl.ds(c, SPAN * SPAN, stride=SPAN), :]
            block = jnp.concatenate(
                [block, jnp.zeros((64 - SPAN * SPAN, LANES), F32)], axis=0
            )
            if abs(c - REACH) <= 1:
                block = jnp.where(closeby, 0.0, block)
            if (j + 1) * LANES > width:
                lane = lax.broadcasted_iota(jnp.int32, (64, LANES), 1)
                block = jnp.where(lane < width - j * LANES, block, 0.0)
            hi, lo = split2(block)
            table[c * 64 : (c + 1) * 64, 2 * j * LANES : (2 * j + 1) * LANES] = hi
            table[c * 64 : (c + 1) * 64, (2 * j + 1) * LANES : (2 * j + 2) * LANES] = lo

    period = 16
    lane16 = lax.broadcasted_iota(jnp.int32, (cols, LANES), 1)
    check = [jnp.zeros((cols, LANES), F32) for _ in range(sz)]
    for t in range(period * Q // LANES):
        members = [s for s in range(period) if s * Q < (t + 1) * LANES and (s + 1) * Q > t * LANES]
        rows = len(members) * cols
        left = []
        for j in range(-(-Q // period)):
            if j * (period * Q // LANES) + t >= tiles:
                continue
            start = (j * period + members[0]) * cols
            left.append(
                jnp.concatenate(
                    [
                        jnp.concatenate(
                            [
                                lm[p, h * 64 * cols + start : h * 64 * cols + start + rows, :]
                                for p in range(sz // 2)
                            ],
                            axis=1,
                        )
                        for h in range(2)
                    ],
                    axis=0,
                ).astype(BF16)
            )
        for z in range(sz):
            total = None
            for j, block in enumerate(left):
                tile = j * (period * Q // LANES) + t
                first = (REACH - z) * 64
                part = dot(
                    block,
                    table[first : first + sz * 64, 2 * tile * LANES : (2 * tile + 2) * LANES],
                )
                total = part if total is None else total + part
            both = total[0:rows, 0:LANES] + (
                total[0:rows, LANES : 2 * LANES] + total[rows : 2 * rows, 0:LANES]
            )
            for i, s in enumerate(members):
                offset = s * Q - t * LANES
                part = both[i * cols : (i + 1) * cols, :]
                part = jnp.where((lane16 >= offset) & (lane16 < offset + Q), part, 0.0)
                check[z] = check[z] + pltpu.roll(part, (-offset) % LANES, 1)

    rows = []
    for pz in range(sz // 2):
        for x in range(sx // 2):
            rows.append(parents[x, :, pz * Q : (pz + 1) * Q])
    above = jnp.concatenate(rows, axis=0)
    below = jnp.concatenate([dot_exact(above, l2l[o]) for o in range(8)], axis=0)
    field = jnp.concatenate([part[:, 0:Q] for part in check], axis=0)
    field = field + dot_exact(spread[...], below)
    local = dot_exact(field, c2e[...])
    dens[...] = jnp.zeros_like(dens)
    dens[0 : sz * cols, 0:Q] = local
    flat = None
    for z in range(sz):
        part = jnp.concatenate(
            [dens[z * cols : (z + 1) * cols, :], jnp.zeros((cols, LANES), F32)], axis=1
        )
        part = pltpu.roll(part, z * Q, 1) if z else part
        flat = part if flat is None else flat + part
    for x in range(sx):
        local_out[x] = flat[x * sy : (x + 1) * sy, 0 : sz * Q]

    turned = dens[...].T[0:64, :]
    hi, lo = split2(turned[:, 0 : sz * cols])
    weights = jnp.concatenate([hi.astype(F32), lo.astype(F32)], axis=1).astype(BF16)
    row = lax.broadcasted_iota(jnp.int32, (2 * sz * cols, sz * CAP), 0) % (sz * cols)
    lane = lax.broadcasted_iota(jnp.int32, (2 * sz * cols, sz * CAP), 1)
    owner = row - (lane // CAP) * cols
    for x in range(sx):
        for y in range(sy):
            one_hot = jnp.where(owner == x * sy + y, 1.0, 0.0).astype(BF16)
            spread_out = dot(weights, one_hot)
            sums = []
            for half in range(2):
                lanes = slice(half * LANES, (half + 1) * LANES)
                d2 = jnp.zeros((64, LANES), F32)
                for c in range(3):
                    gap = pos[c, x, y : y + 1, lanes] - points[c]
                    d2 = d2 + gap * gap
                part = spread_out[:, lanes] * lax.rsqrt(d2)
                sums.append(jnp.sum(part, axis=0, keepdims=True))
            i = x * sy + y
            value = near[i : i + 1, :] + jnp.concatenate(sums, axis=1)
            potential[x, y : y + 1, :] = column_weights(value, counts, x, y, sz)


def source_features_at(sz, hy, arrays, rows, lane):
    ux, uy, uz, w = arrays
    shape = w.shape
    live = w > 0
    g = jnp.where(live, 1.0 / jnp.where(live, w * w, 1.0), 0.0)
    n = (ux * ux + uy * uy + uz * uz + SOFTEN * SOFTEN) * g
    n = jnp.where(live, n, DEAD)
    v = [split3(-2.0 * u * g) for u in (ux, uy, uz)]
    ones = [
        [(rows // hy) % 3 == m for m in range(3)],
        [(rows % hy) % 3 == m for m in range(3)],
        [lane // CAP == m for m in range(sz)],
    ]
    k = 0
    for c in range(3):
        for piece in (0, 0, 0, 1, 1, 2):
            yield k, v[c][piece]
            k += 1
    for c in range(3):
        for mask in ones[c]:
            for piece in range(3):
                yield k, jnp.where(mask, v[c][piece], 0.0)
                k += 1
    for piece in split3(n):
        yield k, piece
        k += 1
    gs = split3(g)
    for c in range(3):
        for mask in ones[c]:
            for piece in (0, 0, 0, 1, 1, 2):
                yield k, jnp.where(mask, gs[piece], 0.0)
                k += 1
    while k < LANES:
        yield k, jnp.zeros(shape, F32)
        k += 1


def target_features_at(dims, arrays, rows, lane):
    sx, sy, sz = dims
    shape = lane.shape
    place = (rows // sy, rows % sy, lane // CAP)
    t = [split3(u) for u in arrays]

    def shift(c, m):
        if c == 2:
            return (place[2] - m).astype(F32)
        return 1.0 - ((m - place[c] + 6) % 3).astype(F32)

    k = 0
    for c in range(3):
        for piece in (0, 1, 2, 0, 1, 0):
            yield k, t[c][piece]
            k += 1
    for c in range(3):
        for m in range(sz if c == 2 else 3):
            for _ in range(3):
                yield k, shift(c, m)
                k += 1
    for _ in range(3):
        yield k, jnp.ones(shape, F32)
        k += 1
    for c in range(3):
        for m in range(sz if c == 2 else 3):
            moved = arrays[c] + shift(c, m)
            parts = list(split3(moved * moved))
            if c == 2:
                reach = jnp.abs(place[2] - m) <= 1
                parts = [jnp.where(reach, p, BIG if i == 0 else 0.0) for i, p in enumerate(parts)]
            for piece in (0, 1, 2, 0, 1, 0):
                yield k, parts[piece]
                k += 1
    while k < LANES:
        yield k, jnp.zeros(shape, F32)
        k += 1


VMEM = pl.BlockSpec(memory_space=pltpu.VMEM)
SMEM = pl.BlockSpec(memory_space=pltpu.SMEM)
ANY = pl.BlockSpec(memory_space=pl.ANY)


def round_up(n, m):
    return -(-n // m) * m


def pack_row(dims, pos, mass, counts, poles):
    sx, sy, sz = dims
    rows = round_up((REACH + 4) * sy, 8)
    shape = jax.ShapeDtypeStruct((rows, sz * CAP), F32)
    return pl.pallas_call(
        functools.partial(pack_row_kernel, dims),
        out_shape=(shape, shape),
        in_specs=[VMEM, VMEM, SMEM, VMEM],
        out_specs=(VMEM, VMEM),
        name="pack_row",
    )(pos, mass, counts, poles)


def pack_col(dims, pos, mass, counts, poles, low, high):
    sx, sy, sz = dims
    rows = round_up(REACH * (sx + 2 * REACH) + 4 * (sx + 2), 8)
    shape = jax.ShapeDtypeStruct((rows, sz * CAP), F32)
    return pl.pallas_call(
        functools.partial(pack_col_kernel, dims),
        out_shape=(shape, shape),
        in_specs=[VMEM, VMEM, SMEM, VMEM, VMEM, VMEM],
        out_specs=(VMEM, VMEM),
        name="pack_col",
    )(pos, mass, counts, poles, low, high)


def main_call(dims, pos, mass, counts, poles, low1, high1, low2, high2, parents, ops, l2l, c2e):
    sx, sy, sz = dims
    cols = sx * sy
    halo = round_up((sx + 2) * (sy + 2), 8)
    pick = jnp.asarray(gather_constant(dims), BF16)
    spread = jnp.asarray(spread_constant(dims))
    points = np.full((3, 64, LANES), 10.0, np.float32)
    points[:, :Q, :] = surface_points().T[:, :, None]
    tiles = -(-ops.shape[1] // LANES)
    last = pl.BlockSpec((ops.shape[0], LANES), lambda _: (0, tiles - 1))
    return pl.pallas_call(
        functools.partial(main_kernel, dims),
        grid=(1,),
        out_shape=(
            jax.ShapeDtypeStruct((sx, sy, sz * CAP), F32),
            jax.ShapeDtypeStruct((sx, sy, sz * Q), F32),
        ),
        in_specs=[VMEM, VMEM, SMEM] + [VMEM] * 6 + [ANY, last] + [VMEM] * 5,
        out_specs=(VMEM, VMEM),
        scratch_shapes=[
            pltpu.VMEM((4, halo, sz * CAP), F32),
            pltpu.VMEM((2, halo * KROWS, LANES), F32),
            pltpu.VMEM(((sx + 2) * (sy + 2) * sz * CAP, LANES), BF16),
            pltpu.VMEM((2, cols * KROWS, LANES), F32),
            pltpu.VMEM((cols, sz * CAP), F32),
            pltpu.VMEM((LANES, 2 * LANES), F32),
            pltpu.VMEM((LANES, 2 * LANES), BF16),
            pltpu.VMEM((sz // 2, 2 * 64 * cols, LANES), F32),
            pltpu.VMEM((tiles, ops.shape[0], LANES), F32),
            pltpu.VMEM((SPAN * 64, 2 * tiles * LANES), BF16),
            pltpu.VMEM((LANES, LANES), F32),
            pltpu.SemaphoreType.DMA((tiles,)),
        ],
        compiler_params=pltpu.CompilerParams(vmem_limit_bytes=60 << 20),
        name="fields",
    )(pos, mass, counts, poles, low1, high1, low2, high2, parents, ops, ops, l2l, c2e, pick, spread,
      jnp.asarray(points))


def body(positions, masses, counts, multipoles, parent_local, m2l_ops, l2l_ops, check_to_equiv):
    sx, sy, slots = masses.shape
    dims = (sx, sy, slots // CAP)

    def exchange(first, last, axis):
        count = lax.axis_size(axis)
        up = [(i, i + 1) for i in range(count - 1)]
        down = [(b, a) for a, b in up]
        return lax.ppermute(last, axis, up), lax.ppermute(first, axis, down)

    first, last = pack_row(dims, positions, masses, counts, multipoles)
    low1, high1 = exchange(first, last, "row")
    first, last = pack_col(dims, positions, masses, counts, multipoles, low1, high1)
    low2, high2 = exchange(first, last, "col")
    return main_call(
        dims, positions, masses, counts, multipoles, low1, high1, low2, high2,
        parent_local, m2l_ops, l2l_ops, check_to_equiv,
    )


def solution(mesh):
    return jax.shard_map(
        body,
        mesh=mesh,
        in_specs=(
            P(None, "row", "col", None),
            P("row", "col", None),
            P("row", "col", None),
            P("row", "col", None),
            P("row", "col", None),
            P(),
            P(),
            P(),
        ),
        out_specs=(P("row", "col", None), P("row", "col", None)),
        check_vma=False,
    )
```

```python
import functools

import jax
import jax.numpy as jnp
import numpy as np
from jax import lax
from jax.experimental import pallas as pl
from jax.experimental.pallas import tpu as pltpu
from jax.sharding import PartitionSpec as P

CAP = 64
P_SIZE = 4
Q = 56
SOFTEN = 0.05
LANES = 128
BIG = 2.0**100
DEAD = 2.0**120
F32, BF16 = jnp.float32, jnp.bfloat16
REACH = 3
SPAN = 2 * REACH + 1
KROWS = 136


def surface_points():
    steps = np.stack(
        np.meshgrid(np.arange(P_SIZE), np.arange(P_SIZE), np.arange(P_SIZE), indexing="ij"), -1
    ).reshape(-1, 3)
    on_face = np.any((steps == 0) | (steps == P_SIZE - 1), axis=1)
    return (0.5 + 1.4 * (steps[on_face] / (P_SIZE - 1) - 0.5)).astype(np.float32)


def admits(shift, parity):
    return -2 - parity <= shift <= 3 - parity


def split2(x):
    hi = x.astype(BF16)
    return hi, (x - hi.astype(F32)).astype(BF16)


def split3(x):
    hi = x.astype(BF16).astype(F32)
    rest = x - hi
    mid = rest.astype(BF16).astype(F32)
    return hi, mid, rest - mid


def dot(a, b):
    return jnp.dot(a, b, preferred_element_type=F32)


def dot_exact(a, b):
    return jnp.dot(a, b, preferred_element_type=F32, precision=lax.Precision.HIGHEST)


def column_weights(masses, counts, x, y, sz):
    lane = lax.broadcasted_iota(jnp.int32, (1, sz * CAP), 1)
    limit = jnp.zeros((1, sz * CAP), jnp.int32)
    for z in range(sz):
        limit = jnp.where(lane // CAP == z, counts[x, y, z], limit)
    return jnp.where(lane % CAP < limit, masses, 0.0)


def is_odd(axis):
    return lax.axis_index(axis) % 2 == 1


def store_pair(odd, to_first_pair, to_second_pair, rows, lanes, low_edge, high_edge):
    to_first_pair[rows, lanes] = jnp.where(odd, low_edge, high_edge)
    to_second_pair[rows, lanes] = jnp.where(odd, high_edge, low_edge)


def pack_row_kernel(dims, pos, mass, counts, poles, send_a, send_b):
    sx, sy, sz = dims
    odd = is_odd("row")
    store = functools.partial(store_pair, odd, send_a, send_b)
    every = slice(0, sz * CAP)
    send_a[...] = jnp.zeros_like(send_a)
    send_b[...] = jnp.zeros_like(send_b)
    for x in range(REACH):
        store(slice(x * sy, (x + 1) * sy), slice(0, sz * Q), poles[x], poles[sx - REACH + x])
    base = REACH * sy
    for c in range(3):
        rows = slice(base + c * sy, base + (c + 1) * sy)
        store(rows, every, pos[c, 0] - 0.5, pos[c, sx - 1] - 0.5)
    for y in range(sy):
        row = base + 3 * sy + y
        store(
            slice(row, row + 1),
            every,
            column_weights(mass[0, y : y + 1, :], counts, 0, y, sz),
            column_weights(mass[sx - 1, y : y + 1, :], counts, sx - 1, y, sz),
        )


def pack_col_kernel(dims, pos, mass, counts, poles, got_a, got_b, send_a, send_b, low, high):
    sx, sy, sz = dims
    odd_row = is_odd("row")
    low[...] = jnp.where(odd_row, got_a[...], got_b[...])
    high[...] = jnp.where(odd_row, got_b[...], got_a[...])
    store = functools.partial(store_pair, is_odd("col"), send_a, send_b)
    every = slice(0, sz * CAP)
    base_in = REACH * sy
    base = REACH * (sx + 2 * REACH)
    px = sx + 2
    send_a[...] = jnp.zeros_like(send_a)
    send_b[...] = jnp.zeros_like(send_b)
    for x in range(sx + 2 * REACH):
        rows = slice(x * REACH, (x + 1) * REACH)
        if REACH <= x < REACH + sx:
            own = poles.at[x - REACH]
            store(rows, slice(0, sz * Q), own[0:REACH, :], own[sy - REACH : sy, :])
        else:
            ref, at = (low, x * sy) if x < REACH else (high, (x - REACH - sx) * sy)
            store(rows, every, ref[at : at + REACH, :], ref[at + sy - REACH : at + sy, :])
    for c in range(4):
        for x in range(px):
            edges = []
            for y in (0, sy - 1):
                at = base_in + c * sy + y
                if x == 0:
                    row = low[at : at + 1, :]
                elif x == px - 1:
                    row = high[at : at + 1, :]
                elif c < 3:
                    row = pos[c, x - 1, y : y + 1, :] - 0.5
                else:
                    row = column_weights(mass[x - 1, y : y + 1, :], counts, x - 1, y, sz)
                edges.append(row)
            at = base + c * px + x
            store(slice(at, at + 1), every, *edges)


def gather_constant(dims):
    sx, sy, _ = dims
    cells = [(x + REACH, y + REACH) for x in range(sx) for y in range(sy)]
    cells += [(x, y + REACH) for x in range(REACH) for y in range(sy)]
    cells += [(x + REACH + sx, y + REACH) for x in range(REACH) for y in range(sy)]
    cells += [(x, y) for x in range(sx + 2 * REACH) for y in range(REACH)]
    cells += [(x, y + REACH + sy) for x in range(sx + 2 * REACH) for y in range(REACH)]
    at = {cell: i for i, cell in enumerate(cells)}
    pick = np.zeros((2 * LANES, sx * sy * LANES), np.float32)
    for x in range(sx):
        for y in range(sy):
            for a in range(SPAN):
                for b in range(SPAN):
                    if admits(a - REACH, x % 2) and admits(b - REACH, y % 2):
                        for half in range(2):
                            col = (x * sy + y) * LANES + half * 64 + a * SPAN + b
                            pick[half * LANES + at[(x + a, y + b)], col] = 1.0
    return pick


def spread_constant(dims):
    sx, sy, sz = dims
    parents = (sx // 2) * (sy // 2) * (sz // 2)
    pick = np.zeros((sx * sy * sz, 8 * parents), np.float32)
    for z in range(sz):
        for x in range(sx):
            for y in range(sy):
                octant = 4 * (x % 2) + 2 * (y % 2) + z % 2
                parent = ((z // 2) * (sx // 2) + x // 2) * (sy // 2) + y // 2
                pick[(z * sx + x) * sy + y, octant * parents + parent] = 1.0
    return pick


def prepare_kernel(ops, tail, table, raw, made, sems, out_sems):
    width = ops.shape[1]
    tiles = raw.shape[0]
    whole = width // LANES

    def fetch(j):
        return pltpu.make_async_copy(ops.at[:, pl.ds(j * LANES, LANES)], raw.at[j], sems.at[j])

    def put(j):
        lanes = pl.ds(2 * j * LANES, 2 * LANES)
        return pltpu.make_async_copy(made.at[:, lanes], table.at[:, lanes], out_sems.at[j])

    for j in range(whole):
        fetch(j).start()
    if whole < tiles:
        raw[whole] = tail[...]
    ab = lax.broadcasted_iota(jnp.int32, (64, LANES), 0)
    closeby = (jnp.abs(ab // SPAN - REACH) <= 1) & (jnp.abs(ab % SPAN - REACH) <= 1)
    for j in range(tiles):
        if j < whole:
            fetch(j).wait()
        for c in range(SPAN):
            block = raw[j, pl.ds(c, SPAN * SPAN, stride=SPAN), :]
            block = jnp.concatenate(
                [block, jnp.zeros((64 - SPAN * SPAN, LANES), F32)], axis=0
            )
            if abs(c - REACH) <= 1:
                block = jnp.where(closeby, 0.0, block)
            if (j + 1) * LANES > width:
                lane = lax.broadcasted_iota(jnp.int32, (64, LANES), 1)
                block = jnp.where(lane < width - j * LANES, block, 0.0)
            hi, lo = split2(block)
            made[c * 64 : (c + 1) * 64, 2 * j * LANES : (2 * j + 1) * LANES] = hi
            made[c * 64 : (c + 1) * 64, (2 * j + 1) * LANES : (2 * j + 2) * LANES] = lo
        put(j).start()
    for j in range(tiles):
        put(j).wait()


def build_sources(sz, place, su, feats, lhs, columns):
    for i in range(su.shape[1] // 8):
        at = i * 8
        for half in range(2):
            rows = lax.broadcasted_iota(jnp.int32, (8, LANES), 0) + at
            lane = lax.broadcasted_iota(jnp.int32, (8, LANES), 1) + half * LANES
            lanes = slice(half * LANES, (half + 1) * LANES)
            arrays = [su[c, at : at + 8, lanes] for c in range(4)]
            for k, value in source_features_at(sz, place(rows), arrays, lane):
                feats[half, pl.ds(at * KROWS + k, 8, stride=KROWS), :] = value
    for i in range(columns):
        for half in range(2):
            block = feats[half, i * KROWS : i * KROWS + LANES, :]
            at = (2 * i + half) * LANES
            lhs[at : at + LANES, :] = block.T.astype(BF16)


def near_sums(sz, lhs, rhs, sources):
    total = [jnp.zeros((8, LANES), F32) for _ in range(2)]
    for src in sources:
        for z in range(sz):
            rows = src * sz * CAP + z * CAP
            d2 = dot(lhs[rows : rows + CAP, :], rhs)
            for half in range(2):
                if any(abs(z - t) <= 1 for t in (2 * half, 2 * half + 1)):
                    part = lax.rsqrt(d2[:, half * LANES : (half + 1) * LANES])
                    total[half] = total[half] + jnp.sum(
                        part.reshape(CAP // 8, 8, LANES), axis=0
                    )
    return jnp.concatenate([jnp.sum(part, axis=0, keepdims=True) for part in total], axis=1)


def near_own_kernel(dims, pos, mass, counts, after, near, rhs, su, feats, lhs, rfeats):
    sx, sy, sz = dims
    cols = sx * sy
    for x in range(sx):
        for c in range(3):
            su[c, x * sy : (x + 1) * sy, :] = pos[c, x] - 0.5
        for y in range(sy):
            row = x * sy + y
            su[3, row : row + 1, :] = column_weights(mass[x, y : y + 1, :], counts, x, y, sz)

    build_sources(sz, lambda rows: (rows // sy + 1, rows % sy + 1), su, feats, lhs, cols)
    for half in range(2):
        lanes = slice(half * LANES, (half + 1) * LANES)
        for at in range(0, cols, 8):
            rows = lax.broadcasted_iota(jnp.int32, (8, LANES), 0) + at
            lane = lax.broadcasted_iota(jnp.int32, (8, LANES), 1) + half * LANES
            arrays = [su[c, at : at + 8, lanes] for c in range(3)]
            for k, value in target_features_at(dims, arrays, rows, lane):
                rfeats[half, pl.ds(at * KROWS + k, 8, stride=KROWS), :] = value
    for i in range(cols):
        for half in range(2):
            rhs[i * LANES : (i + 1) * LANES, half * LANES : (half + 1) * LANES] = rfeats[
                half, i * KROWS : i * KROWS + LANES, :
            ].astype(BF16)
    for x in range(sx):
        for y in range(sy):
            i = x * sy + y
            sources = [
                a * sy + b
                for a in range(max(x - 1, 0), min(x + 2, sx))
                for b in range(max(y - 1, 0), min(y + 2, sy))
            ]
            near[i : i + 1, :] = near_sums(
                sz, lhs, rhs[i * LANES : (i + 1) * LANES, :], sources
            )


def fields_kernel(
    dims,
    pos, counts, poles, a1, b1, a2, b2, near_own, rhs_far, table_far, parents, l2l, c2e, pick,
    spread, points,
    potential, local_out,
    su, feats, lhs, rhs, near, sm, picked, lm, table, dens, sems,
):
    sx, sy, sz = dims
    hx, hy = sx + 2, sy + 2
    cols = sx * sy
    tiles = table.shape[1] // (2 * LANES)
    width = Q * Q

    get_rhs = pltpu.make_async_copy(rhs_far, rhs, sems.at[0])
    get_table = pltpu.make_async_copy(table_far, table, sems.at[1])
    get_rhs.start()
    get_table.start()

    odd_row, odd_col = is_odd("row"), is_odd("col")
    base1 = REACH * sy
    base2 = REACH * (sx + 2 * REACH)
    sides = []
    for odd, got_a, got_b, base, line in (
        (odd_row, a1, b1, base1, sy), (odd_col, a2, b2, base2, hx)
    ):
        for first, second in ((got_a, got_b), (got_b, got_a)):
            sides.append((odd, first, second, base, line))

    su[...] = jnp.zeros_like(su)
    sm[...] = jnp.zeros_like(sm)
    for x in range(sx):
        sm[x * sy : (x + 1) * sy, 0 : sz * Q] = poles[x]
    to, to_poles = 0, cols
    for odd, first, second, base, line in sides:
        value = jnp.where(odd, first[...], second[...])
        sm[to_poles : to_poles + base, :] = value[0:base, :]
        to_poles += base
        for c in range(4):
            su[c, to : to + line, :] = value[base + c * line : base + (c + 1) * line, :]
        to += line

    def place(rows):
        x, y = rows - 2 * sy - hx, jnp.full_like(rows, hy - 1)
        x = jnp.where(rows < 2 * sy + hx, rows - 2 * sy, x)
        y = jnp.where(rows < 2 * sy + hx, 0, y)
        x = jnp.where(rows < 2 * sy, hx - 1, x)
        y = jnp.where(rows < 2 * sy, rows - sy + 1, y)
        x = jnp.where(rows < sy, 0, x)
        y = jnp.where(rows < sy, rows + 1, y)
        return x, y

    halo = {(0, y + 1): y for y in range(sy)}
    halo.update({(hx - 1, y + 1): sy + y for y in range(sy)})
    halo.update({(x, 0): 2 * sy + x for x in range(hx)})
    halo.update({(x, hy - 1): 2 * sy + hx + x for x in range(hx)})
    build_sources(sz, place, su, feats, lhs, len(halo))
    get_rhs.wait()
    for x in range(sx):
        for y in range(sy):
            i = x * sy + y
            cells = [(x + dx, y + dy) for dx in range(3) for dy in range(3)]
            sources = [halo[cell] for cell in cells if cell in halo]
            value = near_own[i : i + 1, :]
            if sources:
                value = value + near_sums(sz, lhs, rhs[i * LANES : (i + 1) * LANES, :], sources)
            near[i : i + 1, :] = value

    for pair in range(sz // 2):
        his, los = [], []
        for zi in range(2):
            z = 2 * pair + zi
            rolled = pltpu.roll(sm[...], (2 * LANES - z * Q) % (2 * LANES), 1)[:, 0:LANES]
            hi, lo = split2(rolled.T[0:64, :])
            his.append(hi)
            los.append(lo)
        keep = lax.broadcasted_iota(jnp.int32, (64, 2 * LANES), 0) < Q
        his = jnp.where(keep, jnp.concatenate(his, axis=1).astype(F32), 0.0)
        los = jnp.where(keep, jnp.concatenate(los, axis=1).astype(F32), 0.0)
        picked[...] = jnp.concatenate([his, los], axis=0).astype(BF16)
        for xy in range(0, cols, 2):
            block = dot(picked[...], pick[:, xy * LANES : (xy + 2) * LANES])
            for i in range(2):
                lm[pair, pl.ds(xy + i, 2 * 64, stride=cols), :] = block[
                    :, i * LANES : (i + 1) * LANES
                ]

    get_table.wait()
    period = 16
    lane16 = lax.broadcasted_iota(jnp.int32, (cols, LANES), 1)
    check = [jnp.zeros((cols, LANES), F32) for _ in range(sz)]
    for t in range(period * Q // LANES):
        members = [s for s in range(period) if s * Q < (t + 1) * LANES and (s + 1) * Q > t * LANES]
        rows = len(members) * cols
        left = []
        for j in range(-(-Q // period)):
            if j * (period * Q // LANES) + t >= tiles:
                continue
            start = (j * period + members[0]) * cols
            left.append(
                jnp.concatenate(
                    [
                        jnp.concatenate(
                            [
                                lm[p, h * 64 * cols + start : h * 64 * cols + start + rows, :]
                                for p in range(sz // 2)
                            ],
                            axis=1,
                        )
                        for h in range(2)
                    ],
                    axis=0,
                ).astype(BF16)
            )
        for z in range(sz):
            total = None
            for j, block in enumerate(left):
                tile = j * (period * Q // LANES) + t
                first = (REACH - z) * 64
                part = dot(
                    block,
                    table[first : first + sz * 64, 2 * tile * LANES : (2 * tile + 2) * LANES],
                )
                total = part if total is None else total + part
            both = total[0:rows, 0:LANES] + (
                total[0:rows, LANES : 2 * LANES] + total[rows : 2 * rows, 0:LANES]
            )
            for i, s in enumerate(members):
                offset = s * Q - t * LANES
                part = both[i * cols : (i + 1) * cols, :]
                part = jnp.where((lane16 >= offset) & (lane16 < offset + Q), part, 0.0)
                check[z] = check[z] + pltpu.roll(part, (-offset) % LANES, 1)

    rows = []
    for pz in range(sz // 2):
        for x in range(sx // 2):
            rows.append(parents[x, :, pz * Q : (pz + 1) * Q])
    above = jnp.concatenate(rows, axis=0)
    below = jnp.concatenate([dot_exact(above, l2l[o]) for o in range(8)], axis=0)
    field = jnp.concatenate([part[:, 0:Q] for part in check], axis=0)
    field = field + dot_exact(spread[...], below)
    local = dot_exact(field, c2e[...])
    dens[...] = jnp.zeros_like(dens)
    dens[0 : sz * cols, 0:Q] = local
    flat = None
    for z in range(sz):
        part = jnp.concatenate(
            [dens[z * cols : (z + 1) * cols, :], jnp.zeros((cols, LANES), F32)], axis=1
        )
        part = pltpu.roll(part, z * Q, 1) if z else part
        flat = part if flat is None else flat + part
    for x in range(sx):
        local_out[x] = flat[x * sy : (x + 1) * sy, 0 : sz * Q]

    turned = dens[...].T[0:64, :]
    hi, lo = split2(turned[:, 0 : sz * cols])
    weights = jnp.concatenate([hi.astype(F32), lo.astype(F32)], axis=1).astype(BF16)
    row = lax.broadcasted_iota(jnp.int32, (2 * sz * cols, sz * CAP), 0) % (sz * cols)
    lane = lax.broadcasted_iota(jnp.int32, (2 * sz * cols, sz * CAP), 1)
    owner = row - (lane // CAP) * cols
    for x in range(sx):
        for y in range(sy):
            one_hot = jnp.where(owner == x * sy + y, 1.0, 0.0).astype(BF16)
            spread_out = dot(weights, one_hot)
            sums = []
            for half in range(2):
                lanes = slice(half * LANES, (half + 1) * LANES)
                d2 = jnp.zeros((64, LANES), F32)
                for c in range(3):
                    gap = pos[c, x, y : y + 1, lanes] - points[c]
                    d2 = d2 + gap * gap
                part = spread_out[:, lanes] * lax.rsqrt(d2)
                sums.append(jnp.sum(part, axis=0, keepdims=True))
            i = x * sy + y
            value = near[i : i + 1, :] + jnp.concatenate(sums, axis=1)
            potential[x, y : y + 1, :] = column_weights(value, counts, x, y, sz)


def source_features_at(sz, place, arrays, lane):
    ux, uy, uz, w = arrays
    shape = w.shape
    live = w > 0
    g = jnp.where(live, 1.0 / jnp.where(live, w * w, 1.0), 0.0)
    n = (ux * ux + uy * uy + uz * uz + SOFTEN * SOFTEN) * g
    n = jnp.where(live, n, DEAD)
    v = [split3(-2.0 * u * g) for u in (ux, uy, uz)]
    ones = [
        [place[0] % 3 == m for m in range(3)],
        [place[1] % 3 == m for m in range(3)],
        [lane // CAP == m for m in range(sz)],
    ]
    k = 0
    for c in range(3):
        for piece in (0, 0, 0, 1, 1, 2):
            yield k, v[c][piece]
            k += 1
    for c in range(3):
        for mask in ones[c]:
            for piece in range(3):
                yield k, jnp.where(mask, v[c][piece], 0.0)
                k += 1
    for piece in split3(n):
        yield k, piece
        k += 1
    gs = split3(g)
    for c in range(3):
        for mask in ones[c]:
            for piece in (0, 0, 0, 1, 1, 2):
                yield k, jnp.where(mask, gs[piece], 0.0)
                k += 1
    while k < LANES:
        yield k, jnp.zeros(shape, F32)
        k += 1


def target_features_at(dims, arrays, rows, lane):
    sx, sy, sz = dims
    shape = lane.shape
    place = (rows // sy, rows % sy, lane // CAP)
    t = [split3(u) for u in arrays]

    def shift(c, m):
        if c == 2:
            return (place[2] - m).astype(F32)
        return 1.0 - ((m - place[c] + 6) % 3).astype(F32)

    k = 0
    for c in range(3):
        for piece in (0, 1, 2, 0, 1, 0):
            yield k, t[c][piece]
            k += 1
    for c in range(3):
        for m in range(sz if c == 2 else 3):
            for _ in range(3):
                yield k, shift(c, m)
                k += 1
    for _ in range(3):
        yield k, jnp.ones(shape, F32)
        k += 1
    for c in range(3):
        for m in range(sz if c == 2 else 3):
            moved = arrays[c] + shift(c, m)
            parts = list(split3(moved * moved))
            if c == 2:
                reach = jnp.abs(place[2] - m) <= 1
                parts = [jnp.where(reach, p, BIG if i == 0 else 0.0) for i, p in enumerate(parts)]
            for piece in (0, 1, 2, 0, 1, 0):
                yield k, parts[piece]
                k += 1
    while k < LANES:
        yield k, jnp.zeros(shape, F32)
        k += 1


VMEM = pl.BlockSpec(memory_space=pltpu.VMEM)
SMEM = pl.BlockSpec(memory_space=pltpu.SMEM)
ANY = pl.BlockSpec(memory_space=pl.ANY)


def round_up(n, m):
    return -(-n // m) * m


def pack_row(dims, pos, mass, counts, poles):
    sx, sy, sz = dims
    rows = round_up((REACH + 4) * sy, 8)
    shape = jax.ShapeDtypeStruct((rows, sz * CAP), F32)
    return pl.pallas_call(
        functools.partial(pack_row_kernel, dims),
        out_shape=(shape, shape),
        in_specs=[VMEM, VMEM, SMEM, VMEM],
        out_specs=(VMEM, VMEM),
        name="pack_row",
    )(pos, mass, counts, poles)


def prepare(ops):
    rows, width = ops.shape
    tiles = -(-width // LANES)
    return pl.pallas_call(
        prepare_kernel,
        grid=(1,),
        out_shape=jax.ShapeDtypeStruct((SPAN * 64, 2 * tiles * LANES), BF16),
        in_specs=[ANY, pl.BlockSpec((rows, LANES), lambda _: (0, tiles - 1))],
        out_specs=ANY,
        scratch_shapes=[
            pltpu.VMEM((tiles, rows, LANES), F32),
            pltpu.VMEM((SPAN * 64, 2 * tiles * LANES), BF16),
            pltpu.SemaphoreType.DMA((tiles,)),
            pltpu.SemaphoreType.DMA((tiles,)),
        ],
        compiler_params=pltpu.CompilerParams(vmem_limit_bytes=20 << 20),
        cost_estimate=pl.CostEstimate(flops=1 << 24, bytes_accessed=10 << 20, transcendentals=0),
        name="prepare",
    )(ops, ops)


def pack_col(dims, pos, mass, counts, poles, got_a, got_b):
    sx, sy, sz = dims
    rows = round_up(REACH * (sx + 2 * REACH) + 4 * (sx + 2), 8)
    shape = jax.ShapeDtypeStruct((rows, sz * CAP), F32)
    return pl.pallas_call(
        functools.partial(pack_col_kernel, dims),
        out_shape=(shape, shape),
        in_specs=[VMEM, VMEM, SMEM, VMEM, VMEM, VMEM],
        out_specs=(VMEM, VMEM),
        scratch_shapes=[pltpu.VMEM(got_a.shape, F32), pltpu.VMEM(got_a.shape, F32)],
        name="pack_col",
    )(pos, mass, counts, poles, got_a, got_b)


def near_own(dims, pos, mass, counts, after):
    sx, sy, sz = dims
    cols = sx * sy
    return pl.pallas_call(
        functools.partial(near_own_kernel, dims),
        out_shape=(
            jax.ShapeDtypeStruct((cols, sz * CAP), F32),
            jax.ShapeDtypeStruct((cols * LANES, sz * CAP), BF16),
        ),
        in_specs=[VMEM, VMEM, SMEM, ANY],
        out_specs=(VMEM, VMEM),
        scratch_shapes=[
            pltpu.VMEM((4, cols, sz * CAP), F32),
            pltpu.VMEM((2, cols * KROWS, LANES), F32),
            pltpu.VMEM((cols * sz * CAP, LANES), BF16),
            pltpu.VMEM((2, cols * KROWS, LANES), F32),
        ],
        compiler_params=pltpu.CompilerParams(vmem_limit_bytes=20 << 20),
        cost_estimate=pl.CostEstimate(flops=1 << 32, bytes_accessed=1 << 20, transcendentals=1 << 22),
        name="near_own",
    )(pos, mass, counts, after)


def fields(dims, pos, counts, poles, a1, b1, a2, b2, near, rhs, table, parents, l2l, c2e):
    sx, sy, sz = dims
    cols = sx * sy
    ring = 2 * sy + 2 * (sx + 2)
    pick = jnp.asarray(gather_constant(dims), BF16)
    spread = jnp.asarray(spread_constant(dims))
    points = np.full((3, 64, LANES), 10.0, np.float32)
    points[:, :Q, :] = surface_points().T[:, :, None]
    return pl.pallas_call(
        functools.partial(fields_kernel, dims),
        out_shape=(
            jax.ShapeDtypeStruct((sx, sy, sz * CAP), F32),
            jax.ShapeDtypeStruct((sx, sy, sz * Q), F32),
        ),
        in_specs=[VMEM, SMEM] + [VMEM] * 6 + [ANY, ANY] + [VMEM] * 6,
        out_specs=(VMEM, VMEM),
        scratch_shapes=[
            pltpu.VMEM((4, round_up(ring, 8), sz * CAP), F32),
            pltpu.VMEM((2, round_up(ring, 8) * KROWS, LANES), F32),
            pltpu.VMEM((ring * sz * CAP, LANES), BF16),
            pltpu.VMEM(rhs.shape, BF16),
            pltpu.VMEM((cols, sz * CAP), F32),
            pltpu.VMEM((LANES, 2 * LANES), F32),
            pltpu.VMEM((LANES, 2 * LANES), BF16),
            pltpu.VMEM((sz // 2, 2 * 64 * cols, LANES), F32),
            pltpu.VMEM(table.shape, BF16),
            pltpu.VMEM((LANES, LANES), F32),
            pltpu.SemaphoreType.DMA((2,)),
        ],
        compiler_params=pltpu.CompilerParams(vmem_limit_bytes=30 << 20),
        name="fields",
    )(pos, counts, poles, a1, b1, a2, b2, near, rhs, table, parents, l2l, c2e, pick, spread,
      jnp.asarray(points))


def exchange(send_a, send_b, axis):
    count = lax.axis_size(axis)
    got = []
    for value, first in ((send_a, 0), (send_b, 1)):
        pairs = [(i, i + 1) for i in range(first, count - 1, 2)]
        got.append(lax.ppermute(value, axis, pairs + [(b, a) for a, b in pairs]))
    return got


def body(positions, masses, counts, multipoles, parent_local, m2l_ops, l2l_ops, check_to_equiv):
    sx, sy, slots = masses.shape
    dims = (sx, sy, slots // CAP)
    table = prepare(m2l_ops)
    a1, b1 = exchange(*pack_row(dims, positions, masses, counts, multipoles), "row")
    send = pack_col(dims, positions, masses, counts, multipoles, a1, b1)
    a2, b2 = exchange(*send, "col")
    near, rhs = near_own(dims, positions, masses, counts, send[0])
    return fields(
        dims, positions, counts, multipoles, a1, b1, a2, b2, near, rhs, table,
        parent_local, l2l_ops, check_to_equiv,
    )


def solution(mesh):
    return jax.shard_map(
        body,
        mesh=mesh,
        in_specs=(
            P(None, "row", "col", None),
            P("row", "col", None),
            P("row", "col", None),
            P("row", "col", None),
            P("row", "col", None),
            P(),
            P(),
            P(),
        ),
        out_specs=(P("row", "col", None), P("row", "col", None)),
        check_vma=False,
    )
```

```python
import functools

import jax
import jax.numpy as jnp
import numpy as np
from jax import lax
from jax.experimental import pallas as pl
from jax.experimental.pallas import tpu as pltpu
from jax.sharding import PartitionSpec as P

CAP = 64
P_SIZE = 4
Q = 56
SOFTEN = 0.05
LANES = 128
BIG = 2.0**100
DEAD = 2.0**120
F32, BF16 = jnp.float32, jnp.bfloat16
REACH = 3
SPAN = 2 * REACH + 1
KROWS = 136


def surface_points():
    steps = np.stack(
        np.meshgrid(np.arange(P_SIZE), np.arange(P_SIZE), np.arange(P_SIZE), indexing="ij"), -1
    ).reshape(-1, 3)
    on_face = np.any((steps == 0) | (steps == P_SIZE - 1), axis=1)
    return (0.5 + 1.4 * (steps[on_face] / (P_SIZE - 1) - 0.5)).astype(np.float32)


def admits(shift, parity):
    return -2 - parity <= shift <= 3 - parity


def split2(x):
    hi = x.astype(BF16)
    return hi, (x - hi.astype(F32)).astype(BF16)


def split3(x):
    hi = x.astype(BF16).astype(F32)
    rest = x - hi
    mid = rest.astype(BF16).astype(F32)
    return hi, mid, rest - mid


def dot(a, b):
    return jnp.dot(a, b, preferred_element_type=F32)


def dot_exact(a, b):
    return jnp.dot(a, b, preferred_element_type=F32, precision=lax.Precision.HIGHEST)


def column_weights(masses, counts, x, y, sz):
    lane = lax.broadcasted_iota(jnp.int32, (1, sz * CAP), 1)
    limit = jnp.zeros((1, sz * CAP), jnp.int32)
    for z in range(sz):
        limit = jnp.where(lane // CAP == z, counts[x, y, z], limit)
    return jnp.where(lane % CAP < limit, masses, 0.0)


def is_odd(axis):
    return lax.axis_index(axis) % 2 == 1


def pack_row_kernel(
    dims, pos_far, mass_far, counts_far, poles_far, send_a, send_b, own,
    pos, mass, counts, poles, sems,
):
    sx, sy, sz = dims
    cols = sx * sy
    copies = [
        pltpu.make_async_copy(far, near, sems.at[i])
        for i, (far, near) in enumerate(
            ((counts_far, counts), (pos_far, pos), (mass_far, mass), (poles_far, poles))
        )
    ]
    for copy in copies:
        copy.start()
    own[...] = jnp.zeros_like(own)
    send_a[...] = jnp.zeros_like(send_a)
    send_b[...] = jnp.zeros_like(send_b)
    for copy in copies:
        copy.wait()
    for x in range(sx):
        at = x * sy
        for c in range(3):
            own[c * cols + at : c * cols + at + sy, :] = pos[c, x] - 0.5
        for y in range(sy):
            row = 3 * cols + at + y
            own[row : row + 1, :] = column_weights(mass[x, y : y + 1, :], counts, x, y, sz)
        own[4 * cols + at : 4 * cols + at + sy, 0 : sz * Q] = poles[x]
    odd = is_odd("row")
    pieces = [(4 * cols, 4 * cols + (sx - REACH) * sy, REACH * sy, 0)]
    base = REACH * sy
    for c in range(4):
        pieces.append((c * cols, c * cols + (sx - 1) * sy, sy, base + c * sy))
    for low, high, rows, at in pieces:
        low_edge, high_edge = own[low : low + rows, :], own[high : high + rows, :]
        send_a[at : at + rows, :] = jnp.where(odd, low_edge, high_edge)
        send_b[at : at + rows, :] = jnp.where(odd, high_edge, low_edge)


def pack_col_kernel(dims, own, got_a, got_b, token, send_a, send_b, next_token, low, high):
    sx, sy, sz = dims
    cols = sx * sy
    odd_row, odd_col = is_odd("row"), is_odd("col")
    next_token[...] = token[...]
    low[...] = jnp.where(odd_row, got_a[...], got_b[...])
    high[...] = jnp.where(odd_row, got_b[...], got_a[...])
    base_in = REACH * sy
    base = REACH * (sx + 2 * REACH)
    px = sx + 2
    send_a[...] = jnp.zeros_like(send_a)
    send_b[...] = jnp.zeros_like(send_b)

    def store(at, rows, ref, start):
        low_edge = ref[start : start + rows, :]
        high_edge = ref[start + sy - rows : start + sy, :]
        send_a[at : at + rows, :] = jnp.where(odd_col, low_edge, high_edge)
        send_b[at : at + rows, :] = jnp.where(odd_col, high_edge, low_edge)

    for x in range(sx + 2 * REACH):
        if REACH <= x < REACH + sx:
            store(x * REACH, REACH, own, 4 * cols + (x - REACH) * sy)
        elif x < REACH:
            store(x * REACH, REACH, low, x * sy)
        else:
            store(x * REACH, REACH, high, (x - REACH - sx) * sy)
    for c in range(4):
        for x in range(px):
            at = base + c * px + x
            if x == 0:
                store(at, 1, low, base_in + c * sy)
            elif x == px - 1:
                store(at, 1, high, base_in + c * sy)
            else:
                store(at, 1, own, c * cols + (x - 1) * sy)


def gather_constant(dims):
    sx, sy, _ = dims
    cells = [(x + REACH, y + REACH) for x in range(sx) for y in range(sy)]
    cells += [(x, y + REACH) for x in range(REACH) for y in range(sy)]
    cells += [(x + REACH + sx, y + REACH) for x in range(REACH) for y in range(sy)]
    cells += [(x, y) for x in range(sx + 2 * REACH) for y in range(REACH)]
    cells += [(x, y + REACH + sy) for x in range(sx + 2 * REACH) for y in range(REACH)]
    at = {cell: i for i, cell in enumerate(cells)}
    pick = np.zeros((2 * LANES, sx * sy * LANES), np.float32)
    for x in range(sx):
        for y in range(sy):
            for a in range(SPAN):
                for b in range(SPAN):
                    if admits(a - REACH, x % 2) and admits(b - REACH, y % 2):
                        for half in range(2):
                            col = (x * sy + y) * LANES + half * 64 + a * SPAN + b
                            pick[half * LANES + at[(x + a, y + b)], col] = 1.0
    return pick


def spread_constant(dims):
    sx, sy, sz = dims
    parents = (sx // 2) * (sy // 2) * (sz // 2)
    pick = np.zeros((sx * sy * sz, 8 * parents), np.float32)
    for z in range(sz):
        for x in range(sx):
            for y in range(sy):
                octant = 4 * (x % 2) + 2 * (y % 2) + z % 2
                parent = ((z // 2) * (sx // 2) + x // 2) * (sy // 2) + y // 2
                pick[(z * sx + x) * sy + y, octant * parents + parent] = 1.0
    return pick


def prepare_kernel(ops, tail, token, table, raw, sems):
    width = ops.shape[1]
    tiles = raw.shape[0]
    whole = tiles - 1

    def fetch(j):
        return pltpu.make_async_copy(ops.at[:, pl.ds(j * LANES, LANES)], raw.at[j], sems.at[j])

    for j in range(whole):
        fetch(j).start()
    raw[tiles - 1] = tail[...]
    ab = lax.broadcasted_iota(jnp.int32, (64, LANES), 0)
    closeby = (jnp.abs(ab // SPAN - REACH) <= 1) & (jnp.abs(ab % SPAN - REACH) <= 1)
    for j in range(tiles):
        if j < whole:
            fetch(j).wait()
        for c in range(SPAN):
            block = raw[j, pl.ds(c, SPAN * SPAN, stride=SPAN), :]
            block = jnp.concatenate(
                [block, jnp.zeros((64 - SPAN * SPAN, LANES), F32)], axis=0
            )
            if abs(c - REACH) <= 1:
                block = jnp.where(closeby, 0.0, block)
            if (j + 1) * LANES > width:
                lane = lax.broadcasted_iota(jnp.int32, (64, LANES), 1)
                block = jnp.where(lane < width - j * LANES, block, 0.0)
            hi, lo = split2(block)
            table[c * 64 : (c + 1) * 64, 2 * j * LANES : (2 * j + 1) * LANES] = hi
            table[c * 64 : (c + 1) * 64, (2 * j + 1) * LANES : (2 * j + 2) * LANES] = lo


def fill_features(sz, place, su, feats, at):
    for half in range(2):
        rows = lax.broadcasted_iota(jnp.int32, (8, LANES), 0) + at
        lane = lax.broadcasted_iota(jnp.int32, (8, LANES), 1) + half * LANES
        lanes = slice(half * LANES, (half + 1) * LANES)
        arrays = [su[c][at : at + 8, lanes] for c in range(4)]
        for k, value in source_features_at(sz, place(rows), arrays, lane):
            feats[half, pl.ds(at * KROWS + k, 8, stride=KROWS), :] = value


def turn_features(feats, lhs, i):
    for half in range(2):
        block = feats[half, i * KROWS : i * KROWS + LANES, :]
        at = (2 * i + half) * LANES
        lhs[at : at + LANES, :] = block.T.astype(BF16)


def near_sums(sz, lhs, rhs, total, src, targets):
    halves = [[h for h in range(2) if any(abs(z - t) <= 1 for t in (2 * h, 2 * h + 1))] for z in range(sz)]

    def add(target, half, d2):
        part = jnp.sum(lax.rsqrt(d2).reshape(d2.shape[0] // 8, 8, LANES), axis=0)
        at, lanes = slice(target * 8, (target + 1) * 8), slice(half * LANES, (half + 1) * LANES)
        total[at, lanes] = total[at, lanes] + part

    def operand(target, half):
        return rhs[target * LANES : (target + 1) * LANES, half * LANES : (half + 1) * LANES]

    base = src * sz * CAP
    middle = [z for z in range(sz) if len(halves[z]) == 2]
    rows = slice(base + middle[0] * CAP, base + (middle[-1] + 1) * CAP)
    for target in targets:
        d2 = dot(lhs[rows, :], rhs[target * LANES : (target + 1) * LANES, :])
        for half in range(2):
            add(target, half, d2[:, half * LANES : (half + 1) * LANES])
    for z in range(sz):
        if len(halves[z]) == 2:
            continue
        half = halves[z][0]
        rows = slice(base + z * CAP, base + (z + 1) * CAP)
        for i in range(0, len(targets), 2):
            both = targets[i : i + 2]
            wide = jnp.concatenate([operand(t, half) for t in both], axis=1)
            d2 = dot(lhs[rows, :], wide)
            for n, target in enumerate(both):
                add(target, half, d2[:, n * LANES : (n + 1) * LANES])


def near_own_kernel(dims, own, near, rhs, token, feats, lhs, rfeats):
    sx, sy, sz = dims
    cols = sx * sy
    token[...] = own[0:8, 0:LANES]
    su = [own.at[c * cols : (c + 1) * cols] for c in range(4)]

    for at in range(0, cols, 8):
        fill_features(sz, lambda rows: (rows // sy + 1, rows % sy + 1), su, feats, at)
    for i in range(cols):
        turn_features(feats, lhs, i)
    for half in range(2):
        lanes = slice(half * LANES, (half + 1) * LANES)
        for at in range(0, cols, 8):
            rows = lax.broadcasted_iota(jnp.int32, (8, LANES), 0) + at
            lane = lax.broadcasted_iota(jnp.int32, (8, LANES), 1) + half * LANES
            arrays = [su[c][at : at + 8, lanes] for c in range(3)]
            for k, value in target_features_at(dims, arrays, rows, lane):
                rfeats[half, pl.ds(at * KROWS + k, 8, stride=KROWS), :] = value
    for i in range(cols):
        for half in range(2):
            rhs[i * LANES : (i + 1) * LANES, half * LANES : (half + 1) * LANES] = rfeats[
                half, i * KROWS : i * KROWS + LANES, :
            ].astype(BF16)
    near[...] = jnp.zeros_like(near)
    for x in range(sx):
        for y in range(sy):
            targets = [
                a * sy + b
                for a in range(max(x - 1, 0), min(x + 2, sx))
                for b in range(max(y - 1, 0), min(y + 2, sy))
            ]
            near_sums(sz, lhs, rhs, near, x * sy + y, targets)


def fields_kernel(
    dims,
    own, a1, b1, a2, b2, near_own, rhs, table, parents, l2l, c2e, pick,
    spread, points,
    potential, local_out,
    halo_slots, feats, lhs, near, sm, picked, lm, dens,
):
    sx, sy, sz = dims
    hx, hy = sx + 2, sy + 2
    cols = sx * sy
    tiles = table.shape[1] // (2 * LANES)
    odd_row, odd_col = is_odd("row"), is_odd("col")
    base1 = REACH * sy
    base2 = REACH * (sx + 2 * REACH)
    sides = []
    for odd, got_a, got_b, base, line in (
        (odd_row, a1, b1, base1, sy), (odd_col, a2, b2, base2, hx)
    ):
        for first, second in ((got_a, got_b), (got_b, got_a)):
            sides.append((odd, first, second, base, line))

    su = [halo_slots.at[c] for c in range(4)]
    halo_slots[...] = jnp.zeros_like(halo_slots)
    sm[...] = jnp.zeros_like(sm)
    sm[0:cols, :] = own[4 * cols : 5 * cols, :]
    to, to_poles = 0, cols
    for odd, first, second, base, line in sides:
        value = jnp.where(odd, first[...], second[...])
        sm[to_poles : to_poles + base, :] = value[0:base, :]
        to_poles += base
        for c in range(4):
            su[c][to : to + line, :] = value[base + c * line : base + (c + 1) * line, :]
        to += line

    def place(rows):
        x, y = rows - 2 * sy - hx, jnp.full_like(rows, hy - 1)
        x = jnp.where(rows < 2 * sy + hx, rows - 2 * sy, x)
        y = jnp.where(rows < 2 * sy + hx, 0, y)
        x = jnp.where(rows < 2 * sy, hx - 1, x)
        y = jnp.where(rows < 2 * sy, rows - sy + 1, y)
        x = jnp.where(rows < sy, 0, x)
        y = jnp.where(rows < sy, rows + 1, y)
        return x, y

    halo = {(0, y + 1): y for y in range(sy)}
    halo.update({(hx - 1, y + 1): sy + y for y in range(sy)})
    halo.update({(x, 0): 2 * sy + x for x in range(hx)})
    halo.update({(x, hy - 1): 2 * sy + hx + x for x in range(hx)})
    for pair in range(sz // 2):
        his, los = [], []
        for zi in range(2):
            z = 2 * pair + zi
            rolled = pltpu.roll(sm[...], (2 * LANES - z * Q) % (2 * LANES), 1)[:, 0:LANES]
            hi, lo = split2(rolled.T[0:64, :])
            his.append(hi)
            los.append(lo)
        keep = lax.broadcasted_iota(jnp.int32, (64, 2 * LANES), 0) < Q
        his = jnp.where(keep, jnp.concatenate(his, axis=1).astype(F32), 0.0)
        los = jnp.where(keep, jnp.concatenate(los, axis=1).astype(F32), 0.0)
        picked[...] = jnp.concatenate([his, los], axis=0).astype(BF16)
        for xy in range(0, cols, 2):
            block = dot(picked[...], pick[:, xy * LANES : (xy + 2) * LANES])
            for i in range(2):
                lm[pair, pl.ds(xy + i, 2 * 64, stride=cols), :] = block[
                    :, i * LANES : (i + 1) * LANES
                ]

    period = 16
    lane16 = lax.broadcasted_iota(jnp.int32, (cols, LANES), 1)
    check = [jnp.zeros((cols, LANES), F32) for _ in range(sz)]
    groups = list(range(0, halo_slots.shape[1], 8))
    turns = list(range(len(halo)))
    spans = period * Q // LANES
    for t in range(spans):
        if groups:
            fill_features(sz, place, su, feats, groups.pop(0))
        else:
            for _ in range(-(-len(turns) // (spans - t))):
                turn_features(feats, lhs, turns.pop(0))
        members = [s for s in range(period) if s * Q < (t + 1) * LANES and (s + 1) * Q > t * LANES]
        rows = len(members) * cols
        left = []
        for j in range(-(-Q // period)):
            if j * (period * Q // LANES) + t >= tiles:
                continue
            start = (j * period + members[0]) * cols
            left.append(
                jnp.concatenate(
                    [
                        jnp.concatenate(
                            [
                                lm[p, h * 64 * cols + start : h * 64 * cols + start + rows, :]
                                for p in range(sz // 2)
                            ],
                            axis=1,
                        )
                        for h in range(2)
                    ],
                    axis=0,
                ).astype(BF16)
            )
        for z in range(sz):
            total = None
            for j, block in enumerate(left):
                tile = j * (period * Q // LANES) + t
                first = (REACH - z) * 64
                part = dot(
                    block,
                    table[first : first + sz * 64, 2 * tile * LANES : (2 * tile + 2) * LANES],
                )
                total = part if total is None else total + part
            both = total[0:rows, 0:LANES] + (
                total[0:rows, LANES : 2 * LANES] + total[rows : 2 * rows, 0:LANES]
            )
            for i, s in enumerate(members):
                offset = s * Q - t * LANES
                part = both[i * cols : (i + 1) * cols, :]
                part = jnp.where((lane16 >= offset) & (lane16 < offset + Q), part, 0.0)
                check[z] = check[z] + pltpu.roll(part, (-offset) % LANES, 1)

    assert not groups and not turns

    rows = []
    for pz in range(sz // 2):
        for x in range(sx // 2):
            rows.append(parents[x, :, pz * Q : (pz + 1) * Q])
    above = jnp.concatenate(rows, axis=0)
    below = jnp.concatenate([dot_exact(above, l2l[o]) for o in range(8)], axis=0)
    field = jnp.concatenate([part[:, 0:Q] for part in check], axis=0)
    field = field + dot_exact(spread[...], below)
    local = dot_exact(field, c2e[...])
    dens[...] = jnp.zeros_like(dens)
    dens[0 : sz * cols, 0:Q] = local
    flat = None
    for z in range(sz):
        part = jnp.concatenate(
            [dens[z * cols : (z + 1) * cols, :], jnp.zeros((cols, LANES), F32)], axis=1
        )
        part = pltpu.roll(part, z * Q, 1) if z else part
        flat = part if flat is None else flat + part
    for x in range(sx):
        local_out[x] = flat[x * sy : (x + 1) * sy, 0 : sz * Q]

    turned = dens[...].T[0:64, :]
    hi, lo = split2(turned[:, 0 : sz * cols])
    weights = jnp.concatenate([hi.astype(F32), lo.astype(F32)], axis=1).astype(BF16)
    row = lax.broadcasted_iota(jnp.int32, (2 * sz * cols, sz * CAP), 0) % (sz * cols)
    lane = lax.broadcasted_iota(jnp.int32, (2 * sz * cols, sz * CAP), 1)
    owner = row - (lane // CAP) * cols

    def far(i):
        one_hot = jnp.where(owner == i, 1.0, 0.0).astype(BF16)
        spread_out = dot(weights, one_hot)
        for half in range(2):
            lanes = slice(half * LANES, (half + 1) * LANES)
            d2 = jnp.zeros((64, LANES), F32)
            for c in range(3):
                gap = own[c * cols + i : c * cols + i + 1, lanes] - points[c]
                d2 = d2 + gap * gap
            part = spread_out[:, lanes] * lax.rsqrt(d2)
            at = slice(i * 8, (i + 1) * 8)
            near[at, lanes] = near[at, lanes] + jnp.sum(part.reshape(8, 8, LANES), axis=0)

    near[...] = near_own[...]
    left = list(range(cols))
    for cell, src in halo.items():
        targets = [
            x * sy + y
            for x in range(sx)
            for y in range(sy)
            if 0 <= cell[0] - x <= 2 and 0 <= cell[1] - y <= 2
        ]
        if left:
            far(left.pop(0))
        near_sums(sz, lhs, rhs, near, src, targets)
    assert not left
    for i in range(cols):
        x, y = i // sy, i % sy
        value = jnp.sum(near[i * 8 : (i + 1) * 8, :], axis=0, keepdims=True)
        live = own[3 * cols + i : 3 * cols + i + 1, :] > 0
        potential[x, y : y + 1, :] = jnp.where(live, value, 0.0)


def source_features_at(sz, place, arrays, lane):
    ux, uy, uz, w = arrays
    shape = w.shape
    live = w > 0
    g = jnp.where(live, 1.0 / jnp.where(live, w * w, 1.0), 0.0)
    n = (ux * ux + uy * uy + uz * uz + SOFTEN * SOFTEN) * g
    n = jnp.where(live, n, DEAD)
    v = [split3(-2.0 * u * g) for u in (ux, uy, uz)]
    ones = [
        [place[0] % 3 == m for m in range(3)],
        [place[1] % 3 == m for m in range(3)],
        [lane // CAP == m for m in range(sz)],
    ]
    k = 0
    for c in range(3):
        for piece in (0, 0, 0, 1, 1, 2):
            yield k, v[c][piece]
            k += 1
    for c in range(3):
        for mask in ones[c]:
            for piece in range(3):
                yield k, jnp.where(mask, v[c][piece], 0.0)
                k += 1
    for piece in split3(n):
        yield k, piece
        k += 1
    gs = split3(g)
    for c in range(3):
        for mask in ones[c]:
            for piece in (0, 0, 0, 1, 1, 2):
                yield k, jnp.where(mask, gs[piece], 0.0)
                k += 1
    while k < LANES:
        yield k, jnp.zeros(shape, F32)
        k += 1


def target_features_at(dims, arrays, rows, lane):
    sx, sy, sz = dims
    shape = lane.shape
    place = (rows // sy, rows % sy, lane // CAP)
    t = [split3(u) for u in arrays]

    def shift(c, m):
        if c == 2:
            return (place[2] - m).astype(F32)
        return 1.0 - ((m - place[c] + 6) % 3).astype(F32)

    k = 0
    for c in range(3):
        for piece in (0, 1, 2, 0, 1, 0):
            yield k, t[c][piece]
            k += 1
    for c in range(3):
        for m in range(sz if c == 2 else 3):
            for _ in range(3):
                yield k, shift(c, m)
                k += 1
    for _ in range(3):
        yield k, jnp.ones(shape, F32)
        k += 1
    for c in range(3):
        for m in range(sz if c == 2 else 3):
            moved = arrays[c] + shift(c, m)
            parts = list(split3(moved * moved))
            if c == 2:
                reach = jnp.abs(place[2] - m) <= 1
                parts = [jnp.where(reach, p, BIG if i == 0 else 0.0) for i, p in enumerate(parts)]
            for piece in (0, 1, 2, 0, 1, 0):
                yield k, parts[piece]
                k += 1
    while k < LANES:
        yield k, jnp.zeros(shape, F32)
        k += 1


VMEM = pl.BlockSpec(memory_space=pltpu.VMEM)
SMEM = pl.BlockSpec(memory_space=pltpu.SMEM)
HBM = pl.BlockSpec(memory_space=pltpu.HBM)


def round_up(n, m):
    return -(-n // m) * m


def pack_row(dims, pos, mass, counts, poles):
    sx, sy, sz = dims
    shape = jax.ShapeDtypeStruct((round_up((REACH + 4) * sy, 8), sz * CAP), F32)
    return pl.pallas_call(
        functools.partial(pack_row_kernel, dims),
        out_shape=(shape, shape, jax.ShapeDtypeStruct((5 * sx * sy, sz * CAP), F32)),
        in_specs=[HBM] * 4,
        out_specs=(VMEM,) * 3,
        scratch_shapes=[
            pltpu.VMEM(pos.shape, F32),
            pltpu.VMEM(mass.shape, F32),
            pltpu.SMEM(counts.shape, jnp.int32),
            pltpu.VMEM(poles.shape, F32),
            pltpu.SemaphoreType.DMA((4,)),
        ],
        name="pack_row",
    )(pos, mass, counts, poles)


def prepare(ops, token):
    rows, width = ops.shape
    tiles = -(-width // LANES)
    tail = jnp.pad(ops[:, (tiles - 1) * LANES :], ((0, 0), (0, tiles * LANES - width)))
    return pl.pallas_call(
        prepare_kernel,
        out_shape=jax.ShapeDtypeStruct((SPAN * 64, 2 * tiles * LANES), BF16),
        in_specs=[HBM, VMEM, VMEM],
        out_specs=VMEM,
        scratch_shapes=[
            pltpu.VMEM((tiles, rows, LANES), F32),
            pltpu.SemaphoreType.DMA((tiles,)),
        ],
        compiler_params=pltpu.CompilerParams(vmem_limit_bytes=12 << 20),
        cost_estimate=pl.CostEstimate(flops=1 << 24, bytes_accessed=10 << 20, transcendentals=0),
        name="prepare",
    )(ops, tail, token)


def pack_col(dims, own, got_a, got_b, token):
    sx, sy, sz = dims
    rows = round_up(REACH * (sx + 2 * REACH) + 4 * (sx + 2), 8)
    shape = jax.ShapeDtypeStruct((rows, sz * CAP), F32)
    return pl.pallas_call(
        functools.partial(pack_col_kernel, dims),
        out_shape=(shape, shape, jax.ShapeDtypeStruct(token.shape, F32)),
        in_specs=[VMEM] * 4,
        out_specs=(VMEM,) * 3,
        scratch_shapes=[pltpu.VMEM(got_a.shape, F32), pltpu.VMEM(got_a.shape, F32)],
        compiler_params=pltpu.CompilerParams(vmem_limit_bytes=2 << 20),
        name="pack_col",
    )(own, got_a, got_b, token)


def near_own(dims, own):
    sx, sy, sz = dims
    cols = sx * sy
    return pl.pallas_call(
        functools.partial(near_own_kernel, dims),
        out_shape=(
            jax.ShapeDtypeStruct((cols * 8, sz * CAP), F32),
            jax.ShapeDtypeStruct((cols * LANES, sz * CAP), BF16),
            jax.ShapeDtypeStruct((8, LANES), F32),
        ),
        in_specs=[VMEM],
        out_specs=(VMEM,) * 3,
        scratch_shapes=[
            pltpu.VMEM((2, cols * KROWS, LANES), F32),
            pltpu.VMEM((cols * sz * CAP, LANES), BF16),
            pltpu.VMEM((2, cols * KROWS, LANES), F32),
        ],
        compiler_params=pltpu.CompilerParams(vmem_limit_bytes=10 << 20),
        cost_estimate=pl.CostEstimate(flops=1 << 32, bytes_accessed=1 << 20, transcendentals=1 << 22),
        name="near_own",
    )(own)


def fields(dims, own, a1, b1, a2, b2, near, rhs, table, parents, l2l, c2e):
    sx, sy, sz = dims
    cols = sx * sy
    ring = 2 * sy + 2 * (sx + 2)
    pick = jnp.asarray(gather_constant(dims), BF16)
    spread = jnp.asarray(spread_constant(dims))
    points = np.full((3, 64, LANES), 10.0, np.float32)
    points[:, :Q, :] = surface_points().T[:, :, None] - 0.5
    return pl.pallas_call(
        functools.partial(fields_kernel, dims),
        out_shape=(
            jax.ShapeDtypeStruct((sx, sy, sz * CAP), F32),
            jax.ShapeDtypeStruct((sx, sy, sz * Q), F32),
        ),
        in_specs=[VMEM] * 14,
        out_specs=(VMEM, VMEM),
        scratch_shapes=[
            pltpu.VMEM((4, round_up(ring, 8), sz * CAP), F32),
            pltpu.VMEM((2, round_up(ring, 8) * KROWS, LANES), F32),
            pltpu.VMEM((ring * sz * CAP, LANES), BF16),
            pltpu.VMEM((cols * 8, sz * CAP), F32),
            pltpu.VMEM((LANES, 2 * LANES), F32),
            pltpu.VMEM((LANES, 2 * LANES), BF16),
            pltpu.VMEM((sz // 2, 2 * 64 * cols, LANES), F32),
            pltpu.VMEM((LANES, LANES), F32),
        ],
        compiler_params=pltpu.CompilerParams(vmem_limit_bytes=16 << 20),
        name="fields",
    )(own, a1, b1, a2, b2, near, rhs, table, parents, l2l, c2e, pick, spread,
      jnp.asarray(points))


def exchange(send_a, send_b, axis):
    count = lax.axis_size(axis)
    got = []
    for value, first in ((send_a, 0), (send_b, 1)):
        pairs = [(i, i + 1) for i in range(first, count - 1, 2)]
        got.append(lax.ppermute(value, axis, pairs + [(b, a) for a, b in pairs]))
    return got


def body(positions, masses, counts, multipoles, parent_local, m2l_ops, l2l_ops, check_to_equiv):
    sx, sy, slots = masses.shape
    dims = (sx, sy, slots // CAP)
    send_a, send_b, own = pack_row(dims, positions, masses, counts, multipoles)
    a1, b1 = exchange(send_a, send_b, "row")
    near, rhs, token = near_own(dims, own)
    send_a, send_b, token = pack_col(dims, own, a1, b1, token)
    a2, b2 = exchange(send_a, send_b, "col")
    table = prepare(m2l_ops, token)
    return fields(
        dims, own, a1, b1, a2, b2, near, rhs, table, parent_local, l2l_ops, check_to_equiv
    )


def solution(mesh):
    return jax.shard_map(
        body,
        mesh=mesh,
        in_specs=(
            P(None, "row", "col", None),
            P("row", "col", None),
            P("row", "col", None),
            P("row", "col", None),
            P("row", "col", None),
            P(),
            P(),
            P(),
        ),
        out_specs=(P("row", "col", None), P("row", "col", None)),
        check_vma=False,
    )
```

```python
import functools

import jax
import jax.numpy as jnp
import numpy as np
from jax import lax
from jax.experimental import pallas as pl
from jax.experimental.pallas import tpu as pltpu
from jax.sharding import PartitionSpec as P

CAP = 64
P_SIZE = 4
Q = 56
SOFTEN = 0.05
LANES = 128
BIG = 2.0**100
DEAD = 2.0**120
F32, BF16 = jnp.float32, jnp.bfloat16
REACH = 3
SPAN = 2 * REACH + 1
PITCH = 136


def surface_points():
    steps = np.stack(
        np.meshgrid(np.arange(P_SIZE), np.arange(P_SIZE), np.arange(P_SIZE), indexing="ij"), -1
    ).reshape(-1, 3)
    on_face = np.any((steps == 0) | (steps == P_SIZE - 1), axis=1)
    return (0.5 + 1.4 * (steps[on_face] / (P_SIZE - 1) - 0.5)).astype(np.float32)


def admits(shift, parity):
    return -2 - parity <= shift <= 3 - parity


def split2(x):
    hi = x.astype(BF16)
    return hi, (x - hi.astype(F32)).astype(BF16)


def split3(x):
    hi = x.astype(BF16).astype(F32)
    rest = x - hi
    mid = rest.astype(BF16).astype(F32)
    return hi, mid, rest - mid


def dot(a, b):
    return jnp.dot(a, b, preferred_element_type=F32)


def dot_exact(a, b):
    return jnp.dot(a, b, preferred_element_type=F32, precision=lax.Precision.HIGHEST)


def column_weights(masses, counts, x, y, sz):
    lane = lax.broadcasted_iota(jnp.int32, (1, sz * CAP), 1)
    limit = jnp.zeros((1, sz * CAP), jnp.int32)
    for z in range(sz):
        limit = jnp.where(lane // CAP == z, counts[x, y, z], limit)
    return jnp.where(lane % CAP < limit, masses, 0.0)


def is_odd(axis):
    return lax.axis_index(axis) % 2 == 1


def pack_row_kernel(
    dims, pos_far, mass_far, counts_far, poles_far, send_a, send_b, own,
    pos, mass, counts, poles, sems,
):
    sx, sy, sz = dims
    cols = sx * sy
    copies = [
        pltpu.make_async_copy(far, near, sems.at[i])
        for i, (far, near) in enumerate(
            ((counts_far, counts), (pos_far, pos), (mass_far, mass), (poles_far, poles))
        )
    ]
    for copy in copies:
        copy.start()
    own[...] = jnp.zeros_like(own)
    send_a[...] = jnp.zeros_like(send_a)
    send_b[...] = jnp.zeros_like(send_b)
    for copy in copies:
        copy.wait()
    for x in range(sx):
        at = x * sy
        for c in range(3):
            own[c * cols + at : c * cols + at + sy, :] = pos[c, x] - 0.5
        for y in range(sy):
            row = 3 * cols + at + y
            own[row : row + 1, :] = column_weights(mass[x, y : y + 1, :], counts, x, y, sz)
        own[4 * cols + at : 4 * cols + at + sy, 0 : sz * Q] = poles[x]
    odd = is_odd("row")
    pieces = [(4 * cols, 4 * cols + (sx - REACH) * sy, REACH * sy, 0)]
    base = REACH * sy
    for c in range(4):
        pieces.append((c * cols, c * cols + (sx - 1) * sy, sy, base + c * sy))
    for low, high, rows, at in pieces:
        low_edge, high_edge = own[low : low + rows, :], own[high : high + rows, :]
        send_a[at : at + rows, :] = jnp.where(odd, low_edge, high_edge)
        send_b[at : at + rows, :] = jnp.where(odd, high_edge, low_edge)


def pack_col_kernel(dims, own, got_a, got_b, token, send_a, send_b, next_token, low, high):
    sx, sy, sz = dims
    cols = sx * sy
    odd_row, odd_col = is_odd("row"), is_odd("col")
    next_token[...] = token[...]
    low[...] = jnp.where(odd_row, got_a[...], got_b[...])
    high[...] = jnp.where(odd_row, got_b[...], got_a[...])
    base_in = REACH * sy
    base = REACH * (sx + 2 * REACH)
    px = sx + 2
    send_a[...] = jnp.zeros_like(send_a)
    send_b[...] = jnp.zeros_like(send_b)

    def store(at, rows, ref, start):
        low_edge = ref[start : start + rows, :]
        high_edge = ref[start + sy - rows : start + sy, :]
        send_a[at : at + rows, :] = jnp.where(odd_col, low_edge, high_edge)
        send_b[at : at + rows, :] = jnp.where(odd_col, high_edge, low_edge)

    for x in range(sx + 2 * REACH):
        if REACH <= x < REACH + sx:
            store(x * REACH, REACH, own, 4 * cols + (x - REACH) * sy)
        elif x < REACH:
            store(x * REACH, REACH, low, x * sy)
        else:
            store(x * REACH, REACH, high, (x - REACH - sx) * sy)
    for c in range(4):
        for x in range(px):
            at = base + c * px + x
            if x == 0:
                store(at, 1, low, base_in + c * sy)
            elif x == px - 1:
                store(at, 1, high, base_in + c * sy)
            else:
                store(at, 1, own, c * cols + (x - 1) * sy)


def gather_constant(dims):
    sx, sy, _ = dims
    cells = [(x + REACH, y + REACH) for x in range(sx) for y in range(sy)]
    cells += [(x, y + REACH) for x in range(REACH) for y in range(sy)]
    cells += [(x + REACH + sx, y + REACH) for x in range(REACH) for y in range(sy)]
    cells += [(x, y) for x in range(sx + 2 * REACH) for y in range(REACH)]
    cells += [(x, y + REACH + sy) for x in range(sx + 2 * REACH) for y in range(REACH)]
    at = {cell: i for i, cell in enumerate(cells)}
    pick = np.zeros((2 * LANES, sx * sy * LANES), np.float32)
    for x in range(sx):
        for y in range(sy):
            for a in range(SPAN):
                for b in range(SPAN):
                    if admits(a - REACH, x % 2) and admits(b - REACH, y % 2):
                        for half in range(2):
                            col = (x * sy + y) * LANES + half * 64 + a * SPAN + b
                            pick[half * LANES + at[(x + a, y + b)], col] = 1.0
    return pick


def spread_constant(dims):
    sx, sy, sz = dims
    parents = (sx // 2) * (sy // 2) * (sz // 2)
    pick = np.zeros((sx * sy * sz, 8 * parents), np.float32)
    for z in range(sz):
        for x in range(sx):
            for y in range(sy):
                octant = 4 * (x % 2) + 2 * (y % 2) + z % 2
                parent = ((z // 2) * (sx // 2) + x // 2) * (sy // 2) + y // 2
                pick[(z * sx + x) * sy + y, octant * parents + parent] = 1.0
    return pick


def prepare_kernel(ops, tail, token, table, raw, sems):
    width = ops.shape[1]
    tiles = raw.shape[0]
    whole = tiles - 1

    def fetch(j):
        return pltpu.make_async_copy(ops.at[:, pl.ds(j * LANES, LANES)], raw.at[j], sems.at[j])

    for j in range(whole):
        fetch(j).start()
    raw[tiles - 1] = tail[...]
    ab = lax.broadcasted_iota(jnp.int32, (64, LANES), 0)
    closeby = (jnp.abs(ab // SPAN - REACH) <= 1) & (jnp.abs(ab % SPAN - REACH) <= 1)
    for j in range(tiles):
        if j < whole:
            fetch(j).wait()
        for c in range(SPAN):
            block = raw[j, pl.ds(c, SPAN * SPAN, stride=SPAN), :]
            block = jnp.concatenate(
                [block, jnp.zeros((64 - SPAN * SPAN, LANES), F32)], axis=0
            )
            if abs(c - REACH) <= 1:
                block = jnp.where(closeby, 0.0, block)
            if (j + 1) * LANES > width:
                lane = lax.broadcasted_iota(jnp.int32, (64, LANES), 1)
                block = jnp.where(lane < width - j * LANES, block, 0.0)
            hi, lo = split2(block)
            table[c * 64 : (c + 1) * 64, 2 * j * LANES : (2 * j + 1) * LANES] = hi
            table[c * 64 : (c + 1) * 64, (2 * j + 1) * LANES : (2 * j + 2) * LANES] = lo


def fill_features(sz, place, su, feats, at):
    for half in range(2):
        rows = lax.broadcasted_iota(jnp.int32, (8, LANES), 0) + at
        lane = lax.broadcasted_iota(jnp.int32, (8, LANES), 1) + half * LANES
        lanes = slice(half * LANES, (half + 1) * LANES)
        arrays = [su[c][at : at + 8, lanes] for c in range(4)]
        for k, value in source_features_at(sz, place(rows), arrays, lane):
            feats[half, at * LANES + 8 * k : at * LANES + 8 * (k + 1), :] = value


def features_of(feats, half, i):
    return feats[half, pl.ds((i // 8) * 8 * LANES + i % 8, LANES, stride=8), :]


def turn_features(feats, lhs, i):
    for half in range(2):
        at = (2 * i + half) * LANES
        lhs[at : at + LANES, :] = features_of(feats, half, i).T.astype(BF16)


def near_sums(sz, lhs, rhs, total, src, targets):
    halves = [[h for h in range(2) if any(abs(z - t) <= 1 for t in (2 * h, 2 * h + 1))] for z in range(sz)]

    def add(target, half, d2):
        part = jnp.sum(lax.rsqrt(d2).reshape(d2.shape[0] // 8, 8, LANES), axis=0)
        at, lanes = slice(target * 8, (target + 1) * 8), slice(half * LANES, (half + 1) * LANES)
        total[at, lanes] = total[at, lanes] + part

    def operand(target, half):
        return rhs[target * LANES : (target + 1) * LANES, half * LANES : (half + 1) * LANES]

    base = src * sz * CAP
    middle = [z for z in range(sz) if len(halves[z]) == 2]
    rows = slice(base + middle[0] * CAP, base + (middle[-1] + 1) * CAP)
    for target in targets:
        d2 = dot(lhs[rows, :], rhs[target * LANES : (target + 1) * LANES, :])
        for half in range(2):
            add(target, half, d2[:, half * LANES : (half + 1) * LANES])
    for z in range(sz):
        if len(halves[z]) == 2:
            continue
        half = halves[z][0]
        rows = slice(base + z * CAP, base + (z + 1) * CAP)
        for i in range(0, len(targets), 2):
            both = targets[i : i + 2]
            wide = jnp.concatenate([operand(t, half) for t in both], axis=1)
            d2 = dot(lhs[rows, :], wide)
            for n, target in enumerate(both):
                add(target, half, d2[:, n * LANES : (n + 1) * LANES])


def near_own_kernel(dims, own, near, rhs, token, feats, lhs, rfeats):
    sx, sy, sz = dims
    cols = sx * sy
    token[...] = own[0:8, 0:LANES]
    su = [own.at[c * cols : (c + 1) * cols] for c in range(4)]

    for at in range(0, cols, 8):
        fill_features(sz, lambda rows: (rows // sy + 1, rows % sy + 1), su, feats, at)
    for i in range(cols):
        turn_features(feats, lhs, i)
    for half in range(2):
        lanes = slice(half * LANES, (half + 1) * LANES)
        for at in range(0, cols, 8):
            rows = lax.broadcasted_iota(jnp.int32, (8, LANES), 0) + at
            lane = lax.broadcasted_iota(jnp.int32, (8, LANES), 1) + half * LANES
            arrays = [su[c][at : at + 8, lanes] for c in range(3)]
            for k, value in target_features_at(dims, arrays, rows, lane):
                rfeats[half, at * LANES + 8 * k : at * LANES + 8 * (k + 1), :] = value
    for i in range(cols):
        for half in range(2):
            lanes = slice(half * LANES, (half + 1) * LANES)
            rhs[i * LANES : (i + 1) * LANES, lanes] = features_of(rfeats, half, i).astype(BF16)
    near[...] = jnp.zeros_like(near)
    for x in range(sx):
        for y in range(sy):
            targets = [
                a * sy + b
                for a in range(max(x - 1, 0), min(x + 2, sx))
                for b in range(max(y - 1, 0), min(y + 2, sy))
            ]
            near_sums(sz, lhs, rhs, near, x * sy + y, targets)


def targets_of(dims, cell):
    sx, sy, _ = dims
    return [
        x * sy + y
        for x in range(sx)
        for y in range(sy)
        if 0 <= cell[0] - x <= 2 and 0 <= cell[1] - y <= 2
    ]


def near_row_kernel(dims, got_a, got_b, near_own, rhs, token, near, slots, feats, lhs):
    sx, sy, sz = dims
    base = REACH * sy
    odd = is_odd("row")
    su = [slots.at[c] for c in range(4)]
    slots[...] = jnp.zeros_like(slots)
    for side, (first, second) in enumerate(((got_a, got_b), (got_b, got_a))):
        for c in range(4):
            rows = slice(base + c * sy, base + (c + 1) * sy)
            su[c][side * sy : (side + 1) * sy, :] = jnp.where(odd, first[rows, :], second[rows, :])

    def place(rows):
        return jnp.where(rows < sy, 0, sx + 1), rows % sy + 1

    for at in range(0, slots.shape[1], 8):
        fill_features(sz, place, su, feats, at)
    for i in range(2 * sy):
        turn_features(feats, lhs, i)
    near[...] = near_own[...]
    for i in range(2 * sy):
        cell = ((sx + 1) * (i // sy), i % sy + 1)
        near_sums(sz, lhs, rhs, near, i, targets_of(dims, cell))


def fields_kernel(
    dims,
    own, a1, b1, a2, b2, near_own, rhs, table, parents, l2l, c2e, pick,
    spread, points,
    potential, local_out,
    halo_slots, feats, lhs, near, sm, picked, lm, dens, inherited,
):
    sx, sy, sz = dims
    hx, hy = sx + 2, sy + 2
    cols = sx * sy
    tiles = table.shape[1] // (2 * LANES)
    odd_row, odd_col = is_odd("row"), is_odd("col")
    base1 = REACH * sy
    base2 = REACH * (sx + 2 * REACH)
    su = [halo_slots.at[c] for c in range(4)]
    halo_slots[...] = jnp.zeros_like(halo_slots)
    sm[...] = jnp.zeros_like(sm)
    sm[0:cols, :] = own[4 * cols : 5 * cols, :]
    at = cols
    for first, second in ((a1, b1), (b1, a1)):
        sm[at : at + base1, :] = jnp.where(odd_row, first[0:base1, :], second[0:base1, :])
        at += base1
    for side, (first, second) in enumerate(((a2, b2), (b2, a2))):
        value = jnp.where(odd_col, first[...], second[...])
        sm[at : at + base2, :] = value[0:base2, :]
        at += base2
        for c in range(4):
            rows = slice(base2 + c * hx, base2 + (c + 1) * hx)
            su[c][side * hx : (side + 1) * hx, :] = value[rows, :]

    def place(rows):
        second = rows >= hx
        return jnp.where(second, rows - hx, rows), jnp.where(second, hy - 1, 0)

    halo = {(x, (hy - 1) * side): side * hx + x for side in range(2) for x in range(hx)}

    rows = []
    for pz in range(sz // 2):
        for x in range(sx // 2):
            rows.append(parents[x, :, pz * Q : (pz + 1) * Q])
    above = jnp.concatenate(rows, axis=0)
    below = jnp.concatenate([dot_exact(above, l2l[o]) for o in range(8)], axis=0)
    inherited[...] = dot_exact(spread[...], below)

    for pair in range(sz // 2):
        his, los = [], []
        for zi in range(2):
            z = 2 * pair + zi
            rolled = pltpu.roll(sm[...], (2 * LANES - z * Q) % (2 * LANES), 1)[:, 0:LANES]
            hi, lo = split2(rolled.T[0:64, :])
            his.append(hi)
            los.append(lo)
        keep = lax.broadcasted_iota(jnp.int32, (64, 2 * LANES), 0) < Q
        his = jnp.where(keep, jnp.concatenate(his, axis=1).astype(F32), 0.0)
        los = jnp.where(keep, jnp.concatenate(los, axis=1).astype(F32), 0.0)
        picked[...] = jnp.concatenate([his, los], axis=0).astype(BF16)
        for xy in range(0, cols, 2):
            block = dot(picked[...], pick[:, xy * LANES : (xy + 2) * LANES])
            for i in range(2):
                at = (xy + i) * PITCH
                lm[pair, at : at + LANES, :] = block[:, i * LANES : (i + 1) * LANES]

    period = 16
    lane16 = lax.broadcasted_iota(jnp.int32, (cols, LANES), 1)
    check = [jnp.zeros((cols, LANES), F32) for _ in range(sz)]
    groups = list(range(0, halo_slots.shape[1], 8))
    turns = list(range(len(halo)))
    spans = period * Q // LANES
    for t in range(spans):
        if groups:
            fill_features(sz, place, su, feats, groups.pop(0))
        else:
            for _ in range(-(-len(turns) // (spans - t))):
                turn_features(feats, lhs, turns.pop(0))
        members = [s for s in range(period) if s * Q < (t + 1) * LANES and (s + 1) * Q > t * LANES]
        rows = len(members) * cols
        left = []
        for j in range(-(-Q // period)):
            if j * (period * Q // LANES) + t >= tiles:
                continue
            vectors = [j * period + s for s in members]
            left.append(
                jnp.concatenate(
                    [
                        jnp.concatenate(
                            [
                                lm[p, pl.ds(h * 64 + q, cols, stride=PITCH), :]
                                for p in range(sz // 2)
                            ],
                            axis=1,
                        )
                        for h in range(2)
                        for q in vectors
                    ],
                    axis=0,
                ).astype(BF16)
            )
        for z in range(sz):
            total = None
            for j, block in enumerate(left):
                tile = j * (period * Q // LANES) + t
                first = (REACH - z) * 64
                part = dot(
                    block,
                    table[first : first + sz * 64, 2 * tile * LANES : (2 * tile + 2) * LANES],
                )
                total = part if total is None else total + part
            both = total[0:rows, 0:LANES] + (
                total[0:rows, LANES : 2 * LANES] + total[rows : 2 * rows, 0:LANES]
            )
            for i, s in enumerate(members):
                offset = s * Q - t * LANES
                part = both[i * cols : (i + 1) * cols, :]
                part = jnp.where((lane16 >= offset) & (lane16 < offset + Q), part, 0.0)
                check[z] = check[z] + pltpu.roll(part, (-offset) % LANES, 1)

    assert not groups and not turns

    field = jnp.concatenate([part[:, 0:Q] for part in check], axis=0) + inherited[...]
    field_hi, field_lo = split2(field)
    map_hi, map_lo = split2(c2e[...])
    local = dot(field_hi, map_hi) + (dot(field_hi, map_lo) + dot(field_lo, map_hi))
    dens[...] = jnp.zeros_like(dens)
    dens[0 : sz * cols, 0:Q] = local
    flat = None
    for z in range(sz):
        part = jnp.concatenate(
            [dens[z * cols : (z + 1) * cols, :], jnp.zeros((cols, LANES), F32)], axis=1
        )
        part = pltpu.roll(part, z * Q, 1) if z else part
        flat = part if flat is None else flat + part
    for x in range(sx):
        local_out[x] = flat[x * sy : (x + 1) * sy, 0 : sz * Q]

    turned = dens[...].T[0:64, :]
    hi, lo = split2(turned[:, 0 : sz * cols])
    weights = jnp.concatenate([hi.astype(F32), lo.astype(F32)], axis=1).astype(BF16)
    row = lax.broadcasted_iota(jnp.int32, (2 * sz * cols, sz * CAP), 0) % (sz * cols)
    lane = lax.broadcasted_iota(jnp.int32, (2 * sz * cols, sz * CAP), 1)
    owner = row - (lane // CAP) * cols

    def far(i):
        one_hot = jnp.where(owner == i, 1.0, 0.0).astype(BF16)
        spread_out = dot(weights, one_hot)
        for half in range(2):
            lanes = slice(half * LANES, (half + 1) * LANES)
            d2 = jnp.zeros((64, LANES), F32)
            for c in range(3):
                gap = own[c * cols + i : c * cols + i + 1, lanes] - points[c]
                d2 = d2 + gap * gap
            part = spread_out[:, lanes] * lax.rsqrt(d2)
            at = slice(i * 8, (i + 1) * 8)
            near[at, lanes] = near[at, lanes] + jnp.sum(part.reshape(8, 8, LANES), axis=0)

    near[...] = near_own[...]
    left = list(range(cols))
    for cell, src in halo.items():
        for _ in range(2):
            if left:
                far(left.pop(0))
        near_sums(sz, lhs, rhs, near, src, targets_of(dims, cell))
    assert not left
    for i in range(cols):
        x, y = i // sy, i % sy
        value = jnp.sum(near[i * 8 : (i + 1) * 8, :], axis=0, keepdims=True)
        live = own[3 * cols + i : 3 * cols + i + 1, :] > 0
        potential[x, y : y + 1, :] = jnp.where(live, value, 0.0)


def source_features_at(sz, place, arrays, lane):
    ux, uy, uz, w = arrays
    shape = w.shape
    live = w > 0
    g = jnp.where(live, 1.0 / jnp.where(live, w * w, 1.0), 0.0)
    n = (ux * ux + uy * uy + uz * uz + SOFTEN * SOFTEN) * g
    n = jnp.where(live, n, DEAD)
    v = [split3(-2.0 * u * g) for u in (ux, uy, uz)]
    ones = [
        [place[0] % 3 == m for m in range(3)],
        [place[1] % 3 == m for m in range(3)],
        [lane // CAP == m for m in range(sz)],
    ]
    k = 0
    for c in range(3):
        for piece in (0, 0, 0, 1, 1, 2):
            yield k, v[c][piece]
            k += 1
    for c in range(3):
        for mask in ones[c]:
            for piece in range(3):
                yield k, jnp.where(mask, v[c][piece], 0.0)
                k += 1
    for piece in split3(n):
        yield k, piece
        k += 1
    gs = split3(g)
    for c in range(3):
        for mask in ones[c]:
            for piece in (0, 0, 0, 1, 1, 2):
                yield k, jnp.where(mask, gs[piece], 0.0)
                k += 1
    while k < LANES:
        yield k, jnp.zeros(shape, F32)
        k += 1


def target_features_at(dims, arrays, rows, lane):
    sx, sy, sz = dims
    shape = lane.shape
    place = (rows // sy, rows % sy, lane // CAP)
    t = [split3(u) for u in arrays]

    def shift(c, m):
        if c == 2:
            return (place[2] - m).astype(F32)
        return 1.0 - ((m - place[c] + 6) % 3).astype(F32)

    k = 0
    for c in range(3):
        for piece in (0, 1, 2, 0, 1, 0):
            yield k, t[c][piece]
            k += 1
    for c in range(3):
        for m in range(sz if c == 2 else 3):
            for _ in range(3):
                yield k, shift(c, m)
                k += 1
    for _ in range(3):
        yield k, jnp.ones(shape, F32)
        k += 1
    for c in range(3):
        for m in range(sz if c == 2 else 3):
            moved = arrays[c] + shift(c, m)
            parts = list(split3(moved * moved))
            if c == 2:
                reach = jnp.abs(place[2] - m) <= 1
                parts = [jnp.where(reach, p, BIG if i == 0 else 0.0) for i, p in enumerate(parts)]
            for piece in (0, 1, 2, 0, 1, 0):
                yield k, parts[piece]
                k += 1
    while k < LANES:
        yield k, jnp.zeros(shape, F32)
        k += 1


VMEM = pl.BlockSpec(memory_space=pltpu.VMEM)
SMEM = pl.BlockSpec(memory_space=pltpu.SMEM)
HBM = pl.BlockSpec(memory_space=pltpu.HBM)


def round_up(n, m):
    return -(-n // m) * m


def pack_row(dims, pos, mass, counts, poles):
    sx, sy, sz = dims
    shape = jax.ShapeDtypeStruct((round_up((REACH + 4) * sy, 8), sz * CAP), F32)
    return pl.pallas_call(
        functools.partial(pack_row_kernel, dims),
        out_shape=(shape, shape, jax.ShapeDtypeStruct((5 * sx * sy, sz * CAP), F32)),
        in_specs=[HBM] * 4,
        out_specs=(VMEM,) * 3,
        scratch_shapes=[
            pltpu.VMEM(pos.shape, F32),
            pltpu.VMEM(mass.shape, F32),
            pltpu.SMEM(counts.shape, jnp.int32),
            pltpu.VMEM(poles.shape, F32),
            pltpu.SemaphoreType.DMA((4,)),
        ],
        compiler_params=pltpu.CompilerParams(vmem_limit_bytes=2 << 20),
        name="pack_row",
    )(*(pltpu.with_memory_space_constraint(a, pltpu.HBM) for a in (pos, mass, counts, poles)))


def prepare(ops, token):
    rows, width = ops.shape
    tiles = -(-width // LANES)
    tail = jnp.pad(ops[:, (tiles - 1) * LANES :], ((0, 0), (0, tiles * LANES - width)))
    return pl.pallas_call(
        prepare_kernel,
        out_shape=jax.ShapeDtypeStruct((SPAN * 64, 2 * tiles * LANES), BF16),
        in_specs=[HBM, VMEM, VMEM],
        out_specs=VMEM,
        scratch_shapes=[
            pltpu.VMEM((tiles, rows, LANES), F32),
            pltpu.SemaphoreType.DMA((tiles,)),
        ],
        compiler_params=pltpu.CompilerParams(vmem_limit_bytes=12 << 20),
        cost_estimate=pl.CostEstimate(flops=1 << 24, bytes_accessed=10 << 20, transcendentals=0),
        name="prepare",
    )(ops, tail, token)


def pack_col(dims, own, got_a, got_b, token):
    sx, sy, sz = dims
    rows = round_up(REACH * (sx + 2 * REACH) + 4 * (sx + 2), 8)
    shape = jax.ShapeDtypeStruct((rows, sz * CAP), F32)
    return pl.pallas_call(
        functools.partial(pack_col_kernel, dims),
        out_shape=(shape, shape, jax.ShapeDtypeStruct(token.shape, F32)),
        in_specs=[VMEM] * 4,
        out_specs=(VMEM,) * 3,
        scratch_shapes=[pltpu.VMEM(got_a.shape, F32), pltpu.VMEM(got_a.shape, F32)],
        compiler_params=pltpu.CompilerParams(vmem_limit_bytes=2 << 20),
        name="pack_col",
    )(own, got_a, got_b, token)


def near_own(dims, own):
    sx, sy, sz = dims
    cols = sx * sy
    return pl.pallas_call(
        functools.partial(near_own_kernel, dims),
        out_shape=(
            jax.ShapeDtypeStruct((cols * 8, sz * CAP), F32),
            jax.ShapeDtypeStruct((cols * LANES, sz * CAP), BF16),
            jax.ShapeDtypeStruct((8, LANES), F32),
        ),
        in_specs=[VMEM],
        out_specs=(VMEM,) * 3,
        scratch_shapes=[
            pltpu.VMEM((2, cols * LANES, LANES), F32),
            pltpu.VMEM((cols * sz * CAP, LANES), BF16),
            pltpu.VMEM((2, cols * LANES, LANES), F32),
        ],
        compiler_params=pltpu.CompilerParams(vmem_limit_bytes=10 << 20),
        cost_estimate=pl.CostEstimate(flops=1 << 32, bytes_accessed=1 << 20, transcendentals=1 << 22),
        name="near_own",
    )(own)


def near_row(dims, got_a, got_b, near, rhs, token):
    sx, sy, sz = dims
    slots = round_up(2 * sy, 8)
    return pl.pallas_call(
        functools.partial(near_row_kernel, dims),
        out_shape=jax.ShapeDtypeStruct(near.shape, F32),
        in_specs=[VMEM] * 5,
        out_specs=VMEM,
        scratch_shapes=[
            pltpu.VMEM((4, slots, sz * CAP), F32),
            pltpu.VMEM((2, slots * LANES, LANES), F32),
            pltpu.VMEM((slots * sz * CAP, LANES), BF16),
        ],
        compiler_params=pltpu.CompilerParams(vmem_limit_bytes=6 << 20),
        cost_estimate=pl.CostEstimate(flops=1 << 30, bytes_accessed=1 << 20, transcendentals=1 << 20),
        name="near_row",
    )(got_a, got_b, near, rhs, token)


def fields(dims, own, a1, b1, a2, b2, near, rhs, table, parents, l2l, c2e):
    sx, sy, sz = dims
    cols = sx * sy
    ring = 2 * (sx + 2)
    pick = jnp.asarray(gather_constant(dims), BF16)
    spread = jnp.asarray(spread_constant(dims))
    points = np.full((3, 64, LANES), 10.0, np.float32)
    points[:, :Q, :] = surface_points().T[:, :, None] - 0.5
    return pl.pallas_call(
        functools.partial(fields_kernel, dims),
        out_shape=(
            jax.ShapeDtypeStruct((sx, sy, sz * CAP), F32),
            jax.ShapeDtypeStruct((sx, sy, sz * Q), F32),
        ),
        in_specs=[VMEM] * 14,
        out_specs=(VMEM, VMEM),
        scratch_shapes=[
            pltpu.VMEM((4, round_up(ring, 8), sz * CAP), F32),
            pltpu.VMEM((2, round_up(ring, 8) * LANES, LANES), F32),
            pltpu.VMEM((ring * sz * CAP, LANES), BF16),
            pltpu.VMEM((cols * 8, sz * CAP), F32),
            pltpu.VMEM((LANES, 2 * LANES), F32),
            pltpu.VMEM((LANES, 2 * LANES), BF16),
            pltpu.VMEM((sz // 2, cols * PITCH, LANES), F32),
            pltpu.VMEM((LANES, LANES), F32),
            pltpu.VMEM((sz * cols, Q), F32),
        ],
        compiler_params=pltpu.CompilerParams(vmem_limit_bytes=16 << 20),
        name="fields",
    )(own, a1, b1, a2, b2, near, rhs, table, parents, l2l, c2e, pick, spread,
      jnp.asarray(points))


def exchange(send_a, send_b, axis):
    count = lax.axis_size(axis)
    got = []
    for value, first in ((send_a, 0), (send_b, 1)):
        pairs = [(i, i + 1) for i in range(first, count - 1, 2)]
        got.append(lax.ppermute(value, axis, pairs + [(b, a) for a, b in pairs]))
    return got


def body(positions, masses, counts, multipoles, parent_local, m2l_ops, l2l_ops, check_to_equiv):
    sx, sy, slots = masses.shape
    dims = (sx, sy, slots // CAP)
    send_a, send_b, own = pack_row(dims, positions, masses, counts, multipoles)
    a1, b1 = exchange(send_a, send_b, "row")
    near, rhs, token = near_own(dims, own)
    send_a, send_b, token = pack_col(dims, own, a1, b1, token)
    a2, b2 = exchange(send_a, send_b, "col")
    table = prepare(m2l_ops, token)
    near = near_row(dims, a1, b1, near, rhs, token)
    return fields(
        dims, own, a1, b1, a2, b2, near, rhs, table, parent_local, l2l_ops, check_to_equiv
    )


def solution(mesh):
    return jax.shard_map(
        body,
        mesh=mesh,
        in_specs=(
            P(None, "row", "col", None),
            P("row", "col", None),
            P("row", "col", None),
            P("row", "col", None),
            P("row", "col", None),
            P(),
            P(),
            P(),
        ),
        out_specs=(P("row", "col", None), P("row", "col", None)),
        check_vma=False,
    )
```

```python
import functools

import jax
import jax.numpy as jnp
import numpy as np
from jax import lax
from jax.experimental import pallas as pl
from jax.experimental.pallas import tpu as pltpu
from jax.sharding import PartitionSpec as P

CAP = 64
P_SIZE = 4
Q = 56
SOFTEN = 0.05
LANES = 128
BIG = 2.0**100
DEAD = 2.0**120
F32, BF16 = jnp.float32, jnp.bfloat16
REACH = 3
SPAN = 2 * REACH + 1
PITCH = 136


def surface_points():
    steps = np.stack(
        np.meshgrid(np.arange(P_SIZE), np.arange(P_SIZE), np.arange(P_SIZE), indexing="ij"), -1
    ).reshape(-1, 3)
    on_face = np.any((steps == 0) | (steps == P_SIZE - 1), axis=1)
    return (0.5 + 1.4 * (steps[on_face] / (P_SIZE - 1) - 0.5)).astype(np.float32)


def admits(shift, parity):
    return -2 - parity <= shift <= 3 - parity


def split2(x):
    hi = x.astype(BF16)
    return hi, (x - hi.astype(F32)).astype(BF16)


def split3(x):
    hi = x.astype(BF16).astype(F32)
    rest = x - hi
    mid = rest.astype(BF16).astype(F32)
    return hi, mid, rest - mid


def dot(a, b):
    return jnp.dot(a, b, preferred_element_type=F32)


def dot3(a, b):
    a_hi, a_lo = split2(a)
    b_hi, b_lo = split2(b)
    return dot(a_hi, b_hi) + (dot(a_hi, b_lo) + dot(a_lo, b_hi))


def column_weights(masses, counts, x, y, sz):
    lane = lax.broadcasted_iota(jnp.int32, (1, sz * CAP), 1)
    limit = jnp.zeros((1, sz * CAP), jnp.int32)
    for z in range(sz):
        limit = jnp.where(lane // CAP == z, counts[x, y, z], limit)
    return jnp.where(lane % CAP < limit, masses, 0.0)


def is_odd(axis):
    return lax.axis_index(axis) % 2 == 1


def pack_row_kernel(
    dims, pos_far, mass_far, counts_far, poles_far, send_a, send_b, own,
    pos, mass, counts, poles, sems,
):
    sx, sy, sz = dims
    cols = sx * sy
    copies = [
        pltpu.make_async_copy(far, near, sems.at[i])
        for i, (far, near) in enumerate(
            ((counts_far, counts), (pos_far, pos), (mass_far, mass), (poles_far, poles))
        )
    ]
    for copy in copies:
        copy.start()
    own[...] = jnp.zeros_like(own)
    send_a[...] = jnp.zeros_like(send_a)
    send_b[...] = jnp.zeros_like(send_b)
    for copy in copies:
        copy.wait()
    for x in range(sx):
        at = x * sy
        for c in range(3):
            own[c * cols + at : c * cols + at + sy, :] = pos[c, x] - 0.5
        for y in range(sy):
            row = 3 * cols + at + y
            own[row : row + 1, :] = column_weights(mass[x, y : y + 1, :], counts, x, y, sz)
        own[4 * cols + at : 4 * cols + at + sy, 0 : sz * Q] = poles[x]
    odd = is_odd("row")
    pieces = [(4 * cols, 4 * cols + (sx - REACH) * sy, REACH * sy, 0)]
    base = REACH * sy
    for c in range(4):
        pieces.append((c * cols, c * cols + (sx - 1) * sy, sy, base + c * sy))
    for low, high, rows, at in pieces:
        low_edge, high_edge = own[low : low + rows, :], own[high : high + rows, :]
        send_a[at : at + rows, :] = jnp.where(odd, low_edge, high_edge)
        send_b[at : at + rows, :] = jnp.where(odd, high_edge, low_edge)


def pack_col_kernel(dims, own, got_a, got_b, token, send_a, send_b, next_token, low, high):
    sx, sy, sz = dims
    cols = sx * sy
    odd_row, odd_col = is_odd("row"), is_odd("col")
    next_token[...] = token[...]
    low[...] = jnp.where(odd_row, got_a[...], got_b[...])
    high[...] = jnp.where(odd_row, got_b[...], got_a[...])
    base_in = REACH * sy
    base = REACH * (sx + 2 * REACH)
    px = sx + 2
    send_a[...] = jnp.zeros_like(send_a)
    send_b[...] = jnp.zeros_like(send_b)

    def store(at, rows, ref, start):
        low_edge = ref[start : start + rows, :]
        high_edge = ref[start + sy - rows : start + sy, :]
        send_a[at : at + rows, :] = jnp.where(odd_col, low_edge, high_edge)
        send_b[at : at + rows, :] = jnp.where(odd_col, high_edge, low_edge)

    for x in range(sx + 2 * REACH):
        if REACH <= x < REACH + sx:
            store(x * REACH, REACH, own, 4 * cols + (x - REACH) * sy)
        elif x < REACH:
            store(x * REACH, REACH, low, x * sy)
        else:
            store(x * REACH, REACH, high, (x - REACH - sx) * sy)
    for c in range(4):
        for x in range(px):
            at = base + c * px + x
            if x == 0:
                store(at, 1, low, base_in + c * sy)
            elif x == px - 1:
                store(at, 1, high, base_in + c * sy)
            else:
                store(at, 1, own, c * cols + (x - 1) * sy)


def surface_features(sz):
    points = np.full((64, 3), 10.0, np.float32)
    points[:Q] = surface_points() - np.float32(0.5)

    def pieces(x):
        out = []
        for _ in range(3):
            out.append(np.asarray(x, BF16).astype(np.float32))
            x = x - out[-1]
        return out

    left = np.zeros((64, LANES), np.float32)
    for c in range(3):
        parts = pieces(-2.0 * points[:, c])
        for n, piece in enumerate((0, 0, 0, 1, 1, 2)):
            left[:, 6 * c + n] = parts[piece]
    at = 18 + 3 * (3 + 3 + sz)
    for n, piece in enumerate(pieces((points * points).sum(1))):
        left[:, at + n] = piece
    at += 3 + 6 * (3 + 3 + sz)
    left[:, at : at + 3] = 1.0
    return np.asarray(left, BF16)


def gather_constant(dims):
    sx, sy, _ = dims
    cells = [(x + REACH, y + REACH) for x in range(sx) for y in range(sy)]
    cells += [(x, y + REACH) for x in range(REACH) for y in range(sy)]
    cells += [(x + REACH + sx, y + REACH) for x in range(REACH) for y in range(sy)]
    cells += [(x, y) for x in range(sx + 2 * REACH) for y in range(REACH)]
    cells += [(x, y + REACH + sy) for x in range(sx + 2 * REACH) for y in range(REACH)]
    at = {cell: i for i, cell in enumerate(cells)}
    pick = np.zeros((2 * LANES, sx * sy * LANES), np.float32)
    for x in range(sx):
        for y in range(sy):
            for a in range(SPAN):
                for b in range(SPAN):
                    if admits(a - REACH, x % 2) and admits(b - REACH, y % 2):
                        for half in range(2):
                            col = (x * sy + y) * LANES + half * 64 + a * SPAN + b
                            pick[half * LANES + at[(x + a, y + b)], col] = 1.0
    return pick


def spread_constant(dims):
    sx, sy, sz = dims
    parents = (sx // 2) * (sy // 2) * (sz // 2)
    pick = np.zeros((sx * sy * sz, 8 * parents), np.float32)
    for z in range(sz):
        for x in range(sx):
            for y in range(sy):
                octant = 4 * (x % 2) + 2 * (y % 2) + z % 2
                parent = ((z // 2) * (sx // 2) + x // 2) * (sy // 2) + y // 2
                pick[(z * sx + x) * sy + y, octant * parents + parent] = 1.0
    return pick


def prepare_kernel(raw, table):
    tiles = raw.shape[0]
    ab = lax.broadcasted_iota(jnp.int32, (64, LANES), 0)
    closeby = (jnp.abs(ab // SPAN - REACH) <= 1) & (jnp.abs(ab % SPAN - REACH) <= 1)
    for j in range(tiles):
        for c in range(SPAN):
            block = raw[j, pl.ds(c, SPAN * SPAN, stride=SPAN), :]
            block = jnp.concatenate(
                [block, jnp.zeros((64 - SPAN * SPAN, LANES), F32)], axis=0
            )
            if abs(c - REACH) <= 1:
                block = jnp.where(closeby, 0.0, block)
            hi, lo = split2(block)
            table[c * 64 : (c + 1) * 64, 2 * j * LANES : (2 * j + 1) * LANES] = hi
            table[c * 64 : (c + 1) * 64, (2 * j + 1) * LANES : (2 * j + 2) * LANES] = lo


def fill_features(sz, place, su, feats, at):
    for half in range(2):
        rows = lax.broadcasted_iota(jnp.int32, (8, LANES), 0) + at
        lane = lax.broadcasted_iota(jnp.int32, (8, LANES), 1) + half * LANES
        lanes = slice(half * LANES, (half + 1) * LANES)
        arrays = [su[c][at : at + 8, lanes] for c in range(4)]
        for k, value in source_features_at(sz, place(rows), arrays, lane):
            feats[half, at * LANES + 8 * k : at * LANES + 8 * (k + 1), :] = value


def features_of(feats, half, i):
    return feats[half, pl.ds((i // 8) * 8 * LANES + i % 8, LANES, stride=8), :]


def turn_features(feats, lhs, i):
    for half in range(2):
        at = (2 * i + half) * LANES
        lhs[at : at + LANES, :] = features_of(feats, half, i).T.astype(BF16)


def near_sums(dims, lhs, rhs, total, src, targets):
    sz = dims[2]
    halves = [[h for h in range(2) if any(abs(z - t) <= 1 for t in (2 * h, 2 * h + 1))] for z in range(sz)]

    def add(target, half, d2):
        part = jnp.sum(lax.rsqrt(d2).reshape(d2.shape[0] // 8, 8, LANES), axis=0)
        at, lanes = slice(target * 8, (target + 1) * 8), slice(half * LANES, (half + 1) * LANES)
        total[at, lanes] = total[at, lanes] + part

    def operand(target, half):
        return rhs[target * LANES : (target + 1) * LANES, half * LANES : (half + 1) * LANES]

    base = src * sz * CAP
    middle = [z for z in range(sz) if len(halves[z]) == 2]
    rows = slice(base + middle[0] * CAP, base + (middle[-1] + 1) * CAP)
    for target in targets:
        d2 = dot(lhs[rows, :], rhs[target * LANES : (target + 1) * LANES, :])
        for half in range(2):
            add(target, half, d2[:, half * LANES : (half + 1) * LANES])
    for z in range(sz):
        if len(halves[z]) == 2:
            continue
        half = halves[z][0]
        rows = slice(base + z * CAP, base + (z + 1) * CAP)
        for i in range(0, len(targets), 2):
            both = targets[i : i + 2]
            wide = jnp.concatenate([operand(t, half) for t in both], axis=1)
            d2 = dot(lhs[rows, :], wide)
            for n, target in enumerate(both):
                add(target, half, d2[:, n * LANES : (n + 1) * LANES])


def near_own_kernel(
    dims, own, near, rhs, token, feats, lhs, rfeats
):
    sx, sy, sz = dims
    cols = sx * sy
    token[...] = own[0:8, 0:LANES]
    su = [own.at[c * cols : (c + 1) * cols] for c in range(4)]

    for at in range(0, cols, 8):
        fill_features(sz, lambda rows: (rows // sy + 1, rows % sy + 1), su, feats, at)
    for i in range(cols):
        turn_features(feats, lhs, i)
    for half in range(2):
        lanes = slice(half * LANES, (half + 1) * LANES)
        for at in range(0, cols, 8):
            rows = lax.broadcasted_iota(jnp.int32, (8, LANES), 0) + at
            lane = lax.broadcasted_iota(jnp.int32, (8, LANES), 1) + half * LANES
            arrays = [su[c][at : at + 8, lanes] for c in range(3)]
            for k, value in target_features_at(dims, arrays, rows, lane):
                rfeats[half, at * LANES + 8 * k : at * LANES + 8 * (k + 1), :] = value
    for i in range(cols):
        for half in range(2):
            lanes = slice(half * LANES, (half + 1) * LANES)
            rhs[i * LANES : (i + 1) * LANES, lanes] = features_of(rfeats, half, i).astype(BF16)
    near[...] = jnp.zeros_like(near)
    for i in range(cols):
        cell = (i // sy + 1, i % sy + 1)
        near_sums(dims, lhs, rhs, near, i, targets_of(dims, cell))


def targets_of(dims, cell):
    sx, sy, _ = dims
    return [
        x * sy + y
        for x in range(sx)
        for y in range(sy)
        if 0 <= cell[0] - x <= 2 and 0 <= cell[1] - y <= 2
    ]


def near_row_kernel(
    dims, got_a, got_b, near_own, rhs, parents, l2l, spread, surface, ops, token,
    near, inherited, inverse, raw, slots, feats, lhs,
):
    sx, sy, sz = dims
    base = REACH * sy
    odd = is_odd("row")
    su = [slots.at[c] for c in range(4)]
    slots[...] = jnp.zeros_like(slots)
    for side, (first, second) in enumerate(((got_a, got_b), (got_b, got_a))):
        for c in range(4):
            rows = slice(base + c * sy, base + (c + 1) * sy)
            su[c][side * sy : (side + 1) * sy, :] = jnp.where(odd, first[rows, :], second[rows, :])

    def place(rows):
        return jnp.where(rows < sy, 0, sx + 1), rows % sy + 1

    for at in range(0, slots.shape[1], 8):
        fill_features(sz, place, su, feats, at)
    for i in range(2 * sy):
        turn_features(feats, lhs, i)
    rows = []
    for pz in range(sz // 2):
        for x in range(sx // 2):
            rows.append(parents[x, :, pz * Q : (pz + 1) * Q])
    above = jnp.concatenate(rows, axis=0)
    below = jnp.concatenate([dot3(above, l2l[o]) for o in range(8)], axis=0)
    below_hi, below_lo = split2(below)
    inherited[...] = dot(spread[...], below_hi) + dot(spread[...], below_lo)
    near[...] = near_own[...]
    width = ops.shape[1]
    left = list(range(raw.shape[0]))
    for i in range(2 * sy):
        cell = ((sx + 1) * (i // sy), i % sy + 1)
        near_sums(dims, lhs, rhs, near, i, targets_of(dims, cell))
        for n in range(i * sx // 2, (i + 1) * sx // 2):
            d2 = dot(surface[...], rhs[n * LANES : (n + 1) * LANES, :])
            hi, lo = split2(lax.rsqrt(d2))
            inverse[n * LANES : n * LANES + 64, :] = hi
            inverse[n * LANES + 64 : (n + 1) * LANES, :] = lo
        for _ in range(-(-len(left) // (2 * sy - i))):
            j = left.pop(0)
            lanes = min(LANES, width - j * LANES)
            raw[j, :, 0:lanes] = ops[:, j * LANES : j * LANES + lanes]
            if lanes < LANES:
                raw[j, :, lanes:LANES] = jnp.zeros((ops.shape[0], LANES - lanes), F32)


def fields_kernel(
    dims,
    own, a1, b1, a2, b2, near_own, rhs, table, inverse, inherited, c2e, pick,
    potential, local_out,
    halo_slots, feats, lhs, near, sm, picked, lm, dens,
):
    sx, sy, sz = dims
    hx, hy = sx + 2, sy + 2
    cols = sx * sy
    tiles = table.shape[1] // (2 * LANES)
    odd_row, odd_col = is_odd("row"), is_odd("col")
    base1 = REACH * sy
    base2 = REACH * (sx + 2 * REACH)
    su = [halo_slots.at[c] for c in range(4)]
    halo_slots[...] = jnp.zeros_like(halo_slots)
    sm[...] = jnp.zeros_like(sm)
    sm[0:cols, :] = own[4 * cols : 5 * cols, :]
    at = cols
    for first, second in ((a1, b1), (b1, a1)):
        sm[at : at + base1, :] = jnp.where(odd_row, first[0:base1, :], second[0:base1, :])
        at += base1
    for side, (first, second) in enumerate(((a2, b2), (b2, a2))):
        value = jnp.where(odd_col, first[...], second[...])
        sm[at : at + base2, :] = value[0:base2, :]
        at += base2
        for c in range(4):
            rows = slice(base2 + c * hx, base2 + (c + 1) * hx)
            su[c][side * hx : (side + 1) * hx, :] = value[rows, :]

    def place(rows):
        second = rows >= hx
        return jnp.where(second, rows - hx, rows), jnp.where(second, hy - 1, 0)

    halo = {(x, (hy - 1) * side): side * hx + x for side in range(2) for x in range(hx)}

    for pair in range(sz // 2):
        his, los = [], []
        for zi in range(2):
            z = 2 * pair + zi
            rolled = pltpu.roll(sm[...], (2 * LANES - z * Q) % (2 * LANES), 1)[:, 0:LANES]
            hi, lo = split2(rolled.T[0:64, :])
            his.append(hi)
            los.append(lo)
        keep = lax.broadcasted_iota(jnp.int32, (64, 2 * LANES), 0) < Q
        his = jnp.where(keep, jnp.concatenate(his, axis=1).astype(F32), 0.0)
        los = jnp.where(keep, jnp.concatenate(los, axis=1).astype(F32), 0.0)
        picked[...] = jnp.concatenate([his, los], axis=0).astype(BF16)
        for xy in range(0, cols, 2):
            block = dot(picked[...], pick[:, xy * LANES : (xy + 2) * LANES])
            for i in range(2):
                at = (xy + i) * PITCH
                lm[pair, at : at + LANES, :] = block[:, i * LANES : (i + 1) * LANES]

    period = 16
    lane16 = lax.broadcasted_iota(jnp.int32, (cols, LANES), 1)
    check = [jnp.zeros((cols, LANES), F32) for _ in range(sz)]
    groups = list(range(0, halo_slots.shape[1], 8))
    turns = list(range(len(halo)))
    spans = period * Q // LANES
    for t in range(spans):
        if groups:
            fill_features(sz, place, su, feats, groups.pop(0))
        else:
            for _ in range(-(-len(turns) // (spans - t))):
                turn_features(feats, lhs, turns.pop(0))
        members = [s for s in range(period) if s * Q < (t + 1) * LANES and (s + 1) * Q > t * LANES]
        rows = len(members) * cols
        left = []
        for j in range(-(-Q // period)):
            if j * (period * Q // LANES) + t >= tiles:
                continue
            vectors = [j * period + s for s in members]
            left.append(
                jnp.concatenate(
                    [
                        jnp.concatenate(
                            [
                                lm[p, pl.ds(h * 64 + q, cols, stride=PITCH), :]
                                for p in range(sz // 2)
                            ],
                            axis=1,
                        )
                        for h in range(2)
                        for q in vectors
                    ],
                    axis=0,
                ).astype(BF16)
            )
        for z in range(sz):
            total = None
            for j, block in enumerate(left):
                tile = j * (period * Q // LANES) + t
                first = (REACH - z) * 64
                part = dot(
                    block,
                    table[first : first + sz * 64, 2 * tile * LANES : (2 * tile + 2) * LANES],
                )
                total = part if total is None else total + part
            both = total[0:rows, 0:LANES] + (
                total[0:rows, LANES : 2 * LANES] + total[rows : 2 * rows, 0:LANES]
            )
            for i, s in enumerate(members):
                offset = s * Q - t * LANES
                part = both[i * cols : (i + 1) * cols, :]
                part = jnp.where((lane16 >= offset) & (lane16 < offset + Q), part, 0.0)
                check[z] = check[z] + pltpu.roll(part, (-offset) % LANES, 1)

    assert not groups and not turns

    field = jnp.concatenate([part[:, 0:Q] for part in check], axis=0) + inherited[...]
    local = dot3(field, c2e[...])
    dens[...] = jnp.zeros_like(dens)
    dens[0 : sz * cols, 0:Q] = local
    flat = None
    for z in range(sz):
        part = jnp.concatenate(
            [dens[z * cols : (z + 1) * cols, :], jnp.zeros((cols, LANES), F32)], axis=1
        )
        part = pltpu.roll(part, z * Q, 1) if z else part
        flat = part if flat is None else flat + part
    for x in range(sx):
        local_out[x] = flat[x * sy : (x + 1) * sy, 0 : sz * Q]

    hi, lo = split2(dens[0 : sz * cols, 0:64])
    none = jnp.zeros_like(hi)
    dens[0 : sz * cols, :] = jnp.concatenate([hi, hi], axis=1).astype(F32)
    dens[sz * cols : 2 * sz * cols, :] = jnp.concatenate([lo, none], axis=1).astype(F32)
    row = lax.broadcasted_iota(jnp.int32, (2 * sz, sz * CAP), 0) % sz
    mine = row == lax.broadcasted_iota(jnp.int32, (2 * sz, sz * CAP), 1) // CAP

    def far(i):
        pieces = dens[pl.ds(i, 2 * sz, stride=cols), :].astype(BF16)
        value = dot(pieces, inverse[i * LANES : (i + 1) * LANES, :])
        at = slice(i * 8, i * 8 + 2 * sz)
        near[at, :] = near[at, :] + jnp.where(mine, value, 0.0)

    near[...] = near_own[...]
    left = list(range(cols))
    for cell, src in halo.items():
        for _ in range(2):
            if left:
                far(left.pop(0))
        near_sums(dims, lhs, rhs, near, src, targets_of(dims, cell))
    assert not left
    for i in range(cols):
        x, y = i // sy, i % sy
        value = jnp.sum(near[i * 8 : (i + 1) * 8, :], axis=0, keepdims=True)
        live = own[3 * cols + i : 3 * cols + i + 1, :] > 0
        potential[x, y : y + 1, :] = jnp.where(live, value, 0.0)


def source_features_at(sz, place, arrays, lane):
    ux, uy, uz, w = arrays
    shape = w.shape
    live = w > 0
    g = jnp.where(live, 1.0 / jnp.where(live, w * w, 1.0), 0.0)
    n = (ux * ux + uy * uy + uz * uz + SOFTEN * SOFTEN) * g
    n = jnp.where(live, n, DEAD)
    v = [split3(-2.0 * u * g) for u in (ux, uy, uz)]
    ones = [
        [place[0] % 3 == m for m in range(3)],
        [place[1] % 3 == m for m in range(3)],
        [lane // CAP == m for m in range(sz)],
    ]
    k = 0
    for c in range(3):
        for piece in (0, 0, 0, 1, 1, 2):
            yield k, v[c][piece]
            k += 1
    for c in range(3):
        for mask in ones[c]:
            for piece in range(3):
                yield k, jnp.where(mask, v[c][piece], 0.0)
                k += 1
    for piece in split3(n):
        yield k, piece
        k += 1
    gs = split3(g)
    for c in range(3):
        for mask in ones[c]:
            for piece in (0, 0, 0, 1, 1, 2):
                yield k, jnp.where(mask, gs[piece], 0.0)
                k += 1
    while k < LANES:
        yield k, jnp.zeros(shape, F32)
        k += 1


def target_features_at(dims, arrays, rows, lane):
    sx, sy, sz = dims
    shape = lane.shape
    place = (rows // sy, rows % sy, lane // CAP)
    t = [split3(u) for u in arrays]

    def shift(c, m):
        if c == 2:
            return (place[2] - m).astype(F32)
        return 1.0 - ((m - place[c] + 6) % 3).astype(F32)

    k = 0
    for c in range(3):
        for piece in (0, 1, 2, 0, 1, 0):
            yield k, t[c][piece]
            k += 1
    for c in range(3):
        for m in range(sz if c == 2 else 3):
            for _ in range(3):
                yield k, shift(c, m)
                k += 1
    for _ in range(3):
        yield k, jnp.ones(shape, F32)
        k += 1
    for c in range(3):
        for m in range(sz if c == 2 else 3):
            moved = arrays[c] + shift(c, m)
            parts = list(split3(moved * moved))
            if c == 2:
                reach = jnp.abs(place[2] - m) <= 1
                parts = [jnp.where(reach, p, BIG if i == 0 else 0.0) for i, p in enumerate(parts)]
            for piece in (0, 1, 2, 0, 1, 0):
                yield k, parts[piece]
                k += 1
    for piece in split3(arrays[0] * arrays[0] + arrays[1] * arrays[1] + arrays[2] * arrays[2]):
        yield k, piece
        k += 1
    while k < LANES:
        yield k, jnp.zeros(shape, F32)
        k += 1


VMEM = pl.BlockSpec(memory_space=pltpu.VMEM)
SMEM = pl.BlockSpec(memory_space=pltpu.SMEM)
HBM = pl.BlockSpec(memory_space=pltpu.HBM)


def round_up(n, m):
    return -(-n // m) * m


def pack_row(dims, pos, mass, counts, poles):
    sx, sy, sz = dims
    shape = jax.ShapeDtypeStruct((round_up((REACH + 4) * sy, 8), sz * CAP), F32)
    return pl.pallas_call(
        functools.partial(pack_row_kernel, dims),
        out_shape=(
            shape,
            shape,
            jax.ShapeDtypeStruct((5 * sx * sy, sz * CAP), F32),
        ),
        in_specs=[HBM] * 4,
        out_specs=(VMEM,) * 3,
        scratch_shapes=[
            pltpu.VMEM(pos.shape, F32),
            pltpu.VMEM(mass.shape, F32),
            pltpu.SMEM(counts.shape, jnp.int32),
            pltpu.VMEM(poles.shape, F32),
            pltpu.SemaphoreType.DMA((4,)),
        ],
        compiler_params=pltpu.CompilerParams(vmem_limit_bytes=2 << 20),
        name="pack_row",
    )(*(pltpu.with_memory_space_constraint(a, pltpu.HBM) for a in (pos, mass, counts, poles)))


def prepare(raw):
    tiles = raw.shape[0]
    return pl.pallas_call(
        prepare_kernel,
        out_shape=jax.ShapeDtypeStruct((SPAN * 64, 2 * tiles * LANES), BF16),
        in_specs=[VMEM],
        out_specs=VMEM,
        compiler_params=pltpu.CompilerParams(vmem_limit_bytes=4 << 20),
        cost_estimate=pl.CostEstimate(flops=1 << 24, bytes_accessed=10 << 20, transcendentals=0),
        name="prepare",
    )(raw)


def pack_col(dims, own, got_a, got_b, token):
    sx, sy, sz = dims
    rows = round_up(REACH * (sx + 2 * REACH) + 4 * (sx + 2), 8)
    shape = jax.ShapeDtypeStruct((rows, sz * CAP), F32)
    return pl.pallas_call(
        functools.partial(pack_col_kernel, dims),
        out_shape=(shape, shape, jax.ShapeDtypeStruct(token.shape, F32)),
        in_specs=[VMEM] * 4,
        out_specs=(VMEM,) * 3,
        scratch_shapes=[pltpu.VMEM(got_a.shape, F32), pltpu.VMEM(got_a.shape, F32)],
        compiler_params=pltpu.CompilerParams(vmem_limit_bytes=2 << 20),
        name="pack_col",
    )(own, got_a, got_b, token)


def near_own(dims, own):
    sx, sy, sz = dims
    cols = sx * sy
    operand = jax.ShapeDtypeStruct((cols * LANES, sz * CAP), BF16)
    return pl.pallas_call(
        functools.partial(near_own_kernel, dims),
        out_shape=(
            jax.ShapeDtypeStruct((cols * 8, sz * CAP), F32),
            operand,
            jax.ShapeDtypeStruct((8, LANES), F32),
        ),
        in_specs=[VMEM],
        out_specs=(VMEM,) * 3,
        scratch_shapes=[
            pltpu.VMEM((2, cols * LANES, LANES), F32),
            pltpu.VMEM((cols * sz * CAP, LANES), BF16),
            pltpu.VMEM((2, cols * LANES, LANES), F32),
        ],
        compiler_params=pltpu.CompilerParams(vmem_limit_bytes=9 << 20),
        cost_estimate=pl.CostEstimate(flops=1 << 32, bytes_accessed=1 << 20, transcendentals=1 << 22),
        name="near_own",
    )(own)


def near_row(dims, got_a, got_b, near, rhs, parents, l2l, ops, token):
    sx, sy, sz = dims
    cols = sx * sy
    slots = round_up(2 * sy, 8)
    rows, width = ops.shape
    surface = jnp.asarray(surface_features(sz))
    spread = jnp.asarray(spread_constant(dims), BF16)
    return pl.pallas_call(
        functools.partial(near_row_kernel, dims),
        out_shape=(
            jax.ShapeDtypeStruct((cols * 8, sz * CAP), F32),
            jax.ShapeDtypeStruct((sz * cols, Q), F32),
            jax.ShapeDtypeStruct(rhs.shape, BF16),
            jax.ShapeDtypeStruct((-(-width // LANES), rows, LANES), F32),
        ),
        in_specs=[VMEM] * 10,
        out_specs=(VMEM,) * 4,
        scratch_shapes=[
            pltpu.VMEM((4, slots, sz * CAP), F32),
            pltpu.VMEM((2, slots * LANES, LANES), F32),
            pltpu.VMEM((slots * sz * CAP, LANES), BF16),
        ],
        compiler_params=pltpu.CompilerParams(vmem_limit_bytes=6 << 20),
        cost_estimate=pl.CostEstimate(flops=1 << 30, bytes_accessed=1 << 20, transcendentals=1 << 20),
        name="near_row",
    )(got_a, got_b, near, rhs, parents, l2l, spread, surface, ops, token)


def fields(dims, own, a1, b1, a2, b2, near, rhs, table, inverse, inherited, c2e):
    sx, sy, sz = dims
    cols = sx * sy
    ring = 2 * (sx + 2)
    pick = jnp.asarray(gather_constant(dims), BF16)
    return pl.pallas_call(
        functools.partial(fields_kernel, dims),
        out_shape=(
            jax.ShapeDtypeStruct((sx, sy, sz * CAP), F32),
            jax.ShapeDtypeStruct((sx, sy, sz * Q), F32),
        ),
        in_specs=[VMEM] * 12,
        out_specs=(VMEM, VMEM),
        scratch_shapes=[
            pltpu.VMEM((4, round_up(ring, 8), sz * CAP), F32),
            pltpu.VMEM((2, round_up(ring, 8) * LANES, LANES), F32),
            pltpu.VMEM((ring * sz * CAP, LANES), BF16),
            pltpu.VMEM(near.shape, F32),
            pltpu.VMEM((LANES, 2 * LANES), F32),
            pltpu.VMEM((LANES, 2 * LANES), BF16),
            pltpu.VMEM((sz // 2, cols * PITCH, LANES), F32),
            pltpu.VMEM((LANES, LANES), F32),
        ],
        compiler_params=pltpu.CompilerParams(vmem_limit_bytes=16 << 20),
        name="fields",
    )(own, a1, b1, a2, b2, near, rhs, table, inverse, inherited, c2e, pick)


def exchange(send_a, send_b, axis):
    count = lax.axis_size(axis)
    got = []
    for value, first in ((send_a, 0), (send_b, 1)):
        pairs = [(i, i + 1) for i in range(first, count - 1, 2)]
        got.append(lax.ppermute(value, axis, pairs + [(b, a) for a, b in pairs]))
    return got


def body(positions, masses, counts, multipoles, parent_local, m2l_ops, l2l_ops, check_to_equiv):
    sx, sy, slots = masses.shape
    dims = (sx, sy, slots // CAP)
    send_a, send_b, own = pack_row(dims, positions, masses, counts, multipoles)
    a1, b1 = exchange(send_a, send_b, "row")
    near, rhs, token = near_own(dims, own)
    send_a, send_b, token = pack_col(dims, own, a1, b1, token)
    a2, b2 = exchange(send_a, send_b, "col")
    near, inherited, inverse, raw = near_row(
        dims, a1, b1, near, rhs, parent_local, l2l_ops, m2l_ops, token
    )
    table = prepare(raw)
    return fields(
        dims, own, a1, b1, a2, b2, near, rhs, table, inverse, inherited, check_to_equiv
    )


def solution(mesh):
    return jax.shard_map(
        body,
        mesh=mesh,
        in_specs=(
            P(None, "row", "col", None),
            P("row", "col", None),
            P("row", "col", None),
            P("row", "col", None),
            P("row", "col", None),
            P(),
            P(),
            P(),
        ),
        out_specs=(P("row", "col", None), P("row", "col", None)),
        check_vma=False,
    )
```

```python
import functools

import jax
import jax.numpy as jnp
import numpy as np
from jax import lax
from jax.experimental import pallas as pl
from jax.experimental.pallas import tpu as pltpu
from jax.sharding import PartitionSpec as P

CAP = 64
P_SIZE = 4
Q = 56
SOFTEN = 0.05
LANES = 128
BIG = 2.0**100
DEAD = 2.0**120
F32, BF16 = jnp.float32, jnp.bfloat16
REACH = 3
SPAN = 2 * REACH + 1
PITCH = 136


def surface_points():
    steps = np.stack(
        np.meshgrid(np.arange(P_SIZE), np.arange(P_SIZE), np.arange(P_SIZE), indexing="ij"), -1
    ).reshape(-1, 3)
    on_face = np.any((steps == 0) | (steps == P_SIZE - 1), axis=1)
    return (0.5 + 1.4 * (steps[on_face] / (P_SIZE - 1) - 0.5)).astype(np.float32)


def admits(shift, parity):
    return -2 - parity <= shift <= 3 - parity


def split2(x):
    hi = x.astype(BF16)
    return hi, (x - hi.astype(F32)).astype(BF16)


def split3(x):
    hi = x.astype(BF16).astype(F32)
    rest = x - hi
    mid = rest.astype(BF16).astype(F32)
    return hi, mid, rest - mid


def dot(a, b):
    return jnp.dot(a, b, preferred_element_type=F32)


def dot3(a, b):
    a_hi, a_lo = split2(a)
    b_hi, b_lo = split2(b)
    return dot(a_hi, b_hi) + (dot(a_hi, b_lo) + dot(a_lo, b_hi))


def column_weights(masses, counts, x, y, sz):
    lane = lax.broadcasted_iota(jnp.int32, (1, sz * CAP), 1)
    limit = jnp.zeros((1, sz * CAP), jnp.int32)
    for z in range(sz):
        limit = jnp.where(lane // CAP == z, counts[x, y, z], limit)
    return jnp.where(lane % CAP < limit, masses, 0.0)


def is_odd(axis):
    return lax.axis_index(axis) % 2 == 1


def pack_row_kernel(
    dims, pos_far, mass_far, counts_far, poles_far, send_a, send_b, own,
    pos, mass, counts, poles, sems,
):
    sx, sy, sz = dims
    cols = sx * sy
    copies = [
        pltpu.make_async_copy(far, near, sems.at[i])
        for i, (far, near) in enumerate(
            ((counts_far, counts), (pos_far, pos), (mass_far, mass), (poles_far, poles))
        )
    ]
    for copy in copies:
        copy.start()
    own[...] = jnp.zeros_like(own)
    send_a[...] = jnp.zeros_like(send_a)
    send_b[...] = jnp.zeros_like(send_b)
    for copy in copies:
        copy.wait()
    for x in range(sx):
        at = x * sy
        for c in range(3):
            own[c * cols + at : c * cols + at + sy, :] = pos[c, x] - 0.5
        for y in range(sy):
            row = 3 * cols + at + y
            own[row : row + 1, :] = column_weights(mass[x, y : y + 1, :], counts, x, y, sz)
        own[4 * cols + at : 4 * cols + at + sy, 0 : sz * Q] = poles[x]
    odd = is_odd("row")
    pieces = [(4 * cols, 4 * cols + (sx - REACH) * sy, REACH * sy, 0)]
    base = REACH * sy
    for c in range(4):
        pieces.append((c * cols, c * cols + (sx - 1) * sy, sy, base + c * sy))
    for low, high, rows, at in pieces:
        low_edge, high_edge = own[low : low + rows, :], own[high : high + rows, :]
        send_a[at : at + rows, :] = jnp.where(odd, low_edge, high_edge)
        send_b[at : at + rows, :] = jnp.where(odd, high_edge, low_edge)


def pack_col_kernel(dims, own, got_a, got_b, token, send_a, send_b, next_token, low, high):
    sx, sy, sz = dims
    cols = sx * sy
    odd_row, odd_col = is_odd("row"), is_odd("col")
    next_token[...] = token[...]
    low[...] = jnp.where(odd_row, got_a[...], got_b[...])
    high[...] = jnp.where(odd_row, got_b[...], got_a[...])
    base_in = REACH * sy
    base = REACH * (sx + 2 * REACH)
    px = sx + 2
    send_a[...] = jnp.zeros_like(send_a)
    send_b[...] = jnp.zeros_like(send_b)

    def store(at, rows, ref, start):
        low_edge = ref[start : start + rows, :]
        high_edge = ref[start + sy - rows : start + sy, :]
        send_a[at : at + rows, :] = jnp.where(odd_col, low_edge, high_edge)
        send_b[at : at + rows, :] = jnp.where(odd_col, high_edge, low_edge)

    for x in range(sx + 2 * REACH):
        if REACH <= x < REACH + sx:
            store(x * REACH, REACH, own, 4 * cols + (x - REACH) * sy)
        elif x < REACH:
            store(x * REACH, REACH, low, x * sy)
        else:
            store(x * REACH, REACH, high, (x - REACH - sx) * sy)
    for c in range(4):
        for x in range(px):
            at = base + c * px + x
            if x == 0:
                store(at, 1, low, base_in + c * sy)
            elif x == px - 1:
                store(at, 1, high, base_in + c * sy)
            else:
                store(at, 1, own, c * cols + (x - 1) * sy)


def surface_features(sz):
    points = np.full((64, 3), 10.0, np.float32)
    points[:Q] = surface_points() - np.float32(0.5)

    def pieces(x):
        out = []
        for _ in range(3):
            out.append(np.asarray(x, BF16).astype(np.float32))
            x = x - out[-1]
        return out

    left = np.zeros((64, LANES), np.float32)
    for c in range(3):
        parts = pieces(-2.0 * points[:, c])
        for n, piece in enumerate((0, 0, 0, 1, 1, 2)):
            left[:, 6 * c + n] = parts[piece]
    at = 18 + 3 * (3 + 3 + sz)
    for n, piece in enumerate(pieces((points * points).sum(1))):
        left[:, at + n] = piece
    at += 3 + 6 * (3 + 3 + sz)
    left[:, at : at + 3] = 1.0
    return np.asarray(left, BF16)


def gather_constant(dims):
    sx, sy, _ = dims
    cells = [(x + REACH, y + REACH) for x in range(sx) for y in range(sy)]
    cells += [(x, y + REACH) for x in range(REACH) for y in range(sy)]
    cells += [(x + REACH + sx, y + REACH) for x in range(REACH) for y in range(sy)]
    cells += [(x, y) for x in range(sx + 2 * REACH) for y in range(REACH)]
    cells += [(x, y + REACH + sy) for x in range(sx + 2 * REACH) for y in range(REACH)]
    at = {cell: i for i, cell in enumerate(cells)}
    pick = np.zeros((2 * LANES, sx * sy * LANES), np.float32)
    for x in range(sx):
        for y in range(sy):
            for a in range(SPAN):
                for b in range(SPAN):
                    if admits(a - REACH, x % 2) and admits(b - REACH, y % 2):
                        for half in range(2):
                            col = (x * sy + y) * LANES + half * 64 + a * SPAN + b
                            pick[half * LANES + at[(x + a, y + b)], col] = 1.0
    return pick


def spread_constant(dims):
    sx, sy, sz = dims
    parents = (sx // 2) * (sy // 2) * (sz // 2)
    pick = np.zeros((sx * sy * sz, 8 * parents), np.float32)
    for z in range(sz):
        for x in range(sx):
            for y in range(sy):
                octant = 4 * (x % 2) + 2 * (y % 2) + z % 2
                parent = ((z // 2) * (sx // 2) + x // 2) * (sy // 2) + y // 2
                pick[(z * sx + x) * sy + y, octant * parents + parent] = 1.0
    return pick


def prepare_kernel(raw, table):
    tiles = raw.shape[0]
    ab = lax.broadcasted_iota(jnp.int32, (64, LANES), 0)
    closeby = (jnp.abs(ab // SPAN - REACH) <= 1) & (jnp.abs(ab % SPAN - REACH) <= 1)
    for j in range(tiles):
        for c in range(SPAN):
            block = raw[j, pl.ds(c, SPAN * SPAN, stride=SPAN), :]
            block = jnp.concatenate(
                [block, jnp.zeros((64 - SPAN * SPAN, LANES), F32)], axis=0
            )
            if abs(c - REACH) <= 1:
                block = jnp.where(closeby, 0.0, block)
            hi, lo = split2(block)
            table[c * 64 : (c + 1) * 64, 2 * j * LANES : (2 * j + 1) * LANES] = hi
            table[c * 64 : (c + 1) * 64, (2 * j + 1) * LANES : (2 * j + 2) * LANES] = lo


def fill_features(sz, place, su, feats, at):
    for half in range(2):
        rows = lax.broadcasted_iota(jnp.int32, (8, LANES), 0) + at
        lane = lax.broadcasted_iota(jnp.int32, (8, LANES), 1) + half * LANES
        lanes = slice(half * LANES, (half + 1) * LANES)
        arrays = [su[c][at : at + 8, lanes] for c in range(4)]
        for k, value in source_features_at(sz, place(rows), arrays, lane):
            feats[half, at * LANES + 8 * k : at * LANES + 8 * (k + 1), :] = value


def features_of(feats, half, i):
    return feats[half, pl.ds((i // 8) * 8 * LANES + i % 8, LANES, stride=8), :]


def turn_features(feats, lhs, i):
    for half in range(2):
        at = (2 * i + half) * LANES
        lhs[at : at + LANES, :] = features_of(feats, half, i).T.astype(BF16)


def near_sums(dims, lhs, rhs, total, src, targets):
    sz = dims[2]
    halves = [[h for h in range(2) if any(abs(z - t) <= 1 for t in (2 * h, 2 * h + 1))] for z in range(sz)]

    def add(target, half, d2):
        part = jnp.sum(lax.rsqrt(d2).reshape(d2.shape[0] // 8, 8, LANES), axis=0)
        at, lanes = slice(target * 8, (target + 1) * 8), slice(half * LANES, (half + 1) * LANES)
        total[at, lanes] = total[at, lanes] + part

    def operand(target, half):
        return rhs[target * LANES : (target + 1) * LANES, half * LANES : (half + 1) * LANES]

    base = src * sz * CAP
    middle = [z for z in range(sz) if len(halves[z]) == 2]
    rows = slice(base + middle[0] * CAP, base + (middle[-1] + 1) * CAP)
    for target in targets:
        d2 = dot(lhs[rows, :], rhs[target * LANES : (target + 1) * LANES, :])
        for half in range(2):
            add(target, half, d2[:, half * LANES : (half + 1) * LANES])
    for z in range(sz):
        if len(halves[z]) == 2:
            continue
        half = halves[z][0]
        rows = slice(base + z * CAP, base + (z + 1) * CAP)
        for i in range(0, len(targets), 2):
            both = targets[i : i + 2]
            wide = jnp.concatenate([operand(t, half) for t in both], axis=1)
            d2 = dot(lhs[rows, :], wide)
            for n, target in enumerate(both):
                add(target, half, d2[:, n * LANES : (n + 1) * LANES])


def near_own_kernel(
    dims, own, near, rhs, token, feats, lhs, rfeats
):
    sx, sy, sz = dims
    cols = sx * sy
    token[...] = own[0:8, 0:LANES]
    su = [own.at[c * cols : (c + 1) * cols] for c in range(4)]

    for at in range(0, cols, 8):
        fill_features(sz, lambda rows: (rows // sy + 1, rows % sy + 1), su, feats, at)
    for i in range(cols):
        turn_features(feats, lhs, i)
    for half in range(2):
        lanes = slice(half * LANES, (half + 1) * LANES)
        for at in range(0, cols, 8):
            rows = lax.broadcasted_iota(jnp.int32, (8, LANES), 0) + at
            lane = lax.broadcasted_iota(jnp.int32, (8, LANES), 1) + half * LANES
            arrays = [su[c][at : at + 8, lanes] for c in range(3)]
            for k, value in target_features_at(dims, arrays, rows, lane):
                rfeats[half, at * LANES + 8 * k : at * LANES + 8 * (k + 1), :] = value
    for i in range(cols):
        for half in range(2):
            lanes = slice(half * LANES, (half + 1) * LANES)
            rhs[i * LANES : (i + 1) * LANES, lanes] = features_of(rfeats, half, i).astype(BF16)
    near[...] = jnp.zeros_like(near)
    for i in range(cols):
        cell = (i // sy + 1, i % sy + 1)
        near_sums(dims, lhs, rhs, near, i, targets_of(dims, cell))


def targets_of(dims, cell):
    sx, sy, _ = dims
    return [
        x * sy + y
        for x in range(sx)
        for y in range(sy)
        if 0 <= cell[0] - x <= 2 and 0 <= cell[1] - y <= 2
    ]


def near_row_kernel(
    dims, got_a, got_b, near_own, rhs, parents, l2l, spread, surface, ops, token,
    near, inherited, inverse, raw, slots, feats, lhs,
):
    sx, sy, sz = dims
    base = REACH * sy
    odd = is_odd("row")
    su = [slots.at[c] for c in range(4)]
    slots[...] = jnp.zeros_like(slots)
    for side, (first, second) in enumerate(((got_a, got_b), (got_b, got_a))):
        for c in range(4):
            rows = slice(base + c * sy, base + (c + 1) * sy)
            su[c][side * sy : (side + 1) * sy, :] = jnp.where(odd, first[rows, :], second[rows, :])

    def place(rows):
        return jnp.where(rows < sy, 0, sx + 1), rows % sy + 1

    for at in range(0, slots.shape[1], 8):
        fill_features(sz, place, su, feats, at)
    for i in range(2 * sy):
        turn_features(feats, lhs, i)
    rows = []
    for pz in range(sz // 2):
        for x in range(sx // 2):
            rows.append(parents[x, :, pz * Q : (pz + 1) * Q])
    above = jnp.concatenate(rows, axis=0)
    below = jnp.concatenate([dot3(above, l2l[o]) for o in range(8)], axis=0)
    below_hi, below_lo = split2(below)
    inherited[...] = dot(spread[...], below_hi) + dot(spread[...], below_lo)
    near[...] = near_own[...]
    width = ops.shape[1]
    left = list(range(raw.shape[0]))
    for i in range(2 * sy):
        cell = ((sx + 1) * (i // sy), i % sy + 1)
        near_sums(dims, lhs, rhs, near, i, targets_of(dims, cell))
        for n in range(i * sx // 2, (i + 1) * sx // 2):
            d2 = dot(surface[...], rhs[n * LANES : (n + 1) * LANES, :])
            hi, lo = split2(lax.rsqrt(d2))
            inverse[n * LANES : n * LANES + 64, :] = hi
            inverse[n * LANES + 64 : (n + 1) * LANES, :] = lo
        for _ in range(-(-len(left) // (2 * sy - i))):
            j = left.pop(0)
            lanes = min(LANES, width - j * LANES)
            raw[j, :, 0:lanes] = ops[:, j * LANES : j * LANES + lanes]
            if lanes < LANES:
                raw[j, :, lanes:LANES] = jnp.zeros((ops.shape[0], LANES - lanes), F32)


def fields_kernel(
    dims,
    own, a1, b1, a2, b2, near_own, rhs, table, inverse, inherited, c2e, pick,
    potential, local_out,
    halo_slots, feats, lhs, near, sm, picked, lm, dens,
):
    sx, sy, sz = dims
    hx, hy = sx + 2, sy + 2
    cols = sx * sy
    tiles = table.shape[1] // (2 * LANES)
    odd_row, odd_col = is_odd("row"), is_odd("col")
    base1 = REACH * sy
    base2 = REACH * (sx + 2 * REACH)
    su = [halo_slots.at[c] for c in range(4)]
    halo_slots[...] = jnp.zeros_like(halo_slots)
    sm[...] = jnp.zeros_like(sm)
    sm[0:cols, :] = own[4 * cols : 5 * cols, :]
    at = cols
    for first, second in ((a1, b1), (b1, a1)):
        sm[at : at + base1, :] = jnp.where(odd_row, first[0:base1, :], second[0:base1, :])
        at += base1
    for side, (first, second) in enumerate(((a2, b2), (b2, a2))):
        value = jnp.where(odd_col, first[...], second[...])
        sm[at : at + base2, :] = value[0:base2, :]
        at += base2
        for c in range(4):
            rows = slice(base2 + c * hx, base2 + (c + 1) * hx)
            su[c][side * hx : (side + 1) * hx, :] = value[rows, :]

    def place(rows):
        second = rows >= hx
        return jnp.where(second, rows - hx, rows), jnp.where(second, hy - 1, 0)

    halo = {(x, (hy - 1) * side): side * hx + x for side in range(2) for x in range(hx)}

    for at in range(0, halo_slots.shape[1], 8):
        fill_features(sz, place, su, feats, at)
    for i in range(len(halo)):
        turn_features(feats, lhs, i)

    for pair in range(sz // 2):
        his, los = [], []
        for zi in range(2):
            z = 2 * pair + zi
            rolled = pltpu.roll(sm[...], (2 * LANES - z * Q) % (2 * LANES), 1)[:, 0:LANES]
            hi, lo = split2(rolled.T[0:64, :])
            his.append(hi)
            los.append(lo)
        keep = lax.broadcasted_iota(jnp.int32, (64, 2 * LANES), 0) < Q
        his = jnp.where(keep, jnp.concatenate(his, axis=1).astype(F32), 0.0)
        los = jnp.where(keep, jnp.concatenate(los, axis=1).astype(F32), 0.0)
        picked[...] = jnp.concatenate([his, los], axis=0).astype(BF16)
        for xy in range(0, cols, 2):
            block = dot(picked[...], pick[:, xy * LANES : (xy + 2) * LANES])
            for i in range(2):
                at = (xy + i) * PITCH
                lm[pair, at : at + LANES, :] = block[:, i * LANES : (i + 1) * LANES]

    period = 16
    lane16 = lax.broadcasted_iota(jnp.int32, (cols, LANES), 1)
    check = [jnp.zeros((cols, LANES), F32) for _ in range(sz)]
    near[...] = near_own[...]
    sources = list(halo.items())
    spans = period * Q // LANES
    for t in range(spans):
        members = [s for s in range(period) if s * Q < (t + 1) * LANES and (s + 1) * Q > t * LANES]
        rows = len(members) * cols
        left = []
        for j in range(-(-Q // period)):
            if j * (period * Q // LANES) + t >= tiles:
                continue
            vectors = [j * period + s for s in members]
            left.append(
                jnp.concatenate(
                    [
                        jnp.concatenate(
                            [
                                lm[p, pl.ds(h * 64 + q, cols, stride=PITCH), :]
                                for p in range(sz // 2)
                            ],
                            axis=1,
                        )
                        for h in range(2)
                        for q in vectors
                    ],
                    axis=0,
                ).astype(BF16)
            )
        for z in range(sz):
            total = None
            for j, block in enumerate(left):
                tile = j * (period * Q // LANES) + t
                first = (REACH - z) * 64
                part = dot(
                    block,
                    table[first : first + sz * 64, 2 * tile * LANES : (2 * tile + 2) * LANES],
                )
                total = part if total is None else total + part
            both = total[0:rows, 0:LANES] + (
                total[0:rows, LANES : 2 * LANES] + total[rows : 2 * rows, 0:LANES]
            )
            for i, s in enumerate(members):
                offset = s * Q - t * LANES
                part = both[i * cols : (i + 1) * cols, :]
                part = jnp.where((lane16 >= offset) & (lane16 < offset + Q), part, 0.0)
                check[z] = check[z] + pltpu.roll(part, (-offset) % LANES, 1)
        for _ in range(-(-len(sources) // (spans - t))):
            cell, src = sources.pop(0)
            near_sums(dims, lhs, rhs, near, src, targets_of(dims, cell))
    assert not sources

    field = jnp.concatenate([part[:, 0:Q] for part in check], axis=0) + inherited[...]
    local = dot3(field, c2e[...])
    dens[...] = jnp.zeros_like(dens)
    dens[0 : sz * cols, 0:Q] = local
    flat = None
    for z in range(sz):
        part = jnp.concatenate(
            [dens[z * cols : (z + 1) * cols, :], jnp.zeros((cols, LANES), F32)], axis=1
        )
        part = pltpu.roll(part, z * Q, 1) if z else part
        flat = part if flat is None else flat + part
    for x in range(sx):
        local_out[x] = flat[x * sy : (x + 1) * sy, 0 : sz * Q]

    hi, lo = split2(dens[0 : sz * cols, 0:64])
    none = jnp.zeros_like(hi)
    dens[0 : sz * cols, :] = jnp.concatenate([hi, hi], axis=1).astype(F32)
    dens[sz * cols : 2 * sz * cols, :] = jnp.concatenate([lo, none], axis=1).astype(F32)
    row = lax.broadcasted_iota(jnp.int32, (2 * sz, sz * CAP), 0) % sz
    mine = row == lax.broadcasted_iota(jnp.int32, (2 * sz, sz * CAP), 1) // CAP

    def far(i):
        pieces = dens[pl.ds(i, 2 * sz, stride=cols), :].astype(BF16)
        value = dot(pieces, inverse[i * LANES : (i + 1) * LANES, :])
        at = slice(i * 8, i * 8 + 2 * sz)
        near[at, :] = near[at, :] + jnp.where(mine, value, 0.0)

    for i in range(cols):
        far(i)
    for i in range(cols):
        x, y = i // sy, i % sy
        value = jnp.sum(near[i * 8 : (i + 1) * 8, :], axis=0, keepdims=True)
        live = own[3 * cols + i : 3 * cols + i + 1, :] > 0
        potential[x, y : y + 1, :] = jnp.where(live, value, 0.0)


def source_features_at(sz, place, arrays, lane):
    ux, uy, uz, w = arrays
    shape = w.shape
    live = w > 0
    g = jnp.where(live, 1.0 / jnp.where(live, w * w, 1.0), 0.0)
    n = (ux * ux + uy * uy + uz * uz + SOFTEN * SOFTEN) * g
    n = jnp.where(live, n, DEAD)
    v = [split3(-2.0 * u * g) for u in (ux, uy, uz)]
    ones = [
        [place[0] % 3 == m for m in range(3)],
        [place[1] % 3 == m for m in range(3)],
        [lane // CAP == m for m in range(sz)],
    ]
    k = 0
    for c in range(3):
        for piece in (0, 0, 0, 1, 1, 2):
            yield k, v[c][piece]
            k += 1
    for c in range(3):
        for mask in ones[c]:
            for piece in range(3):
                yield k, jnp.where(mask, v[c][piece], 0.0)
                k += 1
    for piece in split3(n):
        yield k, piece
        k += 1
    gs = split3(g)
    for c in range(3):
        for mask in ones[c]:
            for piece in (0, 0, 0, 1, 1, 2):
                yield k, jnp.where(mask, gs[piece], 0.0)
                k += 1
    while k < LANES:
        yield k, jnp.zeros(shape, F32)
        k += 1


def target_features_at(dims, arrays, rows, lane):
    sx, sy, sz = dims
    shape = lane.shape
    place = (rows // sy, rows % sy, lane // CAP)
    t = [split3(u) for u in arrays]

    def shift(c, m):
        if c == 2:
            return (place[2] - m).astype(F32)
        return 1.0 - ((m - place[c] + 6) % 3).astype(F32)

    k = 0
    for c in range(3):
        for piece in (0, 1, 2, 0, 1, 0):
            yield k, t[c][piece]
            k += 1
    for c in range(3):
        for m in range(sz if c == 2 else 3):
            for _ in range(3):
                yield k, shift(c, m)
                k += 1
    for _ in range(3):
        yield k, jnp.ones(shape, F32)
        k += 1
    for c in range(3):
        for m in range(sz if c == 2 else 3):
            moved = arrays[c] + shift(c, m)
            parts = list(split3(moved * moved))
            if c == 2:
                reach = jnp.abs(place[2] - m) <= 1
                parts = [jnp.where(reach, p, BIG if i == 0 else 0.0) for i, p in enumerate(parts)]
            for piece in (0, 1, 2, 0, 1, 0):
                yield k, parts[piece]
                k += 1
    for piece in split3(arrays[0] * arrays[0] + arrays[1] * arrays[1] + arrays[2] * arrays[2]):
        yield k, piece
        k += 1
    while k < LANES:
        yield k, jnp.zeros(shape, F32)
        k += 1


VMEM = pl.BlockSpec(memory_space=pltpu.VMEM)
SMEM = pl.BlockSpec(memory_space=pltpu.SMEM)
HBM = pl.BlockSpec(memory_space=pltpu.HBM)


def round_up(n, m):
    return -(-n // m) * m


def pack_row(dims, pos, mass, counts, poles):
    sx, sy, sz = dims
    shape = jax.ShapeDtypeStruct((round_up((REACH + 4) * sy, 8), sz * CAP), F32)
    return pl.pallas_call(
        functools.partial(pack_row_kernel, dims),
        out_shape=(
            shape,
            shape,
            jax.ShapeDtypeStruct((5 * sx * sy, sz * CAP), F32),
        ),
        in_specs=[HBM] * 4,
        out_specs=(VMEM,) * 3,
        scratch_shapes=[
            pltpu.VMEM(pos.shape, F32),
            pltpu.VMEM(mass.shape, F32),
            pltpu.SMEM(counts.shape, jnp.int32),
            pltpu.VMEM(poles.shape, F32),
            pltpu.SemaphoreType.DMA((4,)),
        ],
        compiler_params=pltpu.CompilerParams(vmem_limit_bytes=2 << 20),
        name="pack_row",
    )(*(pltpu.with_memory_space_constraint(a, pltpu.HBM) for a in (pos, mass, counts, poles)))


def prepare(raw):
    tiles = raw.shape[0]
    return pl.pallas_call(
        prepare_kernel,
        out_shape=jax.ShapeDtypeStruct((SPAN * 64, 2 * tiles * LANES), BF16),
        in_specs=[VMEM],
        out_specs=VMEM,
        compiler_params=pltpu.CompilerParams(vmem_limit_bytes=4 << 20),
        cost_estimate=pl.CostEstimate(flops=1 << 24, bytes_accessed=1 << 20, transcendentals=0),
        name="prepare",
    )(raw)


def pack_col(dims, own, got_a, got_b, token):
    sx, sy, sz = dims
    rows = round_up(REACH * (sx + 2 * REACH) + 4 * (sx + 2), 8)
    shape = jax.ShapeDtypeStruct((rows, sz * CAP), F32)
    return pl.pallas_call(
        functools.partial(pack_col_kernel, dims),
        out_shape=(shape, shape, jax.ShapeDtypeStruct(token.shape, F32)),
        in_specs=[VMEM] * 4,
        out_specs=(VMEM,) * 3,
        scratch_shapes=[pltpu.VMEM(got_a.shape, F32), pltpu.VMEM(got_a.shape, F32)],
        compiler_params=pltpu.CompilerParams(vmem_limit_bytes=2 << 20),
        name="pack_col",
    )(own, got_a, got_b, token)


def near_own(dims, own):
    sx, sy, sz = dims
    cols = sx * sy
    operand = jax.ShapeDtypeStruct((cols * LANES, sz * CAP), BF16)
    return pl.pallas_call(
        functools.partial(near_own_kernel, dims),
        out_shape=(
            jax.ShapeDtypeStruct((cols * 8, sz * CAP), F32),
            operand,
            jax.ShapeDtypeStruct((8, LANES), F32),
        ),
        in_specs=[VMEM],
        out_specs=(VMEM,) * 3,
        scratch_shapes=[
            pltpu.VMEM((2, cols * LANES, LANES), F32),
            pltpu.VMEM((cols * sz * CAP, LANES), BF16),
            pltpu.VMEM((2, cols * LANES, LANES), F32),
        ],
        compiler_params=pltpu.CompilerParams(vmem_limit_bytes=9 << 20),
        cost_estimate=pl.CostEstimate(flops=1 << 32, bytes_accessed=1 << 20, transcendentals=1 << 22),
        name="near_own",
    )(own)


def near_row(dims, got_a, got_b, near, rhs, parents, l2l, ops, token):
    sx, sy, sz = dims
    cols = sx * sy
    slots = round_up(2 * sy, 8)
    rows, width = ops.shape
    surface = jnp.asarray(surface_features(sz))
    spread = jnp.asarray(spread_constant(dims), BF16)
    return pl.pallas_call(
        functools.partial(near_row_kernel, dims),
        out_shape=(
            jax.ShapeDtypeStruct((cols * 8, sz * CAP), F32),
            jax.ShapeDtypeStruct((sz * cols, Q), F32),
            jax.ShapeDtypeStruct(rhs.shape, BF16),
            jax.ShapeDtypeStruct((-(-width // LANES), rows, LANES), F32),
        ),
        in_specs=[VMEM] * 10,
        out_specs=(VMEM,) * 4,
        scratch_shapes=[
            pltpu.VMEM((4, slots, sz * CAP), F32),
            pltpu.VMEM((2, slots * LANES, LANES), F32),
            pltpu.VMEM((slots * sz * CAP, LANES), BF16),
        ],
        compiler_params=pltpu.CompilerParams(vmem_limit_bytes=6 << 20),
        cost_estimate=pl.CostEstimate(flops=1 << 26, bytes_accessed=1 << 20, transcendentals=0),
        name="near_row",
    )(got_a, got_b, near, rhs, parents, l2l, spread, surface, ops, token)


def fields(dims, own, a1, b1, a2, b2, near, rhs, table, inverse, inherited, c2e):
    sx, sy, sz = dims
    cols = sx * sy
    ring = 2 * (sx + 2)
    pick = jnp.asarray(gather_constant(dims), BF16)
    return pl.pallas_call(
        functools.partial(fields_kernel, dims),
        out_shape=(
            jax.ShapeDtypeStruct((sx, sy, sz * CAP), F32),
            jax.ShapeDtypeStruct((sx, sy, sz * Q), F32),
        ),
        in_specs=[VMEM] * 12,
        out_specs=(VMEM, VMEM),
        scratch_shapes=[
            pltpu.VMEM((4, round_up(ring, 8), sz * CAP), F32),
            pltpu.VMEM((2, round_up(ring, 8) * LANES, LANES), F32),
            pltpu.VMEM((ring * sz * CAP, LANES), BF16),
            pltpu.VMEM(near.shape, F32),
            pltpu.VMEM((LANES, 2 * LANES), F32),
            pltpu.VMEM((LANES, 2 * LANES), BF16),
            pltpu.VMEM((sz // 2, cols * PITCH, LANES), F32),
            pltpu.VMEM((LANES, LANES), F32),
        ],
        compiler_params=pltpu.CompilerParams(vmem_limit_bytes=16 << 20),
        name="fields",
    )(own, a1, b1, a2, b2, near, rhs, table, inverse, inherited, c2e, pick)


def exchange(send_a, send_b, axis):
    count = lax.axis_size(axis)
    got = []
    for value, first in ((send_a, 0), (send_b, 1)):
        pairs = [(i, i + 1) for i in range(first, count - 1, 2)]
        got.append(lax.ppermute(value, axis, pairs + [(b, a) for a, b in pairs]))
    return got


def body(positions, masses, counts, multipoles, parent_local, m2l_ops, l2l_ops, check_to_equiv):
    sx, sy, slots = masses.shape
    dims = (sx, sy, slots // CAP)
    send_a, send_b, own = pack_row(dims, positions, masses, counts, multipoles)
    a1, b1 = exchange(send_a, send_b, "row")
    near, rhs, token = near_own(dims, own)
    send_a, send_b, token = pack_col(dims, own, a1, b1, token)
    a2, b2 = exchange(send_a, send_b, "col")
    near, inherited, inverse, raw = near_row(
        dims, a1, b1, near, rhs, parent_local, l2l_ops, m2l_ops, token
    )
    table = prepare(raw)
    return fields(
        dims, own, a1, b1, a2, b2, near, rhs, table, inverse, inherited, check_to_equiv
    )


def solution(mesh):
    return jax.shard_map(
        body,
        mesh=mesh,
        in_specs=(
            P(None, "row", "col", None),
            P("row", "col", None),
            P("row", "col", None),
            P("row", "col", None),
            P("row", "col", None),
            P(),
            P(),
            P(),
        ),
        out_specs=(P("row", "col", None), P("row", "col", None)),
        check_vma=False,
    )
```

```python
import functools

import jax
import jax.numpy as jnp
import numpy as np
from jax import lax
from jax.experimental import pallas as pl
from jax.experimental.pallas import tpu as pltpu
from jax.sharding import PartitionSpec as P

CAP = 64
P_SIZE = 4
Q = 56
SOFTEN = 0.05
LANES = 128
BIG = 2.0**100
DEAD = 2.0**120
F32, BF16 = jnp.float32, jnp.bfloat16
REACH = 3
SPAN = 2 * REACH + 1
PITCH = 136


def surface_points():
    steps = np.stack(
        np.meshgrid(np.arange(P_SIZE), np.arange(P_SIZE), np.arange(P_SIZE), indexing="ij"), -1
    ).reshape(-1, 3)
    on_face = np.any((steps == 0) | (steps == P_SIZE - 1), axis=1)
    return (0.5 + 1.4 * (steps[on_face] / (P_SIZE - 1) - 0.5)).astype(np.float32)


def admits(shift, parity):
    return -2 - parity <= shift <= 3 - parity


def split2(x):
    hi = x.astype(BF16)
    return hi, (x - hi.astype(F32)).astype(BF16)


def split3(x):
    hi = x.astype(BF16).astype(F32)
    rest = x - hi
    mid = rest.astype(BF16).astype(F32)
    return hi, mid, rest - mid


def dot(a, b):
    return jnp.dot(a, b, preferred_element_type=F32)


def dot3(a, b):
    a_hi, a_lo = split2(a)
    b_hi, b_lo = split2(b)
    return dot(a_hi, b_hi) + (dot(a_hi, b_lo) + dot(a_lo, b_hi))


def column_weights(masses, counts, x, y, sz):
    lane = lax.broadcasted_iota(jnp.int32, (1, sz * CAP), 1)
    limit = jnp.zeros((1, sz * CAP), jnp.int32)
    for z in range(sz):
        limit = jnp.where(lane // CAP == z, counts[x, y, z], limit)
    return jnp.where(lane % CAP < limit, masses, 0.0)


def is_odd(axis):
    return lax.axis_index(axis) % 2 == 1


def pack_row_kernel(
    dims, pos_far, mass_far, counts_far, poles_far, send_a, send_b, own,
    pos, mass, counts, poles, sems,
):
    sx, sy, sz = dims
    cols = sx * sy
    copies = [
        pltpu.make_async_copy(far, near, sems.at[i])
        for i, (far, near) in enumerate(
            ((counts_far, counts), (pos_far, pos), (mass_far, mass), (poles_far, poles))
        )
    ]
    for copy in copies:
        copy.start()
    own[...] = jnp.zeros_like(own)
    send_a[...] = jnp.zeros_like(send_a)
    send_b[...] = jnp.zeros_like(send_b)
    for copy in copies:
        copy.wait()
    for x in range(sx):
        at = x * sy
        for c in range(3):
            own[c * cols + at : c * cols + at + sy, :] = pos[c, x] - 0.5
        for y in range(sy):
            row = 3 * cols + at + y
            own[row : row + 1, :] = column_weights(mass[x, y : y + 1, :], counts, x, y, sz)
        own[4 * cols + at : 4 * cols + at + sy, 0 : sz * Q] = poles[x]
    odd = is_odd("row")
    pieces = [(4 * cols, 4 * cols + (sx - REACH) * sy, REACH * sy, 0)]
    base = REACH * sy
    for c in range(4):
        pieces.append((c * cols, c * cols + (sx - 1) * sy, sy, base + c * sy))
    for low, high, rows, at in pieces:
        low_edge, high_edge = own[low : low + rows, :], own[high : high + rows, :]
        send_a[at : at + rows, :] = jnp.where(odd, low_edge, high_edge)
        send_b[at : at + rows, :] = jnp.where(odd, high_edge, low_edge)


def pack_col_kernel(dims, own, got_a, got_b, token, send_a, send_b, next_token, low, high):
    sx, sy, sz = dims
    cols = sx * sy
    odd_row, odd_col = is_odd("row"), is_odd("col")
    next_token[...] = token[...]
    low[...] = jnp.where(odd_row, got_a[...], got_b[...])
    high[...] = jnp.where(odd_row, got_b[...], got_a[...])
    base_in = REACH * sy
    base = REACH * (sx + 2 * REACH)
    px = sx + 2
    send_a[...] = jnp.zeros_like(send_a)
    send_b[...] = jnp.zeros_like(send_b)

    def store(at, rows, ref, start):
        low_edge = ref[start : start + rows, :]
        high_edge = ref[start + sy - rows : start + sy, :]
        send_a[at : at + rows, :] = jnp.where(odd_col, low_edge, high_edge)
        send_b[at : at + rows, :] = jnp.where(odd_col, high_edge, low_edge)

    for x in range(sx + 2 * REACH):
        if REACH <= x < REACH + sx:
            store(x * REACH, REACH, own, 4 * cols + (x - REACH) * sy)
        elif x < REACH:
            store(x * REACH, REACH, low, x * sy)
        else:
            store(x * REACH, REACH, high, (x - REACH - sx) * sy)
    for c in range(4):
        for x in range(px):
            at = base + c * px + x
            if x == 0:
                store(at, 1, low, base_in + c * sy)
            elif x == px - 1:
                store(at, 1, high, base_in + c * sy)
            else:
                store(at, 1, own, c * cols + (x - 1) * sy)


def surface_features(sz):
    points = np.full((64, 3), 10.0, np.float32)
    points[:Q] = surface_points() - np.float32(0.5)

    def pieces(x):
        out = []
        for _ in range(3):
            out.append(np.asarray(x, BF16).astype(np.float32))
            x = x - out[-1]
        return out

    left = np.zeros((64, LANES), np.float32)
    for c in range(3):
        parts = pieces(-2.0 * points[:, c])
        for n, piece in enumerate((0, 0, 0, 1, 1, 2)):
            left[:, 6 * c + n] = parts[piece]
    at = 18 + 3 * (3 + 3 + sz)
    for n, piece in enumerate(pieces((points * points).sum(1))):
        left[:, at + n] = piece
    at += 3 + 6 * (3 + 3 + sz)
    left[:, at : at + 3] = 1.0
    return np.asarray(left, BF16)


def gather_constant(dims):
    sx, sy, _ = dims
    cells = [(x + REACH, y + REACH) for x in range(sx) for y in range(sy)]
    cells += [(x, y + REACH) for x in range(REACH) for y in range(sy)]
    cells += [(x + REACH + sx, y + REACH) for x in range(REACH) for y in range(sy)]
    cells += [(x, y) for x in range(sx + 2 * REACH) for y in range(REACH)]
    cells += [(x, y + REACH + sy) for x in range(sx + 2 * REACH) for y in range(REACH)]
    at = {cell: i for i, cell in enumerate(cells)}
    pick = np.zeros((2 * LANES, sx * sy * LANES), np.float32)
    for x in range(sx):
        for y in range(sy):
            for a in range(SPAN):
                for b in range(SPAN):
                    if admits(a - REACH, x % 2) and admits(b - REACH, y % 2):
                        for half in range(2):
                            col = (x * sy + y) * LANES + half * 64 + a * SPAN + b
                            pick[half * LANES + at[(x + a, y + b)], col] = 1.0
    return pick


def spread_constant(dims):
    sx, sy, sz = dims
    parents = (sx // 2) * (sy // 2) * (sz // 2)
    pick = np.zeros((sx * sy * sz, 8 * parents), np.float32)
    for z in range(sz):
        for x in range(sx):
            for y in range(sy):
                octant = 4 * (x % 2) + 2 * (y % 2) + z % 2
                parent = ((z // 2) * (sx // 2) + x // 2) * (sy // 2) + y // 2
                pick[(z * sx + x) * sy + y, octant * parents + parent] = 1.0
    return pick


def prepare_kernel(raw, pick, table):
    tiles = raw.shape[0]
    ab = lax.broadcasted_iota(jnp.int32, (64, LANES), 0)
    closeby = (jnp.abs(ab // SPAN - REACH) <= 1) & (jnp.abs(ab % SPAN - REACH) <= 1)
    for j in range(tiles):
        for c in range(SPAN):
            block = raw[j, pl.ds(c, SPAN * SPAN, stride=SPAN), :]
            block = jnp.concatenate(
                [block, jnp.zeros((64 - SPAN * SPAN, LANES), F32)], axis=0
            )
            if abs(c - REACH) <= 1:
                block = jnp.where(closeby, 0.0, block)
            hi, lo = split2(block)
            table[c * 64 : (c + 1) * 64, 2 * j * LANES : (2 * j + 1) * LANES] = hi
            table[c * 64 : (c + 1) * 64, (2 * j + 1) * LANES : (2 * j + 2) * LANES] = lo


def fill_features(sz, place, su, feats, at):
    for half in range(2):
        rows = lax.broadcasted_iota(jnp.int32, (8, LANES), 0) + at
        lane = lax.broadcasted_iota(jnp.int32, (8, LANES), 1) + half * LANES
        lanes = slice(half * LANES, (half + 1) * LANES)
        arrays = [su[c][at : at + 8, lanes] for c in range(4)]
        for k, value in source_features_at(sz, place(rows), arrays, lane):
            feats[half, at * LANES + 8 * k : at * LANES + 8 * (k + 1), :] = value


def features_of(feats, half, i):
    return feats[half, pl.ds((i // 8) * 8 * LANES + i % 8, LANES, stride=8), :]


def turn_features(feats, lhs, i):
    for half in range(2):
        at = (2 * i + half) * LANES
        lhs[at : at + LANES, :] = features_of(feats, half, i).T.astype(BF16)


def near_sums(dims, lhs, rhs, total, src, targets):
    sz = dims[2]
    halves = [[h for h in range(2) if any(abs(z - t) <= 1 for t in (2 * h, 2 * h + 1))] for z in range(sz)]

    def add(target, half, d2):
        part = jnp.sum(lax.rsqrt(d2).reshape(d2.shape[0] // 8, 8, LANES), axis=0)
        at, lanes = slice(target * 8, (target + 1) * 8), slice(half * LANES, (half + 1) * LANES)
        total[at, lanes] = total[at, lanes] + part

    def operand(target, half):
        return rhs[target * LANES : (target + 1) * LANES, half * LANES : (half + 1) * LANES]

    base = src * sz * CAP
    middle = [z for z in range(sz) if len(halves[z]) == 2]
    rows = slice(base + middle[0] * CAP, base + (middle[-1] + 1) * CAP)
    for target in targets:
        d2 = dot(lhs[rows, :], rhs[target * LANES : (target + 1) * LANES, :])
        for half in range(2):
            add(target, half, d2[:, half * LANES : (half + 1) * LANES])
    for z in range(sz):
        if len(halves[z]) == 2:
            continue
        half = halves[z][0]
        rows = slice(base + z * CAP, base + (z + 1) * CAP)
        for i in range(0, len(targets), 2):
            both = targets[i : i + 2]
            wide = jnp.concatenate([operand(t, half) for t in both], axis=1)
            d2 = dot(lhs[rows, :], wide)
            for n, target in enumerate(both):
                add(target, half, d2[:, n * LANES : (n + 1) * LANES])


def near_own_kernel(
    dims, own, near, rhs, token, feats, lhs, rfeats
):
    sx, sy, sz = dims
    cols = sx * sy
    token[...] = own[0:8, 0:LANES]
    su = [own.at[c * cols : (c + 1) * cols] for c in range(4)]

    for at in range(0, cols, 8):
        fill_features(sz, lambda rows: (rows // sy + 1, rows % sy + 1), su, feats, at)
    for i in range(cols):
        turn_features(feats, lhs, i)
    for half in range(2):
        lanes = slice(half * LANES, (half + 1) * LANES)
        for at in range(0, cols, 8):
            rows = lax.broadcasted_iota(jnp.int32, (8, LANES), 0) + at
            lane = lax.broadcasted_iota(jnp.int32, (8, LANES), 1) + half * LANES
            arrays = [su[c][at : at + 8, lanes] for c in range(3)]
            for k, value in target_features_at(dims, arrays, rows, lane):
                rfeats[half, at * LANES + 8 * k : at * LANES + 8 * (k + 1), :] = value
    for i in range(cols):
        for half in range(2):
            lanes = slice(half * LANES, (half + 1) * LANES)
            rhs[i * LANES : (i + 1) * LANES, lanes] = features_of(rfeats, half, i).astype(BF16)
    near[...] = jnp.zeros_like(near)
    for i in range(cols):
        cell = (i // sy + 1, i % sy + 1)
        near_sums(dims, lhs, rhs, near, i, targets_of(dims, cell))


def targets_of(dims, cell):
    sx, sy, _ = dims
    return [
        x * sy + y
        for x in range(sx)
        for y in range(sy)
        if 0 <= cell[0] - x <= 2 and 0 <= cell[1] - y <= 2
    ]


def near_row_kernel(
    dims, got_a, got_b, near_own, rhs, parents, l2l, spread, surface, ops, token,
    near, inherited, inverse, raw, slots, feats, lhs,
):
    sx, sy, sz = dims
    base = REACH * sy
    odd = is_odd("row")
    su = [slots.at[c] for c in range(4)]
    slots[...] = jnp.zeros_like(slots)
    for side, (first, second) in enumerate(((got_a, got_b), (got_b, got_a))):
        for c in range(4):
            rows = slice(base + c * sy, base + (c + 1) * sy)
            su[c][side * sy : (side + 1) * sy, :] = jnp.where(odd, first[rows, :], second[rows, :])

    def place(rows):
        return jnp.where(rows < sy, 0, sx + 1), rows % sy + 1

    for at in range(0, slots.shape[1], 8):
        fill_features(sz, place, su, feats, at)
    for i in range(2 * sy):
        turn_features(feats, lhs, i)
    rows = []
    for pz in range(sz // 2):
        for x in range(sx // 2):
            rows.append(parents[x, :, pz * Q : (pz + 1) * Q])
    above = jnp.concatenate(rows, axis=0)
    below = jnp.concatenate([dot3(above, l2l[o]) for o in range(8)], axis=0)
    below_hi, below_lo = split2(below)
    inherited[...] = dot(spread[...], below_hi) + dot(spread[...], below_lo)
    near[...] = near_own[...]
    width = ops.shape[1]
    left = list(range(raw.shape[0]))
    for i in range(2 * sy):
        cell = ((sx + 1) * (i // sy), i % sy + 1)
        near_sums(dims, lhs, rhs, near, i, targets_of(dims, cell))
        for n in range(i * sx // 2, (i + 1) * sx // 2):
            d2 = dot(surface[...], rhs[n * LANES : (n + 1) * LANES, :])
            hi, lo = split2(lax.rsqrt(d2))
            inverse[n * LANES : n * LANES + 64, :] = hi
            inverse[n * LANES + 64 : (n + 1) * LANES, :] = lo
        for _ in range(-(-len(left) // (2 * sy - i))):
            j = left.pop(0)
            lanes = min(LANES, width - j * LANES)
            raw[j, :, 0:lanes] = ops[:, j * LANES : j * LANES + lanes]
            if lanes < LANES:
                raw[j, :, lanes:LANES] = jnp.zeros((ops.shape[0], LANES - lanes), F32)


def fields_kernel(
    dims,
    own, a1, b1, a2, b2, near_own, rhs, table, inverse, inherited, c2e, pick,
    potential, local_out,
    halo_slots, feats, lhs, near, sm, picked, lm, dens,
):
    sx, sy, sz = dims
    hx, hy = sx + 2, sy + 2
    cols = sx * sy
    tiles = table.shape[1] // (2 * LANES)
    odd_row, odd_col = is_odd("row"), is_odd("col")
    base1 = REACH * sy
    base2 = REACH * (sx + 2 * REACH)
    su = [halo_slots.at[c] for c in range(4)]
    halo_slots[...] = jnp.zeros_like(halo_slots)
    sm[...] = jnp.zeros_like(sm)
    sm[0:cols, :] = own[4 * cols : 5 * cols, :]
    at = cols
    for first, second in ((a1, b1), (b1, a1)):
        sm[at : at + base1, :] = jnp.where(odd_row, first[0:base1, :], second[0:base1, :])
        at += base1
    for side, (first, second) in enumerate(((a2, b2), (b2, a2))):
        value = jnp.where(odd_col, first[...], second[...])
        sm[at : at + base2, :] = value[0:base2, :]
        at += base2
        for c in range(4):
            rows = slice(base2 + c * hx, base2 + (c + 1) * hx)
            su[c][side * hx : (side + 1) * hx, :] = value[rows, :]

    def place(rows):
        second = rows >= hx
        return jnp.where(second, rows - hx, rows), jnp.where(second, hy - 1, 0)

    halo = {(x, (hy - 1) * side): side * hx + x for side in range(2) for x in range(hx)}

    for at in range(0, halo_slots.shape[1], 8):
        fill_features(sz, place, su, feats, at)
    for i in range(len(halo)):
        turn_features(feats, lhs, i)

    for pair in range(sz // 2):
        his, los = [], []
        for zi in range(2):
            z = 2 * pair + zi
            rolled = pltpu.roll(sm[...], (2 * LANES - z * Q) % (2 * LANES), 1)[:, 0:LANES]
            hi, lo = split2(rolled.T[0:64, :])
            his.append(hi)
            los.append(lo)
        keep = lax.broadcasted_iota(jnp.int32, (64, 2 * LANES), 0) < Q
        his = jnp.where(keep, jnp.concatenate(his, axis=1).astype(F32), 0.0)
        los = jnp.where(keep, jnp.concatenate(los, axis=1).astype(F32), 0.0)
        picked[...] = jnp.concatenate([his, los], axis=0).astype(BF16)
        for xy in range(0, cols, 2):
            block = dot(picked[...], pick[:, xy * LANES : (xy + 2) * LANES])
            for i in range(2):
                at = (xy + i) * PITCH
                lm[pair, at : at + LANES, :] = block[:, i * LANES : (i + 1) * LANES]

    period = 16
    lane16 = lax.broadcasted_iota(jnp.int32, (cols, LANES), 1)
    check = [jnp.zeros((cols, LANES), F32) for _ in range(sz)]
    near[...] = near_own[...]
    sources = list(halo.items())
    spans = period * Q // LANES
    for t in range(spans):
        members = [s for s in range(period) if s * Q < (t + 1) * LANES and (s + 1) * Q > t * LANES]
        rows = len(members) * cols
        left = []
        for j in range(-(-Q // period)):
            if j * (period * Q // LANES) + t >= tiles:
                continue
            vectors = [j * period + s for s in members]
            left.append(
                jnp.concatenate(
                    [
                        jnp.concatenate(
                            [
                                lm[p, pl.ds(h * 64 + q, cols, stride=PITCH), :]
                                for p in range(sz // 2)
                            ],
                            axis=1,
                        )
                        for h in range(2)
                        for q in vectors
                    ],
                    axis=0,
                ).astype(BF16)
            )
        for z in range(sz):
            total = None
            for j, block in enumerate(left):
                tile = j * (period * Q // LANES) + t
                first = (REACH - z) * 64
                part = dot(
                    block,
                    table[first : first + sz * 64, 2 * tile * LANES : (2 * tile + 2) * LANES],
                )
                total = part if total is None else total + part
            both = total[0:rows, 0:LANES] + (
                total[0:rows, LANES : 2 * LANES] + total[rows : 2 * rows, 0:LANES]
            )
            for i, s in enumerate(members):
                offset = s * Q - t * LANES
                part = both[i * cols : (i + 1) * cols, :]
                part = jnp.where((lane16 >= offset) & (lane16 < offset + Q), part, 0.0)
                check[z] = check[z] + pltpu.roll(part, (-offset) % LANES, 1)
        for _ in range(-(-len(sources) // (spans - t))):
            cell, src = sources.pop(0)
            near_sums(dims, lhs, rhs, near, src, targets_of(dims, cell))
    assert not sources

    field = jnp.concatenate([part[:, 0:Q] for part in check], axis=0) + inherited[...]
    local = dot3(field, c2e[...])
    dens[...] = jnp.zeros_like(dens)
    dens[0 : sz * cols, 0:Q] = local
    flat = None
    for z in range(sz):
        part = jnp.concatenate(
            [dens[z * cols : (z + 1) * cols, :], jnp.zeros((cols, LANES), F32)], axis=1
        )
        part = pltpu.roll(part, z * Q, 1) if z else part
        flat = part if flat is None else flat + part
    for x in range(sx):
        local_out[x] = flat[x * sy : (x + 1) * sy, 0 : sz * Q]

    hi, lo = split2(dens[0 : sz * cols, 0:64])
    none = jnp.zeros_like(hi)
    dens[0 : sz * cols, :] = jnp.concatenate([hi, hi], axis=1).astype(F32)
    dens[sz * cols : 2 * sz * cols, :] = jnp.concatenate([lo, none], axis=1).astype(F32)
    row = lax.broadcasted_iota(jnp.int32, (2 * sz, sz * CAP), 0) % sz
    mine = row == lax.broadcasted_iota(jnp.int32, (2 * sz, sz * CAP), 1) // CAP

    def far(i):
        pieces = dens[pl.ds(i, 2 * sz, stride=cols), :].astype(BF16)
        value = dot(pieces, inverse[i * LANES : (i + 1) * LANES, :])
        at = slice(i * 8, i * 8 + 2 * sz)
        near[at, :] = near[at, :] + jnp.where(mine, value, 0.0)

    for i in range(cols):
        far(i)
    for i in range(cols):
        x, y = i // sy, i % sy
        value = jnp.sum(near[i * 8 : (i + 1) * 8, :], axis=0, keepdims=True)
        live = own[3 * cols + i : 3 * cols + i + 1, :] > 0
        potential[x, y : y + 1, :] = jnp.where(live, value, 0.0)


def source_features_at(sz, place, arrays, lane):
    ux, uy, uz, w = arrays
    shape = w.shape
    live = w > 0
    g = jnp.where(live, 1.0 / jnp.where(live, w * w, 1.0), 0.0)
    n = (ux * ux + uy * uy + uz * uz + SOFTEN * SOFTEN) * g
    n = jnp.where(live, n, DEAD)
    v = [split3(-2.0 * u * g) for u in (ux, uy, uz)]
    ones = [
        [place[0] % 3 == m for m in range(3)],
        [place[1] % 3 == m for m in range(3)],
        [lane // CAP == m for m in range(sz)],
    ]
    k = 0
    for c in range(3):
        for piece in (0, 0, 0, 1, 1, 2):
            yield k, v[c][piece]
            k += 1
    for c in range(3):
        for mask in ones[c]:
            for piece in range(3):
                yield k, jnp.where(mask, v[c][piece], 0.0)
                k += 1
    for piece in split3(n):
        yield k, piece
        k += 1
    gs = split3(g)
    for c in range(3):
        for mask in ones[c]:
            for piece in (0, 0, 0, 1, 1, 2):
                yield k, jnp.where(mask, gs[piece], 0.0)
                k += 1
    while k < LANES:
        yield k, jnp.zeros(shape, F32)
        k += 1


def target_features_at(dims, arrays, rows, lane):
    sx, sy, sz = dims
    shape = lane.shape
    place = (rows // sy, rows % sy, lane // CAP)
    t = [split3(u) for u in arrays]

    def shift(c, m):
        if c == 2:
            return (place[2] - m).astype(F32)
        return 1.0 - ((m - place[c] + 6) % 3).astype(F32)

    k = 0
    for c in range(3):
        for piece in (0, 1, 2, 0, 1, 0):
            yield k, t[c][piece]
            k += 1
    for c in range(3):
        for m in range(sz if c == 2 else 3):
            for _ in range(3):
                yield k, shift(c, m)
                k += 1
    for _ in range(3):
        yield k, jnp.ones(shape, F32)
        k += 1
    for c in range(3):
        for m in range(sz if c == 2 else 3):
            moved = arrays[c] + shift(c, m)
            parts = list(split3(moved * moved))
            if c == 2:
                reach = jnp.abs(place[2] - m) <= 1
                parts = [jnp.where(reach, p, BIG if i == 0 else 0.0) for i, p in enumerate(parts)]
            for piece in (0, 1, 2, 0, 1, 0):
                yield k, parts[piece]
                k += 1
    for piece in split3(arrays[0] * arrays[0] + arrays[1] * arrays[1] + arrays[2] * arrays[2]):
        yield k, piece
        k += 1
    while k < LANES:
        yield k, jnp.zeros(shape, F32)
        k += 1


VMEM = pl.BlockSpec(memory_space=pltpu.VMEM)
SMEM = pl.BlockSpec(memory_space=pltpu.SMEM)
HBM = pl.BlockSpec(memory_space=pltpu.HBM)


def round_up(n, m):
    return -(-n // m) * m


def pack_row(dims, pos, mass, counts, poles):
    sx, sy, sz = dims
    shape = jax.ShapeDtypeStruct((round_up((REACH + 4) * sy, 8), sz * CAP), F32)
    return pl.pallas_call(
        functools.partial(pack_row_kernel, dims),
        out_shape=(
            shape,
            shape,
            jax.ShapeDtypeStruct((5 * sx * sy, sz * CAP), F32),
        ),
        in_specs=[HBM] * 4,
        out_specs=(VMEM,) * 3,
        scratch_shapes=[
            pltpu.VMEM(pos.shape, F32),
            pltpu.VMEM(mass.shape, F32),
            pltpu.SMEM(counts.shape, jnp.int32),
            pltpu.VMEM(poles.shape, F32),
            pltpu.SemaphoreType.DMA((4,)),
        ],
        compiler_params=pltpu.CompilerParams(vmem_limit_bytes=2 << 20),
        name="pack_row",
    )(*(pltpu.with_memory_space_constraint(a, pltpu.HBM) for a in (pos, mass, counts, poles)))


def prepare(raw, pick):
    tiles = raw.shape[0]
    return pl.pallas_call(
        prepare_kernel,
        out_shape=jax.ShapeDtypeStruct((SPAN * 64, 2 * tiles * LANES), BF16),
        in_specs=[VMEM, VMEM],
        out_specs=VMEM,
        compiler_params=pltpu.CompilerParams(vmem_limit_bytes=4 << 20),
        cost_estimate=pl.CostEstimate(flops=1 << 24, bytes_accessed=1 << 20, transcendentals=0),
        name="prepare",
    )(raw, pick)


def pack_col(dims, own, got_a, got_b, token):
    sx, sy, sz = dims
    rows = round_up(REACH * (sx + 2 * REACH) + 4 * (sx + 2), 8)
    shape = jax.ShapeDtypeStruct((rows, sz * CAP), F32)
    return pl.pallas_call(
        functools.partial(pack_col_kernel, dims),
        out_shape=(shape, shape, jax.ShapeDtypeStruct(token.shape, F32)),
        in_specs=[VMEM] * 4,
        out_specs=(VMEM,) * 3,
        scratch_shapes=[pltpu.VMEM(got_a.shape, F32), pltpu.VMEM(got_a.shape, F32)],
        compiler_params=pltpu.CompilerParams(vmem_limit_bytes=2 << 20),
        name="pack_col",
    )(own, got_a, got_b, token)


def near_own(dims, own):
    sx, sy, sz = dims
    cols = sx * sy
    operand = jax.ShapeDtypeStruct((cols * LANES, sz * CAP), BF16)
    return pl.pallas_call(
        functools.partial(near_own_kernel, dims),
        out_shape=(
            jax.ShapeDtypeStruct((cols * 8, sz * CAP), F32),
            operand,
            jax.ShapeDtypeStruct((8, LANES), F32),
        ),
        in_specs=[VMEM],
        out_specs=(VMEM,) * 3,
        scratch_shapes=[
            pltpu.VMEM((2, cols * LANES, LANES), F32),
            pltpu.VMEM((cols * sz * CAP, LANES), BF16),
            pltpu.VMEM((2, cols * LANES, LANES), F32),
        ],
        compiler_params=pltpu.CompilerParams(vmem_limit_bytes=9 << 20),
        cost_estimate=pl.CostEstimate(flops=1 << 32, bytes_accessed=1 << 20, transcendentals=1 << 22),
        name="near_own",
    )(own)


def near_row(dims, got_a, got_b, near, rhs, parents, l2l, ops, token):
    sx, sy, sz = dims
    cols = sx * sy
    slots = round_up(2 * sy, 8)
    rows, width = ops.shape
    surface = jnp.asarray(surface_features(sz))
    spread = jnp.asarray(spread_constant(dims), BF16)
    return pl.pallas_call(
        functools.partial(near_row_kernel, dims),
        out_shape=(
            jax.ShapeDtypeStruct((cols * 8, sz * CAP), F32),
            jax.ShapeDtypeStruct((sz * cols, Q), F32),
            jax.ShapeDtypeStruct(rhs.shape, BF16),
            jax.ShapeDtypeStruct((-(-width // LANES), rows, LANES), F32),
        ),
        in_specs=[VMEM] * 10,
        out_specs=(VMEM,) * 4,
        scratch_shapes=[
            pltpu.VMEM((4, slots, sz * CAP), F32),
            pltpu.VMEM((2, slots * LANES, LANES), F32),
            pltpu.VMEM((slots * sz * CAP, LANES), BF16),
        ],
        compiler_params=pltpu.CompilerParams(vmem_limit_bytes=6 << 20),
        cost_estimate=pl.CostEstimate(flops=1 << 26, bytes_accessed=1 << 20, transcendentals=0),
        name="near_row",
    )(got_a, got_b, near, rhs, parents, l2l, spread, surface, ops, token)


def fields(dims, own, a1, b1, a2, b2, near, rhs, table, inverse, inherited, c2e, pick):
    sx, sy, sz = dims
    cols = sx * sy
    ring = 2 * (sx + 2)
    return pl.pallas_call(
        functools.partial(fields_kernel, dims),
        out_shape=(
            jax.ShapeDtypeStruct((sx, sy, sz * CAP), F32),
            jax.ShapeDtypeStruct((sx, sy, sz * Q), F32),
        ),
        in_specs=[VMEM] * 12,
        out_specs=(VMEM, VMEM),
        scratch_shapes=[
            pltpu.VMEM((4, round_up(ring, 8), sz * CAP), F32),
            pltpu.VMEM((2, round_up(ring, 8) * LANES, LANES), F32),
            pltpu.VMEM((ring * sz * CAP, LANES), BF16),
            pltpu.VMEM(near.shape, F32),
            pltpu.VMEM((LANES, 2 * LANES), F32),
            pltpu.VMEM((LANES, 2 * LANES), BF16),
            pltpu.VMEM((sz // 2, cols * PITCH, LANES), F32),
            pltpu.VMEM((LANES, LANES), F32),
        ],
        compiler_params=pltpu.CompilerParams(vmem_limit_bytes=16 << 20),
        name="fields",
    )(own, a1, b1, a2, b2, near, rhs, table, inverse, inherited, c2e, pick)


def exchange(send_a, send_b, axis):
    count = lax.axis_size(axis)
    got = []
    for value, first in ((send_a, 0), (send_b, 1)):
        pairs = [(i, i + 1) for i in range(first, count - 1, 2)]
        got.append(lax.ppermute(value, axis, pairs + [(b, a) for a, b in pairs]))
    return got


def body(positions, masses, counts, multipoles, parent_local, m2l_ops, l2l_ops, check_to_equiv):
    sx, sy, slots = masses.shape
    dims = (sx, sy, slots // CAP)
    send_a, send_b, own = pack_row(dims, positions, masses, counts, multipoles)
    a1, b1 = exchange(send_a, send_b, "row")
    near, rhs, token = near_own(dims, own)
    send_a, send_b, token = pack_col(dims, own, a1, b1, token)
    a2, b2 = exchange(send_a, send_b, "col")
    near, inherited, inverse, raw = near_row(
        dims, a1, b1, near, rhs, parent_local, l2l_ops, m2l_ops, token
    )
    pick = jnp.asarray(gather_constant(dims), BF16)
    table = prepare(raw, pick)
    return fields(
        dims, own, a1, b1, a2, b2, near, rhs, table, inverse, inherited, check_to_equiv,
        pick,
    )


def solution(mesh):
    return jax.shard_map(
        body,
        mesh=mesh,
        in_specs=(
            P(None, "row", "col", None),
            P("row", "col", None),
            P("row", "col", None),
            P("row", "col", None),
            P("row", "col", None),
            P(),
            P(),
            P(),
        ),
        out_specs=(P("row", "col", None), P("row", "col", None)),
        check_vma=False,
    )
```
